32 devices in a mesh: space: 2 (over x), vel: 16 (over z, y, core).
Axes of the slice: x: 2, y: 2, z: 4, core: 2. Of those that a mesh axis runs over, the one named last changes fastest.
Arguments:
- distribution: float32 [8192, 512], P('vel', 'space'), may hold values from 0.1 to 32, as said below
- normals: float32 [4, 3, 512], P(None, None, 'space'), may hold values from -0.3 to 0.3
- adjacency: int32 [4, 512], P(None, 'space'), may hold values from 0 to 511, as said below
- send_list: int32 [2, 2, 256], P('space'), may hold values from 0 to 255
- block_counts: int32 [2, 2], P(None, 'space'), may hold values from 0 to 2, as said below
Outputs:
- relaxed: float32 [8192, 512], P('vel', 'space')
- fields: float32 [13, 512], P(None, 'space')
The draws below stay inside these ranges and needn't reach their ends.
Inputs may be any that keep to these rules, and one draw needn't show every extreme that they name: `adjacency`: every entry of 256 or more names a position below 128 times the sum of block_counts over the senders to its group. `block_counts`: no group sends to itself; every other pair has at least one block; one receiving group gets 2 blocks from every other group. `distribution`: Positive.
All inputs are finite; a program needn't handle non-finite values.
Results may differ from the reference program's by a relative error of at most 0.00011.
Values sent between devices are 32-bit elements; how exact they have to be, the bound alone decides.
A program may use at most 64 MiB of HBM per device.

```python
import math
import jax
import jax.numpy as jnp
from jax import lax

VXY = 32
C_DEV = 256
FACES = 4
TILE = 128
MAXB = 2
BND = 256
ITERS = 2
V = 8192
VZN = 8
CELLS = 512
SLOTS = 256
N_SPACE = 2


def counts_core(key):
    key_one, key_three = jax.random.split(jax.random.fold_in(key, 11), 2)
    counts = jax.random.randint(key_one, (N_SPACE, N_SPACE), 1, MAXB + 1)
    full_group = jax.random.randint(key_three, (), 0, N_SPACE)
    row_ids = jnp.arange(N_SPACE)[:, None]
    col_ids = jnp.arange(N_SPACE)[None, :]
    counts = jnp.where(col_ids == full_group, MAXB, counts)
    return (jnp.where(row_ids == col_ids, 0, counts).astype(jnp.int32), full_group)


def draw_block_counts(key, part):
    counts, full_group = counts_core(key)
    return counts


def draw_adjacency(key, part):
    counts, full_group = counts_core(key)
    packed_total = jnp.sum(counts, axis=0) * TILE
    key_a, key_b, key_c = jax.random.split(jax.random.fold_in(key, 23), 3)
    group_of = jnp.arange(C_DEV * N_SPACE) // C_DEV
    limit = packed_total[group_of]
    local_pick = jax.random.randint(key_a, (FACES, C_DEV * N_SPACE), 0, C_DEV)
    ghost_pick = jax.random.randint(key_b, (FACES, C_DEV * N_SPACE), 0, 1 << 20) % limit[None, :]
    remote = jax.random.randint(key_c, (FACES, C_DEV * N_SPACE), 0, 8) == 0
    result = jnp.where(remote, C_DEV + ghost_pick, local_pick)
    first_cell = full_group * C_DEV
    face_ids = jnp.arange(FACES)[:, None]
    cell_ids = jnp.arange(C_DEV * N_SPACE)[None, :]
    top_value = C_DEV + (N_SPACE - 1) * SLOTS - 1
    result = jnp.where((face_ids == 0) & (cell_ids == first_cell), top_value, result)
    result = jnp.where((face_ids == 1) & (cell_ids == first_cell), 0, result)
    return result.astype(jnp.int32)


def draw_distribution(key, part):
    level = (jnp.arange(V) // (VXY * VXY)).astype(jnp.float32)
    comp_z = (level - (VZN - 1) / 2.0) * 0.3
    z_span = max(VZN - 1, 1) * 0.3
    key_one = jax.random.fold_in(key, 0)
    rough = jnp.exp(jax.random.uniform(key_one, (V, C_DEV * N_SPACE), jnp.float32, math.log(0.3), math.log(3.0)))
    tilt = math.log(5.0) / z_span
    return (rough * jnp.exp(tilt * comp_z)[:, None]).astype(jnp.float32)


def plant(values, own_key, smallest, largest):
    longest = values.shape.index(max(values.shape))
    spots = []
    for shift in (0, 1):
        where = [jax.random.randint(jax.random.fold_in(own_key, axis), (), 0, length) for axis, length in enumerate(values.shape)]
        where[longest] = (where[longest] + shift) % values.shape[longest]
        spots.append(tuple(where))
    return values.at[spots[0]].set(smallest).at[spots[1]].set(largest)


def block_levels(own_key, shape, cuts, least, largest):
    def one(dim, shards_of):
        heights = jax.random.uniform(jax.random.fold_in(jax.random.fold_in(own_key, 6), dim), (shards_of,), jnp.float32, least / len(cuts), largest / len(cuts))
        return jnp.repeat(jnp.exp(heights), shape[dim] // shards_of).reshape((-1,) + (1,) * (len(shape) - dim - 1))

    factor_of = one(*cuts[0])
    for cut in cuts[1:]:
        factor_of = factor_of * one(*cut)
    return factor_of


def setup_inputs(seed: int = 0) -> dict:
    key_list = jax.random.split(jax.random.key(seed), 6)
    distribution = draw_distribution(jax.random.fold_in(key_list[5], 71), 0)
    normals = jnp.clip(jax.random.uniform(key_list[1], (FACES, 3, CELLS), jnp.float32, -0.3, 0.3) * block_levels(key_list[1], (FACES, 3, CELLS), ((2, 2),), -0.4, 0.0), -0.3, 0.3)
    adjacency = draw_adjacency(jax.random.fold_in(key_list[5], 71), 0)
    send_list = plant(jax.random.randint(key_list[3], (N_SPACE, N_SPACE, SLOTS), 0, BND), jax.random.fold_in(key_list[3], 1), 0, BND - 1).astype(jnp.int32)
    block_counts = draw_block_counts(jax.random.fold_in(key_list[5], 71), 0)
    return {"distribution": distribution, "normals": normals, "adjacency": adjacency, "send_list": send_list, "block_counts": block_counts}


spacing = 0.3
ellipsoid_mix = -0.25
prandtl = 0.8
visc_power = 0.26
time_step = 0.025


def velocity_nodes(vel_index, z_count):
    comp_x = (vel_index % VXY).astype(jnp.float32)
    comp_y = ((vel_index // VXY) % VXY).astype(jnp.float32)
    comp_z = (vel_index // (VXY * VXY)).astype(jnp.float32)
    centre = (VXY - 1) / 2.0
    return jnp.stack([(comp_x - centre) * spacing, (comp_y - centre) * spacing, (comp_z - (z_count - 1) / 2.0) * spacing])


def moment_rows(velocity):
    comp_x, comp_y, comp_z = velocity[0], velocity[1], velocity[2]
    squared = comp_x * comp_x + comp_y * comp_y + comp_z * comp_z
    return jnp.stack([jnp.ones_like(comp_x), comp_x, comp_y, comp_z, comp_x * comp_x, comp_y * comp_y, comp_z * comp_z, comp_x * comp_y, comp_x * comp_z, comp_y * comp_z, comp_x * squared, comp_y * squared, comp_z * squared])


def quad_rows(velocity):
    comp_x, comp_y, comp_z = velocity[0], velocity[1], velocity[2]
    return jnp.stack([comp_x * comp_x, comp_y * comp_y, comp_z * comp_z, comp_x * comp_y, comp_x * comp_z, comp_y * comp_z, comp_x, comp_y, comp_z, jnp.ones_like(comp_x)])


def macroscopic(moments):
    density = moments[0]
    mean_x = moments[1] / density
    mean_y = moments[2] / density
    mean_z = moments[3] / density
    second = moments[4:10] / density[None, :]
    third = moments[10:13] / density[None, :]
    theta_xx = second[0] - mean_x * mean_x
    theta_yy = second[1] - mean_y * mean_y
    theta_zz = second[2] - mean_z * mean_z
    theta_xy = second[3] - mean_x * mean_y
    theta_xz = second[4] - mean_x * mean_z
    theta_yz = second[5] - mean_y * mean_z
    temper = (theta_xx + theta_yy + theta_zz) / 3.0
    trace_b = second[0] + second[1] + second[2]
    bu_x = second[0] * mean_x + second[3] * mean_y + second[4] * mean_z
    bu_y = second[3] * mean_x + second[1] * mean_y + second[5] * mean_z
    bu_z = second[4] * mean_x + second[5] * mean_y + second[2] * mean_z
    mean_sq = mean_x * mean_x + mean_y * mean_y + mean_z * mean_z
    flux_x = 0.5 * (third[0] - 2.0 * bu_x - mean_x * trace_b + 2.0 * mean_x * mean_sq)
    flux_y = 0.5 * (third[1] - 2.0 * bu_y - mean_y * trace_b + 2.0 * mean_y * mean_sq)
    flux_z = 0.5 * (third[2] - 2.0 * bu_z - mean_z * trace_b + 2.0 * mean_z * mean_sq)
    iso_part = (1.0 - ellipsoid_mix) * temper
    lam_xx = iso_part + ellipsoid_mix * theta_xx
    lam_yy = iso_part + ellipsoid_mix * theta_yy
    lam_zz = iso_part + ellipsoid_mix * theta_zz
    lam_xy = ellipsoid_mix * theta_xy
    lam_xz = ellipsoid_mix * theta_xz
    lam_yz = ellipsoid_mix * theta_yz
    cof_xx = lam_yy * lam_zz - lam_yz * lam_yz
    cof_xy = lam_yz * lam_xz - lam_xy * lam_zz
    cof_xz = lam_xy * lam_yz - lam_yy * lam_xz
    cof_yy = lam_xx * lam_zz - lam_xz * lam_xz
    cof_yz = lam_xy * lam_xz - lam_xx * lam_yz
    cof_zz = lam_xx * lam_yy - lam_xy * lam_xy
    determinant = lam_xx * cof_xx + lam_xy * cof_xy + lam_xz * cof_xz
    inv_xx = cof_xx / determinant
    inv_yy = cof_yy / determinant
    inv_zz = cof_zz / determinant
    inv_xy = cof_xy / determinant
    inv_xz = cof_xz / determinant
    inv_yz = cof_yz / determinant
    lin_x = inv_xx * mean_x + inv_xy * mean_y + inv_xz * mean_z
    lin_y = inv_xy * mean_x + inv_yy * mean_y + inv_yz * mean_z
    lin_z = inv_xz * mean_x + inv_yz * mean_y + inv_zz * mean_z
    offset = mean_x * lin_x + mean_y * lin_y + mean_z * lin_z
    collide = prandtl * density * jnp.exp(visc_power * jnp.log(temper))
    return jnp.stack([density, mean_x, mean_y, mean_z, theta_xx, theta_yy, theta_zz, theta_xy, theta_xz, theta_yz, flux_x, flux_y, flux_z,
                      inv_xx, inv_yy, inv_zz, 2.0 * inv_xy, 2.0 * inv_xz, 2.0 * inv_yz, -2.0 * lin_x, -2.0 * lin_y, -2.0 * lin_z, offset, collide])


def ghost_slots(adjacency, counts, cells, groups, slot_count):
    ends = (jnp.cumsum(counts) * TILE).astype(jnp.int32)
    starts = (ends - counts * TILE).astype(jnp.int32)
    is_local = adjacency < cells
    position = jnp.maximum(adjacency - cells, 0)
    source = jnp.sum((ends[:, None, None] <= position[None]).astype(jnp.int32), axis=0).astype(jnp.int32)
    source = jnp.minimum(source, groups - 1)
    group_ids = jnp.arange(groups, dtype=jnp.int32)[:, None, None]
    chosen = jnp.sum(jnp.where(group_ids == source[None], starts[:, None, None], 0), axis=0).astype(jnp.int32)
    slot_pos = jnp.clip(position - chosen, 0, slot_count - 1).astype(jnp.int32)
    return is_local, source, slot_pos


def relax(current, neighbours, velocity, normals, params, norm_z, equilibrium):
    gauss = params[0][None, :] * equilibrium / norm_z[None, :]
    outflow = jnp.zeros(current.shape, jnp.float32)
    inflow = jnp.zeros(current.shape, jnp.float32)
    for side in range(normals.shape[0]):
        normal_speed = (velocity[0][:, None] * normals[side, 0][None, :] + velocity[1][:, None] * normals[side, 1][None, :]
                        + velocity[2][:, None] * normals[side, 2][None, :])
        outflow = outflow + jnp.maximum(normal_speed, 0.0)
        inflow = inflow + jnp.minimum(normal_speed, 0.0) * neighbours[side]
    return current + time_step * (params[23][None, :] * (gauss - current) - outflow * current - inflow)


def reference(distribution, normals, adjacency, send_list, block_counts):
    pieces = []
    for group in range(N_SPACE):
        local_adj = adjacency[:, group * C_DEV:(group + 1) * C_DEV]
        is_local, source, slot_pos = ghost_slots(local_adj, block_counts[:, group], C_DEV, N_SPACE, SLOTS)
        listed = send_list[:, group, :]
        remote = source * C_DEV + listed[source, slot_pos]
        pieces.append(jnp.where(is_local, group * C_DEV + local_adj, remote).astype(jnp.int32))
    neighbour_index = jnp.concatenate(pieces, axis=1)
    level_count = V // (VXY * VXY)
    block_rows = VXY * VXY
    velocity = velocity_nodes(jnp.arange(V, dtype=jnp.int32), level_count)
    moment_table = moment_rows(velocity)
    quad_table = quad_rows(velocity).T
    vel_blocks = velocity.reshape(3, level_count, block_rows).transpose(1, 0, 2)
    quad_blocks = quad_table.reshape(level_count, block_rows, 10)

    def reduce_moments(current):
        partial_value = jnp.dot(moment_table, current, precision=lax.Precision.HIGHEST, preferred_element_type=jnp.float32)
        return macroscopic(partial_value / V)

    current = distribution
    for iteration in range(ITERS):
        params = reduce_moments(current)

        def block_equilibrium(quad_block):
            exponent = jnp.dot(quad_block, params[13:23], precision=lax.Precision.HIGHEST, preferred_element_type=jnp.float32)
            return jnp.exp(-0.5 * exponent)

        norm_z = jnp.sum(lax.map(lambda quad_block: jnp.sum(block_equilibrium(quad_block), axis=0), quad_blocks), axis=0) / V
        state_blocks = current.reshape(level_count, block_rows, CELLS)

        def update(inputs):
            state_block, vel_block, quad_block = inputs
            neighbours = [jnp.take(state_block, neighbour_index[side], axis=1) for side in range(FACES)]
            return relax(state_block, neighbours, vel_block, normals, params, norm_z, block_equilibrium(quad_block))

        current = lax.map(update, (state_blocks, vel_blocks, quad_blocks)).reshape(V, CELLS)
    final = reduce_moments(current)
    return current, final[:13]
```

```python
import functools

import jax
import jax.numpy as jnp
from jax import lax
from jax.experimental import pallas as pl
from jax.experimental.pallas import tpu as pltpu
from jax.sharding import PartitionSpec as P

VXY = 32
TILE = 128
ITERS = 2


spacing = 0.3
ellipsoid_mix = -0.25
prandtl = 0.8
visc_power = 0.26
time_step = 0.025


def velocity_nodes(vel_index, z_count):
    comp_x = (vel_index % VXY).astype(jnp.float32)
    comp_y = (vel_index // VXY % VXY).astype(jnp.float32)
    comp_z = (vel_index // (VXY * VXY)).astype(jnp.float32)
    centre = (VXY - 1) / 2.0
    return jnp.stack(
        [
            (comp_x - centre) * spacing,
            (comp_y - centre) * spacing,
            (comp_z - (z_count - 1) / 2.0) * spacing,
        ]
    )


def moment_rows(velocity):
    comp_x, comp_y, comp_z = (velocity[0], velocity[1], velocity[2])
    squared = comp_x * comp_x + comp_y * comp_y + comp_z * comp_z
    return jnp.stack(
        [
            jnp.ones_like(comp_x),
            comp_x,
            comp_y,
            comp_z,
            comp_x * comp_x,
            comp_y * comp_y,
            comp_z * comp_z,
            comp_x * comp_y,
            comp_x * comp_z,
            comp_y * comp_z,
            comp_x * squared,
            comp_y * squared,
            comp_z * squared,
        ]
    )


def quad_rows(velocity):
    comp_x, comp_y, comp_z = (velocity[0], velocity[1], velocity[2])
    return jnp.stack(
        [
            comp_x * comp_x,
            comp_y * comp_y,
            comp_z * comp_z,
            comp_x * comp_y,
            comp_x * comp_z,
            comp_y * comp_z,
            comp_x,
            comp_y,
            comp_z,
            jnp.ones_like(comp_x),
        ]
    )


def macroscopic(moments):
    density = moments[0]
    mean_x = moments[1] / density
    mean_y = moments[2] / density
    mean_z = moments[3] / density
    second = moments[4:10] / density[None, :]
    third = moments[10:13] / density[None, :]
    theta_xx = second[0] - mean_x * mean_x
    theta_yy = second[1] - mean_y * mean_y
    theta_zz = second[2] - mean_z * mean_z
    theta_xy = second[3] - mean_x * mean_y
    theta_xz = second[4] - mean_x * mean_z
    theta_yz = second[5] - mean_y * mean_z
    temper = (theta_xx + theta_yy + theta_zz) / 3.0
    trace_b = second[0] + second[1] + second[2]
    bu_x = second[0] * mean_x + second[3] * mean_y + second[4] * mean_z
    bu_y = second[3] * mean_x + second[1] * mean_y + second[5] * mean_z
    bu_z = second[4] * mean_x + second[5] * mean_y + second[2] * mean_z
    mean_sq = mean_x * mean_x + mean_y * mean_y + mean_z * mean_z
    flux_x = 0.5 * (third[0] - 2.0 * bu_x - mean_x * trace_b + 2.0 * mean_x * mean_sq)
    flux_y = 0.5 * (third[1] - 2.0 * bu_y - mean_y * trace_b + 2.0 * mean_y * mean_sq)
    flux_z = 0.5 * (third[2] - 2.0 * bu_z - mean_z * trace_b + 2.0 * mean_z * mean_sq)
    iso_part = (1.0 - ellipsoid_mix) * temper
    lam_xx = iso_part + ellipsoid_mix * theta_xx
    lam_yy = iso_part + ellipsoid_mix * theta_yy
    lam_zz = iso_part + ellipsoid_mix * theta_zz
    lam_xy = ellipsoid_mix * theta_xy
    lam_xz = ellipsoid_mix * theta_xz
    lam_yz = ellipsoid_mix * theta_yz
    cof_xx = lam_yy * lam_zz - lam_yz * lam_yz
    cof_xy = lam_yz * lam_xz - lam_xy * lam_zz
    cof_xz = lam_xy * lam_yz - lam_yy * lam_xz
    cof_yy = lam_xx * lam_zz - lam_xz * lam_xz
    cof_yz = lam_xy * lam_xz - lam_xx * lam_yz
    cof_zz = lam_xx * lam_yy - lam_xy * lam_xy
    determinant = lam_xx * cof_xx + lam_xy * cof_xy + lam_xz * cof_xz
    inv_xx = cof_xx / determinant
    inv_yy = cof_yy / determinant
    inv_zz = cof_zz / determinant
    inv_xy = cof_xy / determinant
    inv_xz = cof_xz / determinant
    inv_yz = cof_yz / determinant
    lin_x = inv_xx * mean_x + inv_xy * mean_y + inv_xz * mean_z
    lin_y = inv_xy * mean_x + inv_yy * mean_y + inv_yz * mean_z
    lin_z = inv_xz * mean_x + inv_yz * mean_y + inv_zz * mean_z
    offset = mean_x * lin_x + mean_y * lin_y + mean_z * lin_z
    collide = prandtl * density * jnp.exp(visc_power * jnp.log(temper))
    return jnp.stack(
        [
            density,
            mean_x,
            mean_y,
            mean_z,
            theta_xx,
            theta_yy,
            theta_zz,
            theta_xy,
            theta_xz,
            theta_yz,
            flux_x,
            flux_y,
            flux_z,
            inv_xx,
            inv_yy,
            inv_zz,
            2.0 * inv_xy,
            2.0 * inv_xz,
            2.0 * inv_yz,
            -2.0 * lin_x,
            -2.0 * lin_y,
            -2.0 * lin_z,
            offset,
            collide,
        ]
    )


def ghost_slots(adjacency, counts, cells, groups, slot_count):
    ends = jnp.cumsum(counts) * TILE
    starts = ends - counts * TILE
    is_local = adjacency < cells
    position = jnp.maximum(adjacency - cells, 0)
    source = jnp.sum((ends[:, None, None] <= position[None]).astype(jnp.int32), axis=0)
    source = jnp.minimum(source, groups - 1)
    group_ids = jnp.arange(groups, dtype=jnp.int32)[:, None, None]
    chosen = jnp.sum(jnp.where(group_ids == source[None], starts[:, None, None], 0), axis=0)
    slot_pos = jnp.clip(position - chosen, 0, slot_count - 1)
    return (is_local, source, slot_pos)


def relax(current, neighbours, velocity, normals, params, norm_z, equilibrium):
    gauss = params[0][None, :] * equilibrium / norm_z[None, :]
    outflow = jnp.zeros(current.shape, jnp.float32)
    inflow = jnp.zeros(current.shape, jnp.float32)
    for side in range(normals.shape[0]):
        normal_speed = (
            velocity[0][:, None] * normals[side, 0][None, :]
            + velocity[1][:, None] * normals[side, 1][None, :]
            + velocity[2][:, None] * normals[side, 2][None, :]
        )
        outflow = outflow + jnp.maximum(normal_speed, 0.0)
        inflow = inflow + jnp.minimum(normal_speed, 0.0) * neighbours[side]
    return current + time_step * (
        params[23][None, :] * (gauss - current) - outflow * current - inflow
    )


def per_device(distribution, normals, adjacency, send_list, block_counts):
    vel_local = distribution.shape[0]
    cells = distribution.shape[1]
    total_vel = vel_local * lax.axis_size("vel")
    z_count = total_vel // (VXY * VXY)
    groups = send_list.shape[1]
    slot_count = send_list.shape[2]
    vel_index = lax.axis_index("vel") * vel_local + jnp.arange(vel_local, dtype=jnp.int32)
    velocity = velocity_nodes(vel_index, z_count)
    moment_table = moment_rows(velocity)
    quad_table = quad_rows(velocity).T
    is_local, source, slot_pos = ghost_slots(
        adjacency, block_counts[:, 0], cells, groups, slot_count
    )
    ghost_index = source * slot_count + slot_pos
    local_index = jnp.where(is_local, adjacency, 0)
    send_rows = send_list[0].reshape(-1)

    def reduce_moments(current):
        partial_value = (
            jnp.dot(
                moment_table,
                current,
                precision=lax.Precision.HIGHEST,
                preferred_element_type=jnp.float32,
            )
            / total_vel
        )
        return macroscopic(lax.psum(partial_value, "vel"))

    current = distribution
    for iteration in range(ITERS):
        params = reduce_moments(current)
        ghosts = lax.all_to_all(
            jnp.take(current, send_rows, axis=1), "space", split_axis=1, concat_axis=1, tiled=True
        )
        exponent = jnp.dot(
            quad_table,
            params[13:23],
            precision=lax.Precision.HIGHEST,
            preferred_element_type=jnp.float32,
        )
        equilibrium = jnp.exp(-0.5 * exponent)
        norm_z = lax.psum(jnp.sum(equilibrium, axis=0) / total_vel, "vel")
        neighbours = [
            jnp.where(
                is_local[side][None, :],
                jnp.take(current, local_index[side], axis=1),
                jnp.take(ghosts, ghost_index[side], axis=1),
            )
            for side in range(normals.shape[0])
        ]
        current = relax(current, neighbours, velocity, normals, params, norm_z, equilibrium)
    final = reduce_moments(current)
    return (current, final[:13])


MESH = pl.DeviceIdType.MESH
LOG2E = 1.4426950408889634
QUAD = 4
CHUNKS = 4
PIECES = 8
HELD = 3
HI = lax.Precision.HIGHEST


def coefficient_rows(m):
    full = macroscopic_rows(m)
    scale = -0.5 * LOG2E
    return full[:13], [row * scale for row in full[13:23]], full[23]


def macroscopic_rows(m):
    density = m[0]
    inv_d = 1.0 / density
    ux, uy, uz = (m[1] * inv_d, m[2] * inv_d, m[3] * inv_d)
    b = [m[r] * inv_d for r in range(4, 10)]
    third = [m[r] * inv_d for r in range(10, 13)]
    txx, tyy, tzz = (b[0] - ux * ux, b[1] - uy * uy, b[2] - uz * uz)
    txy, txz, tyz = (b[3] - ux * uy, b[4] - ux * uz, b[5] - uy * uz)
    temper = (txx + tyy + tzz) * (1.0 / 3.0)
    trace_b = b[0] + b[1] + b[2]
    bux = b[0] * ux + b[3] * uy + b[4] * uz
    buy = b[3] * ux + b[1] * uy + b[5] * uz
    buz = b[4] * ux + b[5] * uy + b[2] * uz
    usq = ux * ux + uy * uy + uz * uz
    qx = 0.5 * (third[0] - 2.0 * bux - ux * trace_b + 2.0 * ux * usq)
    qy = 0.5 * (third[1] - 2.0 * buy - uy * trace_b + 2.0 * uy * usq)
    qz = 0.5 * (third[2] - 2.0 * buz - uz * trace_b + 2.0 * uz * usq)
    iso = (1.0 - ellipsoid_mix) * temper
    lxx, lyy, lzz = (iso + ellipsoid_mix * txx, iso + ellipsoid_mix * tyy, iso + ellipsoid_mix * tzz)
    lxy, lxz, lyz = (ellipsoid_mix * txy, ellipsoid_mix * txz, ellipsoid_mix * tyz)
    cxx = lyy * lzz - lyz * lyz
    cxy = lyz * lxz - lxy * lzz
    cxz = lxy * lyz - lyy * lxz
    cyy = lxx * lzz - lxz * lxz
    cyz = lxy * lxz - lxx * lyz
    czz = lxx * lyy - lxy * lxy
    inv_det = 1.0 / (lxx * cxx + lxy * cxy + lxz * cxz)
    ixx, iyy, izz = (cxx * inv_det, cyy * inv_det, czz * inv_det)
    ixy, ixz, iyz = (cxy * inv_det, cxz * inv_det, cyz * inv_det)
    wx = ixx * ux + ixy * uy + ixz * uz
    wy = ixy * ux + iyy * uy + iyz * uz
    wz = ixz * ux + iyz * uy + izz * uz
    offset = ux * wx + uy * wy + uz * wz
    collide = prandtl * density * jnp.exp(visc_power * jnp.log(temper))
    return [
        density, ux, uy, uz, txx, tyy, tzz, txy, txz, tyz, qx, qy, qz,
        ixx, iyy, izz, 2.0 * ixy, 2.0 * ixz, 2.0 * iyz,
        -2.0 * wx, -2.0 * wy, -2.0 * wz, offset, collide,
    ]


def node_velocity(index, z_count):
    shift = VXY.bit_length() - 1
    centre = (VXY - 1) / 2.0
    vx = ((index & (VXY - 1)).astype(jnp.float32) - centre) * spacing
    vy = (((index >> shift) & (VXY - 1)).astype(jnp.float32) - centre) * spacing
    vz = ((index >> (2 * shift)).astype(jnp.float32) - (z_count - 1) / 2.0) * spacing
    return vx, vy, vz


def x_column(first, rows, width):
    index = lax.broadcasted_iota(jnp.int32, (rows, width), 0) + first
    return (index.astype(jnp.float32) - (VXY - 1) / 2.0) * spacing


def pair_polynomials(half):
    def grow(before, now):
        rows = [now]
        for _ in range(half - 1):
            shifted = [0.0] + rows[-1]
            twice = [2.0 * v for v in rows[-1]] + [0.0]
            older = before + [0.0] * (len(shifted) - len(before))
            before = rows[-1]
            rows.append([x + y - z for x, y, z in zip(shifted, twice, older)])
        return rows

    return grow([1.0], [1.0]), grow([-1.0], [1.0])


def level_coefficients(q, z_count, powers):
    half = z_count // 2
    even, odd = pair_polynomials(half)
    weights = [jnp.exp2(q[2] * ((k + 0.5) * spacing) ** 2) for k in range(half)]
    result = []
    for c in range(powers):
        table = odd if c % 2 else even
        row = []
        for j in range(half):
            total = None
            for k in range(j, half):
                term = weights[k] * (table[k][j] * ((k + 0.5) * spacing) ** c)
                total = term if total is None else total + term
            row.append(total)
        result.append(row)
    return result


def horner(row, x):
    value = row[-1]
    for c in row[-2::-1]:
        value = value * x + c
    return value


def gauss_columns(q, width, block):
    step = 0.5 * spacing
    vx = x_column(block * 8, 8, width)
    base = (q[0] * vx + q[6]) * vx + q[9]
    lean = q[3] * vx + q[7]
    rise = (q[4] * vx + q[8]) * step
    for j in range(VXY // 2):
        vy = (j + 0.5) * spacing
        mid = base + q[1] * (vy * vy)
        tilt = lean * vy
        side = q[5] * (vy * step)
        columns = []
        for sign in (1.0, -1.0):
            flat = jnp.exp2(mid + tilt if sign > 0 else mid - tilt)
            slope = rise + side if sign > 0 else rise - side
            up, down = jnp.exp2(slope), jnp.exp2(-slope)
            diff = up - down
            columns.append((flat * (up + down), flat * diff, diff * diff))
        yield vx, vy, columns


def gauss_total(q, width, z_count):
    (even,) = level_coefficients(q, z_count, 1)

    def block(b, acc):
        for _, _, columns in gauss_columns(q, width, b):
            for plus, _, delta in columns:
                acc = acc + plus * horner(even, delta)
        return acc

    acc = lax.fori_loop(0, VXY // 8, block, jnp.zeros((8, width), jnp.float32))
    return jnp.sum(acc, axis=0, keepdims=True)


def gauss_moments(q, width, z_count):
    levels = level_coefficients(q, z_count, 4)
    zero = jnp.zeros((8, width), jnp.float32)

    def block(b, carry):
        sums = [[zero] * n for n in (4, 3, 2, 1)]
        for vx, vy, ((p_up, d_up, x_up), (p_down, d_down, x_down)) in gauss_columns(q, width, b):
            for c in range(4):
                above = (d_up if c % 2 else p_up) * horner(levels[c], x_up)
                below = (d_down if c % 2 else p_down) * horner(levels[c], x_down)
                both = above + below
                sums[c][0] = sums[c][0] + both
                if c < 3:
                    diff = (above - below) * vy
                    sums[c][1] = sums[c][1] + diff
                if c < 2:
                    sums[c][2] = sums[c][2] + both * (vy * vy)
                if c < 1:
                    sums[c][3] = sums[c][3] + diff * (vy * vy)
        (s0, s1, s2, s3), (z0, z1, z2), (zz0, zz1), (zc,) = sums
        vxx = vx * vx
        new = (
            s0, vx * s0, s1, z0, vxx * s0, s2, zz0, vx * s1, vx * z0, z1,
            vx * (vxx * s0 + s2 + zz0), vxx * s1 + s3 + zz1, vxx * z0 + z2 + zc,
        )
        return tuple(x + y for x, y in zip(carry, new))

    terms = lax.fori_loop(0, VXY // 8, block, (zero,) * 13)
    return [jnp.sum(t, axis=0, keepdims=True) for t in terms]


def split_dot(lhs, rhs):
    return jnp.dot(lhs, rhs, precision=HI, preferred_element_type=jnp.float32)


def step_kernel(
    total_vel,
    f_hbm, n_hbm, adj_hbm, send_hbm,
    out_ref, fields_ref,
    f_ref, n_ref, adj_ref, send_ref, load_s,
    fx, nx, adjx, sendx, ncat, xn, oh, tr0, fnew, tr1, phi_ref,
    qb0, zb0, total_mine, total_theirs, qb1, zb1, qb2, zb2,
    bulk_s, bulk_r, meta_s, meta_r, stage_s, stage_r,
):
    nodes, cells = f_hbm.shape
    both = 2 * cells
    faces = n_hbm.shape[1]
    z_count = total_vel // (VXY * VXY)
    rows = nodes // CHUNKS
    group = lax.axis_index("space")
    other = 1 - group
    vel = lax.axis_index("vel")
    ring = total_vel // nodes // QUAD
    me_q = lax.rem(vel, QUAD)
    me_z = vel // QUAD

    def at(space, z, q):
        return (space, z * QUAD + q)

    def q_of(step):
        return lax.rem(me_q + step, QUAD)

    def z_of(step):
        return lax.rem(me_z + step, ring)

    barrier = pltpu.get_barrier_semaphore()
    for step in range(1, ring):
        pl.semaphore_signal(barrier, inc=1, device_id=at(group, z_of(step), me_q), device_id_type=MESH)
    for step in range(1, QUAD):
        pl.semaphore_signal(barrier, inc=1, device_id=at(group, me_z, q_of(step)), device_id_type=MESH)
    pl.semaphore_signal(barrier, inc=1, device_id=at(other, me_z, me_q), device_id_type=MESH)

    def chunk(c):
        return pl.ds(pl.multiple_of(c * rows, rows), rows)

    loads = [
        pltpu.make_async_copy(f_hbm.at[pl.ds(c * rows, rows)], f_ref.at[pl.ds(c * rows, rows)], load_s.at[c])
        for c in range(CHUNKS)
    ]
    small_loads = [
        pltpu.make_async_copy(src, dst, load_s.at[CHUNKS + i])
        for i, (src, dst) in enumerate([(send_hbm, send_ref), (adj_hbm, adj_ref), (n_hbm, n_ref)])
    ]
    for copy in loads + small_loads:
        copy.start()

    lane_v = node_velocity(lax.broadcasted_iota(jnp.int32, (1, nodes), 1) + vel * nodes, z_count)
    lx, ly, lz = lane_v
    sq = lx * lx + ly * ly + lz * lz
    table = [
        jnp.ones_like(lx), lx, ly, lz, lx * lx, ly * ly, lz * lz,
        lx * ly, lx * lz, ly * lz, lx * sq, ly * sq, lz * sq,
    ]
    row_id = lax.broadcasted_iota(jnp.int32, (16, nodes), 0)
    phi = jnp.zeros((16, nodes), jnp.float32)
    for r, row in enumerate(table):
        phi = jnp.where(row_id == r, row, phi)
    phi_ref[...] = phi
    inv_total = 1.0 / total_vel
    partial = jnp.zeros((16, cells), jnp.float32)
    for c in range(CHUNKS):
        loads[c].wait()
        part = slice(c * rows, (c + 1) * rows)
        partial = partial + split_dot(phi[:, part], f_ref[part, :])
    qb0[me_q] = partial * inv_total

    with jax.named_scope("W_bar"):
        pl.semaphore_wait(barrier, QUAD + ring - 1)

    def remote(src, dst, s, r, dev):
        return pltpu.make_async_remote_copy(
            src_ref=src, dst_ref=dst, send_sem=s, recv_sem=r, device_id=dev, device_id_type=MESH
        )

    pair = at(other, me_z, me_q)

    def in_quad(buffer, i):
        for t in range(1, QUAD):
            remote(buffer.at[me_q], buffer.at[me_q], stage_s.at[i], stage_r.at[i], at(group, me_z, q_of(t))).start()

    def along_z(buffer, i):
        for t in range(1, ring):
            remote(buffer.at[me_z], buffer.at[me_z], stage_s.at[i], stage_r.at[i], at(group, z_of(t), me_q)).start()

    def all_of(buffer, sem, count):
        part = buffer.at[pl.ds(0, count)]
        pltpu.make_async_copy(part, part, sem).wait()

    def collect(i, buffer, count):
        with jax.named_scope(f"W_stage{i}"):
            all_of(buffer, stage_r.at[i], count - 1)
        result = buffer[0]
        for t in range(1, count):
            result = result + buffer[t]
        return result

    piece = nodes // PIECES
    ratio = PIECES // CHUNKS

    def bulk(c):
        part = pl.ds(pl.multiple_of(c * piece, piece), piece)
        return remote(f_hbm.at[part], fx.at[part], bulk_s, bulk_r.at[c // ratio], pair)

    def bulk_wait(c):
        with jax.named_scope("W_bulk"):
            part = fx.at[chunk(c)]
            pltpu.make_async_copy(part, part, bulk_r.at[c]).wait()

    metas = [
        remote(send_hbm, sendx, meta_s.at[0], meta_r.at[0], pair),
        remote(adj_hbm, adjx, meta_s.at[1], meta_r.at[1], pair),
        remote(n_hbm, nx, meta_s.at[2], meta_r.at[2], pair),
    ]
    in_quad(qb0, 0)
    for copy in metas:
        copy.start()
    for c in range(PIECES - HELD):
        bulk(c).start()

    for copy in small_loads:
        copy.wait()
    with jax.named_scope("W_meta"):
        for copy in metas:
            copy.wait_recv()
    zb0[me_z] = collect(0, qb0, QUAD)
    along_z(zb0, 1)

    slot_id = lax.broadcasted_iota(jnp.int32, (cells, cells), 0)
    cell_id = lax.broadcasted_iota(jnp.int32, (both, both), 0)
    diagonal = (cell_id == lax.broadcasted_iota(jnp.int32, (both, both), 1)).astype(jnp.float32)

    def listed(send_row, adjacency):
        hit = (slot_id == adjacency - cells).astype(jnp.bfloat16)
        values = jnp.broadcast_to(send_row, (8, cells)).astype(jnp.float32).astype(jnp.bfloat16)
        got = jnp.dot(values, hit, preferred_element_type=jnp.float32)
        return got[0:1].astype(jnp.int32)

    to_me = sendx[0, pl.ds(group, 1), :]
    to_other = send_ref[0, pl.ds(other, 1), :]
    vx_col = x_column(0, VXY, both)
    n_sum = [jnp.zeros((1, both), jnp.float32) for _ in range(3)]
    for k in range(faces):
        own = adj_ref[k : k + 1, :]
        theirs = adjx[k : k + 1, :]
        own = jnp.where(own < cells, own, cells + listed(to_me, own))
        theirs = jnp.where(theirs < cells, cells + theirs, listed(to_other, theirs))
        index = jnp.concatenate([own, theirs], axis=1)
        oh[k] = (jnp.where(cell_id == index, 1.0, 0.0) - diagonal).astype(jnp.bfloat16)
        for d in range(3):
            line = jnp.concatenate([n_ref[d, k : k + 1, :], nx[d, k : k + 1, :]], axis=1)
            ncat[d, k : k + 1, :] = line
            n_sum[d] = n_sum[d] + line
            if d == 0:
                xn[k] = vx_col * line
    for d in range(3):
        ncat[d, faces : faces + 1, :] = n_sum[d]
    xn[faces] = vx_col * n_sum[0]

    centre = (VXY - 1) / 2.0
    shift = VXY.bit_length() - 1

    def line_velocity(c, sub):
        line = (vel * nodes + c * rows) // VXY + sub
        vy = ((line & (VXY - 1)).astype(jnp.float32) - centre) * spacing
        vz = ((line >> shift).astype(jnp.float32) - (z_count - 1) / 2.0) * spacing
        return vy, vz

    subs = rows // VXY

    def transport(state, c, width):
        high = state.astype(jnp.bfloat16)
        low = (state - high.astype(jnp.float32)).astype(jnp.bfloat16)
        lhs = jnp.concatenate([high, low], axis=0)
        speeds = [line_velocity(c, sub) for sub in range(subs)]

        def speed(k, sub):
            vy, vz = speeds[sub]
            return xn[k, :, :width] + (vy * ncat[1, k : k + 1, :width] + vz * ncat[2, k : k + 1, :width])

        result = [state[sub * VXY : (sub + 1) * VXY, :width] * speed(faces, sub) for sub in range(subs)]
        for k in range(faces):
            got = jnp.dot(lhs, oh[k, :, 0:width], preferred_element_type=jnp.float32)
            for sub in range(subs):
                lines = slice(sub * VXY, (sub + 1) * VXY)
                low_lines = slice(rows + sub * VXY, rows + (sub + 1) * VXY)
                result[sub] = result[sub] + jnp.minimum(speed(k, sub), 0.0) * (got[lines] + got[low_lines])
        return jnp.concatenate(result, axis=0)

    def equilibrium(quad, c, width):
        vx = x_column(0, VXY, width)
        square = quad[0] * vx
        parts = []
        for sub in range(subs):
            vy, vz = line_velocity(c, sub)
            slope = quad[3] * vy + quad[4] * vz + quad[6]
            level = vy * (quad[1] * vy + quad[5] * vz + quad[7]) + (vz * (quad[2] * vz + quad[8]) + quad[9])
            parts.append(jnp.exp2(vx * (square + slope) + level))
        return jnp.concatenate(parts, axis=0)

    def wide(c):
        part = chunk(c)
        return part, jnp.concatenate([f_ref[part, :], fx[part, :]], axis=1)

    def first_transport(c, carry):
        bulk_wait(c)
        part, state = wide(c)
        tr0[part, :] = transport(state, c, both)
        return carry

    lax.fori_loop(0, 1, first_transport, 0)
    total_mine[...] = collect(1, zb0, ring)
    remote(total_mine, total_theirs, stage_s.at[2], stage_r.at[2], pair).start()
    for c in range(PIECES - HELD, PIECES):
        bulk(c).start()

    def rows_of(moments):
        return [moments[r : r + 1] for r in range(13)]

    mom0 = rows_of(total_mine[...])
    fields0, own_quad, freq0 = coefficient_rows(mom0)
    with jax.named_scope("G_mom0"):
        sums0 = gauss_moments(own_quad, cells, z_count)
    lift0 = time_step * freq0 * fields0[0] / sums0[0]
    own_gain = lift0 * float(total_vel)
    own_keep = 1.0 - time_step * freq0
    lax.fori_loop(1, CHUNKS - 1, first_transport, 0)
    with jax.named_scope("W_stage2"):
        pltpu.make_async_copy(total_theirs, total_theirs, stage_r.at[2]).wait()
    fields_x, their_quad, freq_x = coefficient_rows(rows_of(total_theirs[...]))
    with jax.named_scope("G_tot"):
        norm_x = gauss_total(their_quad, cells, z_count) * inv_total
    their_gain = time_step * freq_x * fields_x[0] / norm_x
    their_keep = 1.0 - time_step * freq_x
    quad0 = [jnp.concatenate([a, b], axis=1) for a, b in zip(own_quad, their_quad)]
    gain0 = jnp.concatenate([own_gain, their_gain], axis=1)
    keep0 = jnp.concatenate([own_keep, their_keep], axis=1)
    ahead = nodes - rows
    phi = phi_ref[...]
    m_t0 = split_dot(phi[:, :ahead], tr0[:ahead, :cells])
    lax.fori_loop(CHUNKS - 1, CHUNKS, first_transport, 0)
    qb1[me_q] = (m_t0 + split_dot(phi[:, ahead:], tr0[ahead:, :cells])) * inv_total
    in_quad(qb1, 3)

    def second_transport(c, carry):
        part, state = wide(c)
        state = keep0 * state - time_step * tr0[part, :] + gain0 * equilibrium(quad0, c, both)
        fnew[part, :] = state[:, :cells]
        tr1[part, :] = transport(state, c, cells)
        return carry

    lax.fori_loop(0, CHUNKS - 1, second_transport, 0)
    zb1[me_z] = collect(3, qb1, QUAD)
    along_z(zb1, 4)
    lax.fori_loop(CHUNKS - 1, CHUNKS, second_transport, 0)
    qb2[me_q] = split_dot(phi, tr1[...]) * inv_total
    in_quad(qb2, 5)
    zb2[me_z] = collect(5, qb2, QUAD)
    along_z(zb2, 6)
    mom_t0 = collect(4, zb1, ring)
    mom1 = [
        own_keep * mom0[r] - time_step * mom_t0[r : r + 1] + lift0 * sums0[r] for r in range(13)
    ]
    fields1, quad1, freq1 = coefficient_rows(mom1)
    with jax.named_scope("G_mom1"):
        sums = gauss_moments(quad1, cells, z_count)
    inv_sum = 1.0 / sums[0]
    lift = time_step * freq1 * fields1[0]
    gain1 = lift * inv_sum * float(total_vel)
    keep1 = 1.0 - time_step * freq1

    def finish(c, carry):
        part = chunk(c)
        out_ref[part, :] = (
            keep1 * fnew[part, :] - time_step * tr1[part, :] + gain1 * equilibrium(quad1, c, cells)
        )
        return carry

    lax.fori_loop(0, CHUNKS, finish, 0)
    mom_t = collect(6, zb2, ring)
    slope = lift * inv_sum
    last = [
        keep1 * mom1[r] - time_step * mom_t[r : r + 1] + slope * sums[r] for r in range(13)
    ]
    final = macroscopic_rows(last)
    for r in range(13):
        fields_ref[r : r + 1, :] = final[r]
    with jax.named_scope("W_send"):
        pltpu.make_async_copy(fx, fx, bulk_s).wait()
        for copy in metas:
            copy.wait_send()
        for i, (buffer, count) in enumerate([
            (qb0, QUAD - 1), (zb0, ring - 1), (None, 0), (qb1, QUAD - 1), (zb1, ring - 1), (qb2, QUAD - 1), (zb2, ring - 1),
        ]):
            if buffer is None:
                pltpu.make_async_copy(total_mine, total_mine, stage_s.at[i]).wait()
            else:
                all_of(buffer, stage_s.at[i], count)


def store_kernel(state_ref, fields_ref, state_out, fields_out, sems):
    copies = [
        pltpu.make_async_copy(fields_ref, fields_out, sems.at[0]),
        pltpu.make_async_copy(state_ref, state_out, sems.at[1]),
    ]
    for copy in copies:
        copy.start()
    for copy in copies:
        copy.wait()


def per_device_pair(distribution, normals, adjacency, send_list, block_counts):
    nodes, cells = distribution.shape
    normals = normals.transpose(1, 0, 2)
    size = lax.axis_size("vel")
    ring = size // QUAD
    faces = normals.shape[1]
    f32 = jnp.float32
    dma = pltpu.SemaphoreType.DMA
    vmem = pl.BlockSpec(memory_space=pltpu.VMEM)
    hbm = pl.BlockSpec(memory_space=pltpu.HBM)
    shapes = (
        jax.ShapeDtypeStruct((nodes, cells), f32),
        jax.ShapeDtypeStruct((13, cells), f32),
    )
    state, fields = pl.pallas_call(
        functools.partial(step_kernel, nodes * size),
        out_shape=shapes,
        in_specs=[hbm] * 4,
        out_specs=(vmem, vmem),
        scratch_shapes=[
            pltpu.VMEM((nodes, cells), f32),
            pltpu.VMEM(normals.shape, f32),
            pltpu.VMEM(adjacency.shape, jnp.int32),
            pltpu.VMEM(send_list.shape, jnp.int32),
            dma((CHUNKS + 3,)),
            pltpu.VMEM((nodes, cells), f32),
            pltpu.VMEM(normals.shape, f32),
            pltpu.VMEM(adjacency.shape, jnp.int32),
            pltpu.VMEM(send_list.shape, jnp.int32),
            pltpu.VMEM((3, 8, 2 * cells), f32),
            pltpu.VMEM((faces + 1, VXY, 2 * cells), f32),
            pltpu.VMEM((faces, 2 * cells, 2 * cells), jnp.bfloat16),
            pltpu.VMEM((nodes, 2 * cells), f32),
            pltpu.VMEM((nodes, cells), f32),
            pltpu.VMEM((nodes, cells), f32),
            pltpu.VMEM((16, nodes), f32),
            pltpu.VMEM((QUAD, 16, cells), f32),
            pltpu.VMEM((ring, 16, cells), f32),
            pltpu.VMEM((16, cells), f32),
            pltpu.VMEM((16, cells), f32),
            pltpu.VMEM((QUAD, 16, cells), f32),
            pltpu.VMEM((ring, 16, cells), f32),
            pltpu.VMEM((QUAD, 16, cells), f32),
            pltpu.VMEM((ring, 16, cells), f32),
            dma, dma((CHUNKS,)), dma((3,)), dma((3,)), dma((7,)), dma((7,)),
        ],
        compiler_params=pltpu.CompilerParams(
            collective_id=0, has_side_effects=True, vmem_limit_bytes=16 * 1024 * 1024
        ),
        name="steps",
    )(*[pltpu.with_memory_space_constraint(x, pltpu.HBM) for x in (distribution, normals, adjacency, send_list)])
    anywhere = pl.BlockSpec(memory_space=pl.ANY)
    return pl.pallas_call(
        store_kernel,
        out_shape=shapes,
        in_specs=[anywhere, anywhere],
        out_specs=(hbm, hbm),
        scratch_shapes=[dma((2,))],
        compiler_params=pltpu.CompilerParams(vmem_limit_bytes=16 * 1024 * 1024),
        name="store",
    )(state, fields)


def solution(mesh):
    placed = (
        P("vel", "space"),
        P(None, None, "space"),
        P(None, "space"),
        P("space", None, None),
        P(None, "space"),
    )
    pair = mesh.shape["space"] == 2 and mesh.shape["vel"] % QUAD == 0 and ITERS == 2
    return jax.shard_map(
        per_device_pair if pair else per_device,
        mesh=mesh,
        in_specs=placed,
        out_specs=(P("vel", "space"), P(None, "space")),
        check_vma=False,
    )
```

```python
import functools

import jax
import jax.numpy as jnp
from jax import lax
from jax.experimental import pallas as pl
from jax.experimental.pallas import tpu as pltpu
from jax.sharding import PartitionSpec as P

VXY = 32
TILE = 128
ITERS = 2


spacing = 0.3
ellipsoid_mix = -0.25
prandtl = 0.8
visc_power = 0.26
time_step = 0.025


def velocity_nodes(vel_index, z_count):
    comp_x = (vel_index % VXY).astype(jnp.float32)
    comp_y = (vel_index // VXY % VXY).astype(jnp.float32)
    comp_z = (vel_index // (VXY * VXY)).astype(jnp.float32)
    centre = (VXY - 1) / 2.0
    return jnp.stack(
        [
            (comp_x - centre) * spacing,
            (comp_y - centre) * spacing,
            (comp_z - (z_count - 1) / 2.0) * spacing,
        ]
    )


def moment_rows(velocity):
    comp_x, comp_y, comp_z = (velocity[0], velocity[1], velocity[2])
    squared = comp_x * comp_x + comp_y * comp_y + comp_z * comp_z
    return jnp.stack(
        [
            jnp.ones_like(comp_x),
            comp_x,
            comp_y,
            comp_z,
            comp_x * comp_x,
            comp_y * comp_y,
            comp_z * comp_z,
            comp_x * comp_y,
            comp_x * comp_z,
            comp_y * comp_z,
            comp_x * squared,
            comp_y * squared,
            comp_z * squared,
        ]
    )


def quad_rows(velocity):
    comp_x, comp_y, comp_z = (velocity[0], velocity[1], velocity[2])
    return jnp.stack(
        [
            comp_x * comp_x,
            comp_y * comp_y,
            comp_z * comp_z,
            comp_x * comp_y,
            comp_x * comp_z,
            comp_y * comp_z,
            comp_x,
            comp_y,
            comp_z,
            jnp.ones_like(comp_x),
        ]
    )


def macroscopic(moments):
    density = moments[0]
    mean_x = moments[1] / density
    mean_y = moments[2] / density
    mean_z = moments[3] / density
    second = moments[4:10] / density[None, :]
    third = moments[10:13] / density[None, :]
    theta_xx = second[0] - mean_x * mean_x
    theta_yy = second[1] - mean_y * mean_y
    theta_zz = second[2] - mean_z * mean_z
    theta_xy = second[3] - mean_x * mean_y
    theta_xz = second[4] - mean_x * mean_z
    theta_yz = second[5] - mean_y * mean_z
    temper = (theta_xx + theta_yy + theta_zz) / 3.0
    trace_b = second[0] + second[1] + second[2]
    bu_x = second[0] * mean_x + second[3] * mean_y + second[4] * mean_z
    bu_y = second[3] * mean_x + second[1] * mean_y + second[5] * mean_z
    bu_z = second[4] * mean_x + second[5] * mean_y + second[2] * mean_z
    mean_sq = mean_x * mean_x + mean_y * mean_y + mean_z * mean_z
    flux_x = 0.5 * (third[0] - 2.0 * bu_x - mean_x * trace_b + 2.0 * mean_x * mean_sq)
    flux_y = 0.5 * (third[1] - 2.0 * bu_y - mean_y * trace_b + 2.0 * mean_y * mean_sq)
    flux_z = 0.5 * (third[2] - 2.0 * bu_z - mean_z * trace_b + 2.0 * mean_z * mean_sq)
    iso_part = (1.0 - ellipsoid_mix) * temper
    lam_xx = iso_part + ellipsoid_mix * theta_xx
    lam_yy = iso_part + ellipsoid_mix * theta_yy
    lam_zz = iso_part + ellipsoid_mix * theta_zz
    lam_xy = ellipsoid_mix * theta_xy
    lam_xz = ellipsoid_mix * theta_xz
    lam_yz = ellipsoid_mix * theta_yz
    cof_xx = lam_yy * lam_zz - lam_yz * lam_yz
    cof_xy = lam_yz * lam_xz - lam_xy * lam_zz
    cof_xz = lam_xy * lam_yz - lam_yy * lam_xz
    cof_yy = lam_xx * lam_zz - lam_xz * lam_xz
    cof_yz = lam_xy * lam_xz - lam_xx * lam_yz
    cof_zz = lam_xx * lam_yy - lam_xy * lam_xy
    determinant = lam_xx * cof_xx + lam_xy * cof_xy + lam_xz * cof_xz
    inv_xx = cof_xx / determinant
    inv_yy = cof_yy / determinant
    inv_zz = cof_zz / determinant
    inv_xy = cof_xy / determinant
    inv_xz = cof_xz / determinant
    inv_yz = cof_yz / determinant
    lin_x = inv_xx * mean_x + inv_xy * mean_y + inv_xz * mean_z
    lin_y = inv_xy * mean_x + inv_yy * mean_y + inv_yz * mean_z
    lin_z = inv_xz * mean_x + inv_yz * mean_y + inv_zz * mean_z
    offset = mean_x * lin_x + mean_y * lin_y + mean_z * lin_z
    collide = prandtl * density * jnp.exp(visc_power * jnp.log(temper))
    return jnp.stack(
        [
            density,
            mean_x,
            mean_y,
            mean_z,
            theta_xx,
            theta_yy,
            theta_zz,
            theta_xy,
            theta_xz,
            theta_yz,
            flux_x,
            flux_y,
            flux_z,
            inv_xx,
            inv_yy,
            inv_zz,
            2.0 * inv_xy,
            2.0 * inv_xz,
            2.0 * inv_yz,
            -2.0 * lin_x,
            -2.0 * lin_y,
            -2.0 * lin_z,
            offset,
            collide,
        ]
    )


def ghost_slots(adjacency, counts, cells, groups, slot_count):
    ends = jnp.cumsum(counts) * TILE
    starts = ends - counts * TILE
    is_local = adjacency < cells
    position = jnp.maximum(adjacency - cells, 0)
    source = jnp.sum((ends[:, None, None] <= position[None]).astype(jnp.int32), axis=0)
    source = jnp.minimum(source, groups - 1)
    group_ids = jnp.arange(groups, dtype=jnp.int32)[:, None, None]
    chosen = jnp.sum(jnp.where(group_ids == source[None], starts[:, None, None], 0), axis=0)
    slot_pos = jnp.clip(position - chosen, 0, slot_count - 1)
    return (is_local, source, slot_pos)


def relax(current, neighbours, velocity, normals, params, norm_z, equilibrium):
    gauss = params[0][None, :] * equilibrium / norm_z[None, :]
    outflow = jnp.zeros(current.shape, jnp.float32)
    inflow = jnp.zeros(current.shape, jnp.float32)
    for side in range(normals.shape[0]):
        normal_speed = (
            velocity[0][:, None] * normals[side, 0][None, :]
            + velocity[1][:, None] * normals[side, 1][None, :]
            + velocity[2][:, None] * normals[side, 2][None, :]
        )
        outflow = outflow + jnp.maximum(normal_speed, 0.0)
        inflow = inflow + jnp.minimum(normal_speed, 0.0) * neighbours[side]
    return current + time_step * (
        params[23][None, :] * (gauss - current) - outflow * current - inflow
    )


def per_device(distribution, normals, adjacency, send_list, block_counts):
    vel_local = distribution.shape[0]
    cells = distribution.shape[1]
    total_vel = vel_local * lax.axis_size("vel")
    z_count = total_vel // (VXY * VXY)
    groups = send_list.shape[1]
    slot_count = send_list.shape[2]
    vel_index = lax.axis_index("vel") * vel_local + jnp.arange(vel_local, dtype=jnp.int32)
    velocity = velocity_nodes(vel_index, z_count)
    moment_table = moment_rows(velocity)
    quad_table = quad_rows(velocity).T
    is_local, source, slot_pos = ghost_slots(
        adjacency, block_counts[:, 0], cells, groups, slot_count
    )
    ghost_index = source * slot_count + slot_pos
    local_index = jnp.where(is_local, adjacency, 0)
    send_rows = send_list[0].reshape(-1)

    def reduce_moments(current):
        partial_value = (
            jnp.dot(
                moment_table,
                current,
                precision=lax.Precision.HIGHEST,
                preferred_element_type=jnp.float32,
            )
            / total_vel
        )
        return macroscopic(lax.psum(partial_value, "vel"))

    current = distribution
    for iteration in range(ITERS):
        params = reduce_moments(current)
        ghosts = lax.all_to_all(
            jnp.take(current, send_rows, axis=1), "space", split_axis=1, concat_axis=1, tiled=True
        )
        exponent = jnp.dot(
            quad_table,
            params[13:23],
            precision=lax.Precision.HIGHEST,
            preferred_element_type=jnp.float32,
        )
        equilibrium = jnp.exp(-0.5 * exponent)
        norm_z = lax.psum(jnp.sum(equilibrium, axis=0) / total_vel, "vel")
        neighbours = [
            jnp.where(
                is_local[side][None, :],
                jnp.take(current, local_index[side], axis=1),
                jnp.take(ghosts, ghost_index[side], axis=1),
            )
            for side in range(normals.shape[0])
        ]
        current = relax(current, neighbours, velocity, normals, params, norm_z, equilibrium)
    final = reduce_moments(current)
    return (current, final[:13])


MESH = pl.DeviceIdType.MESH
LOG2E = 1.4426950408889634
QUAD = 4
CHUNKS = 4
PIECES = 16
MARKS = (5, 8, 11)
SLABS = 2
EARLY = 3
HI = lax.Precision.HIGHEST


def coefficient_rows(m):
    full = macroscopic_rows(m)
    scale = -0.5 * LOG2E
    return full[:13], [row * scale for row in full[13:23]], full[23]


def macroscopic_rows(m):
    density = m[0]
    inv_d = 1.0 / density
    ux, uy, uz = (m[1] * inv_d, m[2] * inv_d, m[3] * inv_d)
    b = [m[r] * inv_d for r in range(4, 10)]
    third = [m[r] * inv_d for r in range(10, 13)]
    txx, tyy, tzz = (b[0] - ux * ux, b[1] - uy * uy, b[2] - uz * uz)
    txy, txz, tyz = (b[3] - ux * uy, b[4] - ux * uz, b[5] - uy * uz)
    temper = (txx + tyy + tzz) * (1.0 / 3.0)
    trace_b = b[0] + b[1] + b[2]
    bux = b[0] * ux + b[3] * uy + b[4] * uz
    buy = b[3] * ux + b[1] * uy + b[5] * uz
    buz = b[4] * ux + b[5] * uy + b[2] * uz
    usq = ux * ux + uy * uy + uz * uz
    qx = 0.5 * (third[0] - 2.0 * bux - ux * trace_b + 2.0 * ux * usq)
    qy = 0.5 * (third[1] - 2.0 * buy - uy * trace_b + 2.0 * uy * usq)
    qz = 0.5 * (third[2] - 2.0 * buz - uz * trace_b + 2.0 * uz * usq)
    iso = (1.0 - ellipsoid_mix) * temper
    lxx, lyy, lzz = (iso + ellipsoid_mix * txx, iso + ellipsoid_mix * tyy, iso + ellipsoid_mix * tzz)
    lxy, lxz, lyz = (ellipsoid_mix * txy, ellipsoid_mix * txz, ellipsoid_mix * tyz)
    cxx = lyy * lzz - lyz * lyz
    cxy = lyz * lxz - lxy * lzz
    cxz = lxy * lyz - lyy * lxz
    cyy = lxx * lzz - lxz * lxz
    cyz = lxy * lxz - lxx * lyz
    czz = lxx * lyy - lxy * lxy
    inv_det = 1.0 / (lxx * cxx + lxy * cxy + lxz * cxz)
    ixx, iyy, izz = (cxx * inv_det, cyy * inv_det, czz * inv_det)
    ixy, ixz, iyz = (cxy * inv_det, cxz * inv_det, cyz * inv_det)
    wx = ixx * ux + ixy * uy + ixz * uz
    wy = ixy * ux + iyy * uy + iyz * uz
    wz = ixz * ux + iyz * uy + izz * uz
    offset = ux * wx + uy * wy + uz * wz
    collide = prandtl * density * jnp.exp(visc_power * jnp.log(temper))
    return [
        density, ux, uy, uz, txx, tyy, tzz, txy, txz, tyz, qx, qy, qz,
        ixx, iyy, izz, 2.0 * ixy, 2.0 * ixz, 2.0 * iyz,
        -2.0 * wx, -2.0 * wy, -2.0 * wz, offset, collide,
    ]


def node_velocity(index, z_count):
    shift = VXY.bit_length() - 1
    centre = (VXY - 1) / 2.0
    vx = ((index & (VXY - 1)).astype(jnp.float32) - centre) * spacing
    vy = (((index >> shift) & (VXY - 1)).astype(jnp.float32) - centre) * spacing
    vz = ((index >> (2 * shift)).astype(jnp.float32) - (z_count - 1) / 2.0) * spacing
    return vx, vy, vz


def x_column(first, rows, width):
    index = lax.broadcasted_iota(jnp.int32, (rows, width), 0) + first
    return (index.astype(jnp.float32) - (VXY - 1) / 2.0) * spacing


def pair_polynomials(half):
    def grow(before, now):
        rows = [now]
        for _ in range(half - 1):
            shifted = [0.0] + rows[-1]
            twice = [2.0 * v for v in rows[-1]] + [0.0]
            older = before + [0.0] * (len(shifted) - len(before))
            before = rows[-1]
            rows.append([x + y - z for x, y, z in zip(shifted, twice, older)])
        return rows

    return grow([1.0], [1.0]), grow([-1.0], [1.0])


def level_coefficients(q, z_count, powers):
    half = z_count // 2
    even, odd = pair_polynomials(half)
    weights = [jnp.exp2(q[2] * ((k + 0.5) * spacing) ** 2) for k in range(half)]
    result = []
    for c in range(powers):
        table = odd if c % 2 else even
        row = []
        for j in range(half):
            total = None
            for k in range(j, half):
                term = weights[k] * (table[k][j] * ((k + 0.5) * spacing) ** c)
                total = term if total is None else total + term
            row.append(total)
        result.append(row)
    return result


def horner(row, x):
    value = row[-1]
    for c in row[-2::-1]:
        value = value * x + c
    return value


def gauss_columns(q, width, block):
    step = 0.5 * spacing
    vx = x_column(block * 8, 8, width)
    base = (q[0] * vx + q[6]) * vx + q[9]
    lean = q[3] * vx + q[7]
    rise = (q[4] * vx + q[8]) * step
    for j in range(VXY // 2):
        vy = (j + 0.5) * spacing
        mid = base + q[1] * (vy * vy)
        tilt = lean * vy
        side = q[5] * (vy * step)
        columns = []
        for sign in (1.0, -1.0):
            flat = jnp.exp2(mid + tilt if sign > 0 else mid - tilt)
            slope = rise + side if sign > 0 else rise - side
            up, down = jnp.exp2(slope), jnp.exp2(-slope)
            diff = up - down
            columns.append((flat * (up + down), flat * diff, diff * diff))
        yield vx, vy, columns


def gauss_total(q, width, z_count):
    (even,) = level_coefficients(q, z_count, 1)

    def block(b, acc):
        for _, _, columns in gauss_columns(q, width, b):
            for plus, _, delta in columns:
                acc = acc + plus * horner(even, delta)
        return acc

    acc = lax.fori_loop(0, VXY // 8, block, jnp.zeros((8, width), jnp.float32))
    return jnp.sum(acc, axis=0, keepdims=True)


def gauss_moments(q, width, z_count):
    levels = level_coefficients(q, z_count, 4)
    zero = jnp.zeros((8, width), jnp.float32)

    def block(b, carry):
        sums = [[zero] * n for n in (4, 3, 2, 1)]
        for vx, vy, ((p_up, d_up, x_up), (p_down, d_down, x_down)) in gauss_columns(q, width, b):
            for c in range(4):
                above = (d_up if c % 2 else p_up) * horner(levels[c], x_up)
                below = (d_down if c % 2 else p_down) * horner(levels[c], x_down)
                both = above + below
                sums[c][0] = sums[c][0] + both
                if c < 3:
                    diff = (above - below) * vy
                    sums[c][1] = sums[c][1] + diff
                if c < 2:
                    sums[c][2] = sums[c][2] + both * (vy * vy)
                if c < 1:
                    sums[c][3] = sums[c][3] + diff * (vy * vy)
        (s0, s1, s2, s3), (z0, z1, z2), (zz0, zz1), (zc,) = sums
        vxx = vx * vx
        new = (
            s0, vx * s0, s1, z0, vxx * s0, s2, zz0, vx * s1, vx * z0, z1,
            vx * (vxx * s0 + s2 + zz0), vxx * s1 + s3 + zz1, vxx * z0 + z2 + zc,
        )
        return tuple(x + y for x, y in zip(carry, new))

    terms = lax.fori_loop(0, VXY // 8, block, (zero,) * 13)
    return [jnp.sum(t, axis=0, keepdims=True) for t in terms]


def split_dot(lhs, rhs):
    return jnp.dot(lhs, rhs, precision=HI, preferred_element_type=jnp.float32)


def step_kernel(
    total_vel,
    f_hbm, n_hbm, adj_hbm, send_hbm,
    out_ref, fields_ref,
    f_ref, n_ref, adj_ref, send_ref, load_s,
    fx, nx, adjx, sendx, ncat, xn, oh, tr0, wide, fnew, tr1, phi_ref, phi_two,
    qb0, zb0, total_mine, total_theirs, qb1, zb1, qb2, zb2, lent0, got0, lent1, got1,
    bulk_s, bulk_r, meta_s, meta_r, stage_s, stage_r,
):
    nodes, cells = f_hbm.shape
    both = 2 * cells
    faces = n_hbm.shape[1]
    z_count = total_vel // (VXY * VXY)
    rows = nodes // CHUNKS
    group = lax.axis_index("space")
    other = 1 - group
    vel = lax.axis_index("vel")
    ring = total_vel // nodes // QUAD
    me_q = lax.rem(vel, QUAD)
    me_z = vel // QUAD

    def at(space, z, q):
        return (space, z * QUAD + q)

    def q_of(step):
        return lax.rem(me_q + step, QUAD)

    def z_of(step):
        return lax.rem(me_z + step, ring)

    barrier = pltpu.get_barrier_semaphore()
    for step in range(1, ring):
        pl.semaphore_signal(barrier, inc=1, device_id=at(group, z_of(step), me_q), device_id_type=MESH)
    for step in range(1, QUAD):
        pl.semaphore_signal(barrier, inc=1, device_id=at(group, me_z, q_of(step)), device_id_type=MESH)
    pl.semaphore_signal(barrier, inc=1, device_id=at(other, me_z, me_q), device_id_type=MESH)

    def chunk(c):
        return pl.ds(pl.multiple_of(c * rows, rows), rows)

    loads = [
        pltpu.make_async_copy(f_hbm.at[pl.ds(c * rows, rows)], f_ref.at[pl.ds(c * rows, rows)], load_s.at[c])
        for c in range(CHUNKS)
    ]
    small_loads = [
        pltpu.make_async_copy(src, dst, load_s.at[CHUNKS + i])
        for i, (src, dst) in enumerate([(send_hbm, send_ref), (adj_hbm, adj_ref), (n_hbm, n_ref)])
    ]
    for copy in loads + small_loads:
        copy.start()

    lane_v = node_velocity(lax.broadcasted_iota(jnp.int32, (1, nodes), 1) + vel * nodes, z_count)
    lx, ly, lz = lane_v
    sq = lx * lx + ly * ly + lz * lz
    table = [
        jnp.ones_like(lx), lx, ly, lz, lx * lx, ly * ly, lz * lz,
        lx * ly, lx * lz, ly * lz, lx * sq, ly * sq, lz * sq,
    ]
    row_id = lax.broadcasted_iota(jnp.int32, (16, nodes), 0)
    phi = jnp.zeros((16, nodes), jnp.float32)
    for r, row in enumerate(table):
        phi = jnp.where(row_id == r, row, phi)
    phi_ref[...] = phi
    phi_high = phi.astype(jnp.bfloat16)
    phi_two[0:16, :] = phi_high
    phi_two[16:32, :] = (phi - phi_high.astype(jnp.float32)).astype(jnp.bfloat16)
    inv_total = 1.0 / total_vel
    partial = jnp.zeros((16, cells), jnp.float32)
    for c in range(CHUNKS):
        loads[c].wait()
        part = slice(c * rows, (c + 1) * rows)
        partial = partial + split_dot(phi[:, part], f_ref[part, :])
    qb0[me_q] = partial * inv_total

    with jax.named_scope("W_bar"):
        pl.semaphore_wait(barrier, QUAD + ring - 1)

    def remote(src, dst, s, r, dev):
        return pltpu.make_async_remote_copy(
            src_ref=src, dst_ref=dst, send_sem=s, recv_sem=r, device_id=dev, device_id_type=MESH
        )

    pair = at(other, me_z, me_q)

    def in_quad(buffer, i):
        for t in range(1, QUAD):
            remote(buffer.at[me_q], buffer.at[me_q], stage_s.at[i], stage_r.at[i], at(group, me_z, q_of(t))).start()

    def along_z(buffer, i):
        for t in range(1, ring):
            remote(buffer.at[me_z], buffer.at[me_z], stage_s.at[i], stage_r.at[i], at(group, z_of(t), me_q)).start()

    def across(src, dst, i):
        remote(src, dst, stage_s.at[i], stage_r.at[i], pair).start()

    def arrived(dst, i):
        with jax.named_scope(f"W_stage{i}"):
            pltpu.make_async_copy(dst, dst, stage_r.at[i]).wait()

    def all_of(buffer, sem, count):
        part = buffer.at[pl.ds(0, count)]
        pltpu.make_async_copy(part, part, sem).wait()

    def collect(i, buffer, count):
        with jax.named_scope(f"W_stage{i}"):
            all_of(buffer, stage_r.at[i], count - 1)
        result = buffer[0]
        for t in range(1, count):
            result = result + buffer[t]
        return result

    piece = nodes // PIECES
    ratio = PIECES // CHUNKS

    def bulk(first, last):
        for c in range(first, last):
            part = pl.ds(c * piece, piece)
            remote(f_hbm.at[part], fx.at[part], bulk_s, bulk_r.at[c // ratio], pair).start()

    def bulk_wait(c):
        with jax.named_scope("W_bulk"):
            part = fx.at[chunk(c)]
            pltpu.make_async_copy(part, part, bulk_r.at[c]).wait()

    metas = [
        remote(send_hbm, sendx, meta_s.at[0], meta_r.at[0], pair),
        remote(adj_hbm, adjx, meta_s.at[1], meta_r.at[1], pair),
        remote(n_hbm, nx, meta_s.at[2], meta_r.at[2], pair),
    ]
    in_quad(qb0, 0)
    for copy in metas:
        copy.start()
    bulk(0, MARKS[0])

    for copy in small_loads:
        copy.wait()
    mine, far = slice(0, cells), slice(cells, both)
    slot_id = lax.broadcasted_iota(jnp.int32, (cells, cells), 0)
    eye = (slot_id == lax.broadcasted_iota(jnp.int32, (cells, cells), 1)).astype(jnp.float32)
    vx_col = x_column(0, VXY, cells)

    def listed(send_row, adjacency):
        hit = jnp.where(slot_id == adjacency - cells, 1.0, 0.0).astype(jnp.bfloat16)
        values = jnp.broadcast_to(send_row, (8, cells)).astype(jnp.float32).astype(jnp.bfloat16)
        got = jnp.dot(values, hit, preferred_element_type=jnp.float32)
        return jnp.where(adjacency < cells, -1, got[0:1].astype(jnp.int32))

    def choose(k, source, target, index):
        hit = jnp.where(slot_id == index, 1.0, 0.0)
        oh[k, source, target] = (hit - eye if source == target else hit).astype(jnp.bfloat16)

    def lay_normals(ref, target):
        for d in range(3):
            lines = [ref[d, k : k + 1, :] for k in range(faces)]
            lines.append(sum(lines[1:], lines[0]))
            for k, line in enumerate(lines):
                if d == 0:
                    xn[k, :, target] = vx_col * line
                else:
                    ncat[d, k : k + 1, target] = line

    lay_normals(n_ref, mine)
    for k in range(faces):
        choose(k, mine, mine, adj_ref[k : k + 1, :])

    zb0[me_z] = collect(0, qb0, QUAD)
    along_z(zb0, 1)

    with jax.named_scope("W_meta"):
        for copy in metas:
            copy.wait_recv()
    to_me = sendx[0, pl.ds(group, 1), :]
    to_other = send_ref[0, pl.ds(other, 1), :]
    lay_normals(nx, far)
    for k in range(faces):
        choose(k, mine, far, listed(to_other, adjx[k : k + 1, :]))

    centre = (VXY - 1) / 2.0
    shift = VXY.bit_length() - 1

    def line_velocity(first):
        line = (vel * nodes + first) // VXY
        vy = ((line & (VXY - 1)).astype(jnp.float32) - centre) * spacing
        vz = ((line >> shift).astype(jnp.float32) - (z_count - 1) / 2.0) * spacing
        return vy, vz

    def halves(state):
        high = state.astype(jnp.bfloat16)
        low = (state - high.astype(jnp.float32)).astype(jnp.bfloat16)
        return jnp.concatenate([high, low], axis=0)

    def transport(lhs, source, target, leaving, first, count):
        speeds = [line_velocity(first + sub * VXY) for sub in range(count // VXY)]

        def speed(k, sub):
            vy, vz = speeds[sub]
            return xn[k, :, target] + (vy * ncat[1, k : k + 1, target] + vz * ncat[2, k : k + 1, target])

        def lines(sub, offset=0):
            return slice(offset + sub * VXY, offset + (sub + 1) * VXY)

        result = [
            None if leaving is None else leaving[lines(sub)] * speed(faces, sub) for sub in range(count // VXY)
        ]
        for k in range(faces):
            got = jnp.dot(lhs, oh[k, source, target], preferred_element_type=jnp.float32)
            for sub in range(count // VXY):
                value = got[lines(sub)]
                if lhs.shape[0] > count:
                    value = value + got[lines(sub, count)]
                term = jnp.minimum(speed(k, sub), 0.0) * value
                result[sub] = term if result[sub] is None else result[sub] + term
        return jnp.concatenate(result, axis=0)

    def equilibrium(quad, first, count):
        square = quad[0] * vx_col
        parts = []
        for sub in range(count // VXY):
            vy, vz = line_velocity(first + sub * VXY)
            slope = quad[3] * vy + quad[4] * vz + quad[6]
            level = vy * (quad[1] * vy + quad[5] * vz + quad[7]) + (vz * (quad[2] * vz + quad[8]) + quad[9])
            parts.append(jnp.exp2(vx_col * (square + slope) + level))
        return jnp.concatenate(parts, axis=0)

    def two_dot(part, state):
        high = state.astype(jnp.bfloat16)
        low = (state - high.astype(jnp.float32)).astype(jnp.bfloat16)
        first = jnp.dot(phi_two[:, part], high, preferred_element_type=jnp.float32)
        return first[0:16] + first[16:32] + jnp.dot(phi_two[0:16, part], low, preferred_element_type=jnp.float32)

    blocks = [(c * (nodes // SLABS), nodes // SLABS) for c in range(SLABS)]
    sent = jnp.zeros((16, cells), jnp.float32)
    with jax.named_scope("T0p"):
        for first, count in blocks:
            part = slice(first, first + count)
            state = f_ref[part, :]
            lhs = halves(state)
            tr0[part, mine] = transport(lhs, mine, mine, state, first, count)
            moved = transport(lhs, mine, far, None, first, count)
            tr0[part, far] = moved
            sent = sent + two_dot(part, moved)
    lent0[...] = sent * (-time_step * inv_total)
    across(lent0, got0, 7)
    bulk(MARKS[0], MARKS[1])

    with jax.named_scope("oh2"):
        for k in range(faces):
            choose(k, far, mine, listed(to_me, adj_ref[k : k + 1, :]))
            theirs = adjx[k : k + 1, :]
            choose(k, far, far, theirs)

    total_mine[...] = collect(1, zb0, ring)
    across(total_mine, total_theirs, 2)
    bulk(MARKS[1], MARKS[2])

    def rows_of(moments):
        return [moments[r : r + 1] for r in range(13)]

    fields0, own_quad, freq0 = coefficient_rows(rows_of(total_mine[...]))
    with jax.named_scope("G_tot0"):
        norm0 = gauss_total(own_quad, cells, z_count) * inv_total
    own_gain = time_step * freq0 * fields0[0] / norm0
    own_keep = 1.0 - time_step * freq0

    with jax.named_scope("f1p"):
        for first, count in blocks:
            part = slice(first, first + count)
            state = (
                own_keep * f_ref[part, :] - time_step * tr0[part, mine] + own_gain * equilibrium(own_quad, first, count)
            )
            fnew[part, :] = state
            wide[part, mine] = state.astype(jnp.bfloat16)
            away = -time_step * tr0[part, far]
            tr0[part, far] = away
            wide[part, far] = away.astype(jnp.bfloat16)
        kept = split_dot(phi_ref[...], fnew[...]) * inv_total
    arrived(got0, 7)
    qb1[me_q] = kept + got0[...]
    in_quad(qb1, 3)

    def second_moments(target, leaving):
        total = jnp.zeros((16, cells), jnp.float32)
        for first, count in blocks:
            part = slice(first, first + count)
            moved = transport(wide[part, :], slice(0, both), target, leaving(part), first, count)
            total = total + two_dot(part, moved)
        return total * inv_total

    with jax.named_scope("T1p_far"):
        lent1[...] = second_moments(far, lambda part: tr0[part, far])
    across(lent1, got1, 8)
    bulk(MARKS[2], PIECES)
    with jax.named_scope("T1p_mine"):
        stay = second_moments(mine, lambda part: fnew[part, :])

    zb1[me_z] = collect(3, qb1, QUAD)
    along_z(zb1, 4)

    arrived(total_theirs, 2)
    fields_x, their_quad, freq_x = coefficient_rows(rows_of(total_theirs[...]))
    with jax.named_scope("G_totx"):
        norm_x = gauss_total(their_quad, cells, z_count) * inv_total
    their_gain = time_step * freq_x * fields_x[0] / norm_x
    their_keep = 1.0 - time_step * freq_x

    arrived(got1, 8)
    qb2[me_q] = stay + got1[...]
    in_quad(qb2, 5)

    def received(c, carry):
        bulk_wait(c)
        part, first = chunk(c), c * rows
        state = fx[part, :]
        lhs = halves(state)
        here = fnew[part, :] - time_step * transport(lhs, far, mine, None, first, rows)
        there = (
            their_keep * state
            + (tr0[part, far] - time_step * transport(lhs, far, far, state, first, rows))
            + their_gain * equilibrium(their_quad, first, rows)
        )
        fnew[part, :] = here
        lhs = halves(jnp.concatenate([here, there], axis=1))
        tr1[part, :] = transport(lhs, slice(0, both), mine, here, first, rows)
        return carry

    lax.fori_loop(0, EARLY, received, 0)
    zb2[me_z] = collect(5, qb2, QUAD)
    along_z(zb2, 6)
    mom1 = rows_of(collect(4, zb1, ring))
    fields1, quad1, freq1 = coefficient_rows(mom1)
    with jax.named_scope("G_mom1"):
        sums = gauss_moments(quad1, cells, z_count)
    inv_sum = 1.0 / sums[0]
    lift = time_step * freq1 * fields1[0]
    gain1 = lift * inv_sum * float(total_vel)
    keep1 = 1.0 - time_step * freq1
    lax.fori_loop(EARLY, CHUNKS, received, 0)

    def finish(c, carry):
        part = chunk(c)
        out_ref[part, :] = (
            keep1 * fnew[part, :] - time_step * tr1[part, :] + gain1 * equilibrium(quad1, c * rows, rows)
        )
        return carry

    with jax.named_scope("fin"):
        lax.fori_loop(0, CHUNKS, finish, 0)
    mom_t = collect(6, zb2, ring)
    slope = lift * inv_sum
    last = [
        keep1 * mom1[r] - time_step * mom_t[r : r + 1] + slope * sums[r] for r in range(13)
    ]
    final = macroscopic_rows(last)
    for r in range(13):
        fields_ref[r : r + 1, :] = final[r]
    with jax.named_scope("W_send"):
        pltpu.make_async_copy(fx, fx, bulk_s).wait()
        for copy in metas:
            copy.wait_send()
        for i, buffer in ((2, total_mine), (7, lent0), (8, lent1)):
            pltpu.make_async_copy(buffer, buffer, stage_s.at[i]).wait()
        for i, buffer, count in (
            (0, qb0, QUAD), (1, zb0, ring), (3, qb1, QUAD), (4, zb1, ring), (5, qb2, QUAD), (6, zb2, ring),
        ):
            all_of(buffer, stage_s.at[i], count - 1)


def store_kernel(state_ref, fields_ref, state_out, fields_out, sems):
    copies = [
        pltpu.make_async_copy(fields_ref, fields_out, sems.at[0]),
        pltpu.make_async_copy(state_ref, state_out, sems.at[1]),
    ]
    for copy in copies:
        copy.start()
    for copy in copies:
        copy.wait()


def per_device_pair(distribution, normals, adjacency, send_list, block_counts):
    nodes, cells = distribution.shape
    normals = normals.transpose(1, 0, 2)
    size = lax.axis_size("vel")
    ring = size // QUAD
    faces = normals.shape[1]
    f32 = jnp.float32
    dma = pltpu.SemaphoreType.DMA
    vmem = pl.BlockSpec(memory_space=pltpu.VMEM)
    hbm = pl.BlockSpec(memory_space=pltpu.HBM)
    shapes = (
        jax.ShapeDtypeStruct((nodes, cells), f32),
        jax.ShapeDtypeStruct((13, cells), f32),
    )
    state, fields = pl.pallas_call(
        functools.partial(step_kernel, nodes * size),
        out_shape=shapes,
        in_specs=[hbm] * 4,
        out_specs=(vmem, vmem),
        scratch_shapes=[
            pltpu.VMEM((nodes, cells), f32),
            pltpu.VMEM(normals.shape, f32),
            pltpu.VMEM(adjacency.shape, jnp.int32),
            pltpu.VMEM(send_list.shape, jnp.int32),
            dma((CHUNKS + 3,)),
            pltpu.VMEM((nodes, cells), f32),
            pltpu.VMEM(normals.shape, f32),
            pltpu.VMEM(adjacency.shape, jnp.int32),
            pltpu.VMEM(send_list.shape, jnp.int32),
            pltpu.VMEM((3, 8, 2 * cells), f32),
            pltpu.VMEM((faces + 1, VXY, 2 * cells), f32),
            pltpu.VMEM((faces, 2 * cells, 2 * cells), jnp.bfloat16),
            pltpu.VMEM((nodes, 2 * cells), f32),
            pltpu.VMEM((nodes, 2 * cells), jnp.bfloat16),
            pltpu.VMEM((nodes, cells), f32),
            pltpu.VMEM((nodes, cells), f32),
            pltpu.VMEM((16, nodes), f32),
            pltpu.VMEM((32, nodes), jnp.bfloat16),
            pltpu.VMEM((QUAD, 16, cells), f32),
            pltpu.VMEM((ring, 16, cells), f32),
            pltpu.VMEM((16, cells), f32),
            pltpu.VMEM((16, cells), f32),
            pltpu.VMEM((QUAD, 16, cells), f32),
            pltpu.VMEM((ring, 16, cells), f32),
            pltpu.VMEM((QUAD, 16, cells), f32),
            pltpu.VMEM((ring, 16, cells), f32),
            pltpu.VMEM((16, cells), f32),
            pltpu.VMEM((16, cells), f32),
            pltpu.VMEM((16, cells), f32),
            pltpu.VMEM((16, cells), f32),
            dma, dma((CHUNKS,)), dma((3,)), dma((3,)), dma((9,)), dma((9,)),
        ],
        compiler_params=pltpu.CompilerParams(
            collective_id=0, has_side_effects=True, vmem_limit_bytes=16 * 1024 * 1024
        ),
        name="steps",
    )(*[pltpu.with_memory_space_constraint(x, pltpu.HBM) for x in (distribution, normals, adjacency, send_list)])
    anywhere = pl.BlockSpec(memory_space=pl.ANY)
    return pl.pallas_call(
        store_kernel,
        out_shape=shapes,
        in_specs=[anywhere, anywhere],
        out_specs=(hbm, hbm),
        scratch_shapes=[dma((2,))],
        compiler_params=pltpu.CompilerParams(vmem_limit_bytes=16 * 1024 * 1024),
        name="store",
    )(state, fields)


def solution(mesh):
    placed = (
        P("vel", "space"),
        P(None, None, "space"),
        P(None, "space"),
        P("space", None, None),
        P(None, "space"),
    )
    pair = mesh.shape["space"] == 2 and mesh.shape["vel"] % QUAD == 0 and ITERS == 2
    return jax.shard_map(
        per_device_pair if pair else per_device,
        mesh=mesh,
        in_specs=placed,
        out_specs=(P("vel", "space"), P(None, "space")),
        check_vma=False,
    )
```

```python
import functools

import jax
import jax.numpy as jnp
from jax import lax
from jax.experimental import pallas as pl
from jax.experimental.pallas import tpu as pltpu
from jax.sharding import PartitionSpec as P

VXY = 32
TILE = 128
ITERS = 2


spacing = 0.3
ellipsoid_mix = -0.25
prandtl = 0.8
visc_power = 0.26
time_step = 0.025


def velocity_nodes(vel_index, z_count):
    comp_x = (vel_index % VXY).astype(jnp.float32)
    comp_y = (vel_index // VXY % VXY).astype(jnp.float32)
    comp_z = (vel_index // (VXY * VXY)).astype(jnp.float32)
    centre = (VXY - 1) / 2.0
    return jnp.stack(
        [
            (comp_x - centre) * spacing,
            (comp_y - centre) * spacing,
            (comp_z - (z_count - 1) / 2.0) * spacing,
        ]
    )


def moment_rows(velocity):
    comp_x, comp_y, comp_z = (velocity[0], velocity[1], velocity[2])
    squared = comp_x * comp_x + comp_y * comp_y + comp_z * comp_z
    return jnp.stack(
        [
            jnp.ones_like(comp_x),
            comp_x,
            comp_y,
            comp_z,
            comp_x * comp_x,
            comp_y * comp_y,
            comp_z * comp_z,
            comp_x * comp_y,
            comp_x * comp_z,
            comp_y * comp_z,
            comp_x * squared,
            comp_y * squared,
            comp_z * squared,
        ]
    )


def quad_rows(velocity):
    comp_x, comp_y, comp_z = (velocity[0], velocity[1], velocity[2])
    return jnp.stack(
        [
            comp_x * comp_x,
            comp_y * comp_y,
            comp_z * comp_z,
            comp_x * comp_y,
            comp_x * comp_z,
            comp_y * comp_z,
            comp_x,
            comp_y,
            comp_z,
            jnp.ones_like(comp_x),
        ]
    )


def macroscopic(moments):
    density = moments[0]
    mean_x = moments[1] / density
    mean_y = moments[2] / density
    mean_z = moments[3] / density
    second = moments[4:10] / density[None, :]
    third = moments[10:13] / density[None, :]
    theta_xx = second[0] - mean_x * mean_x
    theta_yy = second[1] - mean_y * mean_y
    theta_zz = second[2] - mean_z * mean_z
    theta_xy = second[3] - mean_x * mean_y
    theta_xz = second[4] - mean_x * mean_z
    theta_yz = second[5] - mean_y * mean_z
    temper = (theta_xx + theta_yy + theta_zz) / 3.0
    trace_b = second[0] + second[1] + second[2]
    bu_x = second[0] * mean_x + second[3] * mean_y + second[4] * mean_z
    bu_y = second[3] * mean_x + second[1] * mean_y + second[5] * mean_z
    bu_z = second[4] * mean_x + second[5] * mean_y + second[2] * mean_z
    mean_sq = mean_x * mean_x + mean_y * mean_y + mean_z * mean_z
    flux_x = 0.5 * (third[0] - 2.0 * bu_x - mean_x * trace_b + 2.0 * mean_x * mean_sq)
    flux_y = 0.5 * (third[1] - 2.0 * bu_y - mean_y * trace_b + 2.0 * mean_y * mean_sq)
    flux_z = 0.5 * (third[2] - 2.0 * bu_z - mean_z * trace_b + 2.0 * mean_z * mean_sq)
    iso_part = (1.0 - ellipsoid_mix) * temper
    lam_xx = iso_part + ellipsoid_mix * theta_xx
    lam_yy = iso_part + ellipsoid_mix * theta_yy
    lam_zz = iso_part + ellipsoid_mix * theta_zz
    lam_xy = ellipsoid_mix * theta_xy
    lam_xz = ellipsoid_mix * theta_xz
    lam_yz = ellipsoid_mix * theta_yz
    cof_xx = lam_yy * lam_zz - lam_yz * lam_yz
    cof_xy = lam_yz * lam_xz - lam_xy * lam_zz
    cof_xz = lam_xy * lam_yz - lam_yy * lam_xz
    cof_yy = lam_xx * lam_zz - lam_xz * lam_xz
    cof_yz = lam_xy * lam_xz - lam_xx * lam_yz
    cof_zz = lam_xx * lam_yy - lam_xy * lam_xy
    determinant = lam_xx * cof_xx + lam_xy * cof_xy + lam_xz * cof_xz
    inv_xx = cof_xx / determinant
    inv_yy = cof_yy / determinant
    inv_zz = cof_zz / determinant
    inv_xy = cof_xy / determinant
    inv_xz = cof_xz / determinant
    inv_yz = cof_yz / determinant
    lin_x = inv_xx * mean_x + inv_xy * mean_y + inv_xz * mean_z
    lin_y = inv_xy * mean_x + inv_yy * mean_y + inv_yz * mean_z
    lin_z = inv_xz * mean_x + inv_yz * mean_y + inv_zz * mean_z
    offset = mean_x * lin_x + mean_y * lin_y + mean_z * lin_z
    collide = prandtl * density * jnp.exp(visc_power * jnp.log(temper))
    return jnp.stack(
        [
            density,
            mean_x,
            mean_y,
            mean_z,
            theta_xx,
            theta_yy,
            theta_zz,
            theta_xy,
            theta_xz,
            theta_yz,
            flux_x,
            flux_y,
            flux_z,
            inv_xx,
            inv_yy,
            inv_zz,
            2.0 * inv_xy,
            2.0 * inv_xz,
            2.0 * inv_yz,
            -2.0 * lin_x,
            -2.0 * lin_y,
            -2.0 * lin_z,
            offset,
            collide,
        ]
    )


def ghost_slots(adjacency, counts, cells, groups, slot_count):
    ends = jnp.cumsum(counts) * TILE
    starts = ends - counts * TILE
    is_local = adjacency < cells
    position = jnp.maximum(adjacency - cells, 0)
    source = jnp.sum((ends[:, None, None] <= position[None]).astype(jnp.int32), axis=0)
    source = jnp.minimum(source, groups - 1)
    group_ids = jnp.arange(groups, dtype=jnp.int32)[:, None, None]
    chosen = jnp.sum(jnp.where(group_ids == source[None], starts[:, None, None], 0), axis=0)
    slot_pos = jnp.clip(position - chosen, 0, slot_count - 1)
    return (is_local, source, slot_pos)


def relax(current, neighbours, velocity, normals, params, norm_z, equilibrium):
    gauss = params[0][None, :] * equilibrium / norm_z[None, :]
    outflow = jnp.zeros(current.shape, jnp.float32)
    inflow = jnp.zeros(current.shape, jnp.float32)
    for side in range(normals.shape[0]):
        normal_speed = (
            velocity[0][:, None] * normals[side, 0][None, :]
            + velocity[1][:, None] * normals[side, 1][None, :]
            + velocity[2][:, None] * normals[side, 2][None, :]
        )
        outflow = outflow + jnp.maximum(normal_speed, 0.0)
        inflow = inflow + jnp.minimum(normal_speed, 0.0) * neighbours[side]
    return current + time_step * (
        params[23][None, :] * (gauss - current) - outflow * current - inflow
    )


def per_device(distribution, normals, adjacency, send_list, block_counts):
    vel_local = distribution.shape[0]
    cells = distribution.shape[1]
    total_vel = vel_local * lax.axis_size("vel")
    z_count = total_vel // (VXY * VXY)
    groups = send_list.shape[1]
    slot_count = send_list.shape[2]
    vel_index = lax.axis_index("vel") * vel_local + jnp.arange(vel_local, dtype=jnp.int32)
    velocity = velocity_nodes(vel_index, z_count)
    moment_table = moment_rows(velocity)
    quad_table = quad_rows(velocity).T
    is_local, source, slot_pos = ghost_slots(
        adjacency, block_counts[:, 0], cells, groups, slot_count
    )
    ghost_index = source * slot_count + slot_pos
    local_index = jnp.where(is_local, adjacency, 0)
    send_rows = send_list[0].reshape(-1)

    def reduce_moments(current):
        partial_value = (
            jnp.dot(
                moment_table,
                current,
                precision=lax.Precision.HIGHEST,
                preferred_element_type=jnp.float32,
            )
            / total_vel
        )
        return macroscopic(lax.psum(partial_value, "vel"))

    current = distribution
    for iteration in range(ITERS):
        params = reduce_moments(current)
        ghosts = lax.all_to_all(
            jnp.take(current, send_rows, axis=1), "space", split_axis=1, concat_axis=1, tiled=True
        )
        exponent = jnp.dot(
            quad_table,
            params[13:23],
            precision=lax.Precision.HIGHEST,
            preferred_element_type=jnp.float32,
        )
        equilibrium = jnp.exp(-0.5 * exponent)
        norm_z = lax.psum(jnp.sum(equilibrium, axis=0) / total_vel, "vel")
        neighbours = [
            jnp.where(
                is_local[side][None, :],
                jnp.take(current, local_index[side], axis=1),
                jnp.take(ghosts, ghost_index[side], axis=1),
            )
            for side in range(normals.shape[0])
        ]
        current = relax(current, neighbours, velocity, normals, params, norm_z, equilibrium)
    final = reduce_moments(current)
    return (current, final[:13])


MESH = pl.DeviceIdType.MESH
LOG2E = 1.4426950408889634
QUAD = 4
CHUNKS = 4
PIECES = 16
ISSUE = (1, 4, 1, 0, 0, 1, 1, 1, 1, 1, 1, 16)
TAKEN = (0, 8, 12, 16)
PLACES = (2, 2)
SLABS = 2
HI = lax.Precision.HIGHEST


def coefficient_rows(m):
    full = macroscopic_rows(m)
    scale = -0.5 * LOG2E
    return full[:13], [row * scale for row in full[13:23]], full[23]


def macroscopic_rows(m):
    density = m[0]
    inv_d = 1.0 / density
    ux, uy, uz = (m[1] * inv_d, m[2] * inv_d, m[3] * inv_d)
    b = [m[r] * inv_d for r in range(4, 10)]
    third = [m[r] * inv_d for r in range(10, 13)]
    txx, tyy, tzz = (b[0] - ux * ux, b[1] - uy * uy, b[2] - uz * uz)
    txy, txz, tyz = (b[3] - ux * uy, b[4] - ux * uz, b[5] - uy * uz)
    temper = (txx + tyy + tzz) * (1.0 / 3.0)
    trace_b = b[0] + b[1] + b[2]
    bux = b[0] * ux + b[3] * uy + b[4] * uz
    buy = b[3] * ux + b[1] * uy + b[5] * uz
    buz = b[4] * ux + b[5] * uy + b[2] * uz
    usq = ux * ux + uy * uy + uz * uz
    qx = 0.5 * (third[0] - 2.0 * bux - ux * trace_b + 2.0 * ux * usq)
    qy = 0.5 * (third[1] - 2.0 * buy - uy * trace_b + 2.0 * uy * usq)
    qz = 0.5 * (third[2] - 2.0 * buz - uz * trace_b + 2.0 * uz * usq)
    iso = (1.0 - ellipsoid_mix) * temper
    lxx, lyy, lzz = (iso + ellipsoid_mix * txx, iso + ellipsoid_mix * tyy, iso + ellipsoid_mix * tzz)
    lxy, lxz, lyz = (ellipsoid_mix * txy, ellipsoid_mix * txz, ellipsoid_mix * tyz)
    cxx = lyy * lzz - lyz * lyz
    cxy = lyz * lxz - lxy * lzz
    cxz = lxy * lyz - lyy * lxz
    cyy = lxx * lzz - lxz * lxz
    cyz = lxy * lxz - lxx * lyz
    czz = lxx * lyy - lxy * lxy
    inv_det = 1.0 / (lxx * cxx + lxy * cxy + lxz * cxz)
    ixx, iyy, izz = (cxx * inv_det, cyy * inv_det, czz * inv_det)
    ixy, ixz, iyz = (cxy * inv_det, cxz * inv_det, cyz * inv_det)
    wx = ixx * ux + ixy * uy + ixz * uz
    wy = ixy * ux + iyy * uy + iyz * uz
    wz = ixz * ux + iyz * uy + izz * uz
    offset = ux * wx + uy * wy + uz * wz
    collide = prandtl * density * jnp.exp(visc_power * jnp.log(temper))
    return [
        density, ux, uy, uz, txx, tyy, tzz, txy, txz, tyz, qx, qy, qz,
        ixx, iyy, izz, 2.0 * ixy, 2.0 * ixz, 2.0 * iyz,
        -2.0 * wx, -2.0 * wy, -2.0 * wz, offset, collide,
    ]


def node_velocity(index, z_count):
    shift = VXY.bit_length() - 1
    centre = (VXY - 1) / 2.0
    vx = ((index & (VXY - 1)).astype(jnp.float32) - centre) * spacing
    vy = (((index >> shift) & (VXY - 1)).astype(jnp.float32) - centre) * spacing
    vz = ((index >> (2 * shift)).astype(jnp.float32) - (z_count - 1) / 2.0) * spacing
    return vx, vy, vz


def x_column(first, rows, width):
    index = lax.broadcasted_iota(jnp.int32, (rows, width), 0) + first
    return (index.astype(jnp.float32) - (VXY - 1) / 2.0) * spacing


def pair_polynomials(half):
    def grow(before, now):
        rows = [now]
        for _ in range(half - 1):
            shifted = [0.0] + rows[-1]
            twice = [2.0 * v for v in rows[-1]] + [0.0]
            older = before + [0.0] * (len(shifted) - len(before))
            before = rows[-1]
            rows.append([x + y - z for x, y, z in zip(shifted, twice, older)])
        return rows

    return grow([1.0], [1.0]), grow([-1.0], [1.0])


def level_coefficients(q, z_count, powers):
    half = z_count // 2
    even, odd = pair_polynomials(half)
    weights = [jnp.exp2(q[2] * ((k + 0.5) * spacing) ** 2) for k in range(half)]
    result = []
    for c in range(powers):
        table = odd if c % 2 else even
        row = []
        for j in range(half):
            total = None
            for k in range(j, half):
                term = weights[k] * (table[k][j] * ((k + 0.5) * spacing) ** c)
                total = term if total is None else total + term
            row.append(total)
        result.append(row)
    return result


def horner(row, x):
    value = row[-1]
    for c in row[-2::-1]:
        value = value * x + c
    return value


def gauss_columns(q, width, block):
    step = 0.5 * spacing
    vx = x_column(block * 8, 8, width)
    base = (q[0] * vx + q[6]) * vx + q[9]
    lean = q[3] * vx + q[7]
    rise = (q[4] * vx + q[8]) * step
    for j in range(VXY // 2):
        vy = (j + 0.5) * spacing
        mid = base + q[1] * (vy * vy)
        tilt = lean * vy
        side = q[5] * (vy * step)
        columns = []
        for sign in (1.0, -1.0):
            flat = jnp.exp2(mid + tilt if sign > 0 else mid - tilt)
            slope = rise + side if sign > 0 else rise - side
            up, down = jnp.exp2(slope), jnp.exp2(-slope)
            diff = up - down
            columns.append((flat * (up + down), flat * diff, diff * diff))
        yield vx, vy, columns


def gauss_total(q, width, z_count):
    (even,) = level_coefficients(q, z_count, 1)

    def block(b, acc):
        for _, _, columns in gauss_columns(q, width, b):
            for plus, _, delta in columns:
                acc = acc + plus * horner(even, delta)
        return acc

    acc = lax.fori_loop(0, VXY // 8, block, jnp.zeros((8, width), jnp.float32))
    return jnp.sum(acc, axis=0, keepdims=True)


def gauss_moments(q, width, z_count):
    levels = level_coefficients(q, z_count, 4)
    zero = jnp.zeros((8, width), jnp.float32)

    def block(b, carry):
        sums = [[zero] * n for n in (4, 3, 2, 1)]
        for vx, vy, ((p_up, d_up, x_up), (p_down, d_down, x_down)) in gauss_columns(q, width, b):
            for c in range(4):
                above = (d_up if c % 2 else p_up) * horner(levels[c], x_up)
                below = (d_down if c % 2 else p_down) * horner(levels[c], x_down)
                both = above + below
                sums[c][0] = sums[c][0] + both
                if c < 3:
                    diff = (above - below) * vy
                    sums[c][1] = sums[c][1] + diff
                if c < 2:
                    sums[c][2] = sums[c][2] + both * (vy * vy)
                if c < 1:
                    sums[c][3] = sums[c][3] + diff * (vy * vy)
        (s0, s1, s2, s3), (z0, z1, z2), (zz0, zz1), (zc,) = sums
        vxx = vx * vx
        new = (
            s0, vx * s0, s1, z0, vxx * s0, s2, zz0, vx * s1, vx * z0, z1,
            vx * (vxx * s0 + s2 + zz0), vxx * s1 + s3 + zz1, vxx * z0 + z2 + zc,
        )
        return tuple(x + y for x, y in zip(carry, new))

    terms = lax.fori_loop(0, VXY // 8, block, (zero,) * 13)
    return [jnp.sum(t, axis=0, keepdims=True) for t in terms]


def split_dot(lhs, rhs):
    return jnp.dot(lhs, rhs, precision=HI, preferred_element_type=jnp.float32)


def step_kernel(
    total_vel,
    f_hbm, n_hbm, adj_hbm, send_hbm,
    out_ref, fields_ref,
    f_ref, n_ref, adj_ref, send_ref, load_s,
    fx, nx, adjx, sendx, ncat, xn, oh, tr0, split, wide, fnew, tr1, phi_ref, phi_parts,
    qb0, zb0, total_mine, total_theirs, qb1, zb1, qb2, zb2, lent0, got0, lent1, got1,
    bulk_s, bulk_r, meta_s, meta_r, stage_s, stage_r,
):
    nodes, cells = f_hbm.shape
    both = 2 * cells
    faces = n_hbm.shape[1]
    z_count = total_vel // (VXY * VXY)
    rows = nodes // CHUNKS
    group = lax.axis_index("space")
    other = 1 - group
    vel = lax.axis_index("vel")
    ring = total_vel // nodes // QUAD
    me_q = lax.rem(vel, QUAD)
    me_z = vel // QUAD

    def at(space, z, q):
        return (space, z * QUAD + q)

    def q_of(step):
        return lax.rem(me_q + step, QUAD)

    def z_of(step):
        return lax.rem(me_z + step, ring)

    def lay_rows(ref, moments, extra=None):
        for r in range(13):
            row = moments[r] if isinstance(moments, list) else moments[r : r + 1]
            ref[r] = row if extra is None else row + extra[r]

    barrier = pltpu.get_barrier_semaphore()
    for step in range(1, ring):
        pl.semaphore_signal(barrier, inc=1, device_id=at(group, z_of(step), me_q), device_id_type=MESH)
    for step in range(1, QUAD):
        pl.semaphore_signal(barrier, inc=1, device_id=at(group, me_z, q_of(step)), device_id_type=MESH)
    pl.semaphore_signal(barrier, inc=1, device_id=at(other, me_z, me_q), device_id_type=MESH)

    def chunk(c):
        return pl.ds(pl.multiple_of(c * rows, rows), rows)

    loads = [
        pltpu.make_async_copy(f_hbm.at[pl.ds(c * rows, rows)], f_ref.at[pl.ds(c * rows, rows)], load_s.at[c])
        for c in range(CHUNKS)
    ]
    small_loads = [
        pltpu.make_async_copy(src, dst, load_s.at[CHUNKS + i])
        for i, (src, dst) in enumerate([(send_hbm, send_ref), (adj_hbm, adj_ref), (n_hbm, n_ref)])
    ]
    for copy in loads + small_loads:
        copy.start()

    lane_v = node_velocity(lax.broadcasted_iota(jnp.int32, (1, nodes), 1) + vel * nodes, z_count)
    lx, ly, lz = lane_v
    sq = lx * lx + ly * ly + lz * lz
    table = [
        jnp.ones_like(lx), lx, ly, lz, lx * lx, ly * ly, lz * lz,
        lx * ly, lx * lz, ly * lz, lx * sq, ly * sq, lz * sq,
    ]
    row_id = lax.broadcasted_iota(jnp.int32, (16, nodes), 0)
    phi = jnp.zeros((16, nodes), jnp.float32)
    for r, row in enumerate(table):
        phi = jnp.where(row_id == r, row, phi)
    phi_ref[...] = phi
    rest = phi
    for i in range(3):
        leading = rest.astype(jnp.bfloat16)
        phi_parts[i * 16 : (i + 1) * 16, :] = leading
        rest = rest - leading.astype(jnp.float32)
    with jax.named_scope("W_bar"):
        pl.semaphore_wait(barrier, QUAD + ring - 1)

    def remote(src, dst, s, r, dev):
        return pltpu.make_async_remote_copy(
            src_ref=src, dst_ref=dst, send_sem=s, recv_sem=r, device_id=dev, device_id_type=MESH
        )

    pair = at(other, me_z, me_q)

    piece = nodes // PIECES

    plan, started = iter(ISSUE), []

    def more():
        first = len(started)
        last = min(PIECES, first + next(plan))
        for c in range(first, last):
            started.append(c)
            part = pl.ds(c * piece, piece)
            remote(f_hbm.at[part], fx.at[part], bulk_s, bulk_r.at[sum(c >= t for t in TAKEN) - 1], pair).start()

    metas = [
        remote(send_hbm, sendx, meta_s.at[0], meta_r.at[0], pair),
        remote(adj_hbm, adjx, meta_s.at[1], meta_r.at[1], pair),
        remote(n_hbm, nx, meta_s.at[2], meta_r.at[2], pair),
    ]
    for copy in metas:
        copy.start()
    more()

    def two_dot(part, state):
        high = state.astype(jnp.bfloat16)
        low = (state - high.astype(jnp.float32)).astype(jnp.bfloat16)
        lead = jnp.dot(phi_parts[:, part], high, preferred_element_type=jnp.float32)
        tail = jnp.dot(phi_parts[0:32, part], low, preferred_element_type=jnp.float32)
        return lead[0:16] + (lead[16:32] + tail[0:16]) + (lead[32:48] + tail[16:32])

    inv_total = 1.0 / total_vel
    partial = jnp.zeros((16, cells), jnp.float32)
    for c in range(CHUNKS):
        loads[c].wait()
        part = slice(c * rows, (c + 1) * rows)
        partial = partial + two_dot(part, f_ref[part, :])
    lay_rows(qb0.at[me_q], partial * inv_total)

    def in_quad(buffer, i):
        for t in range(1, QUAD):
            remote(buffer.at[me_q], buffer.at[me_q], stage_s.at[i], stage_r.at[i], at(group, me_z, q_of(t))).start()

    def along_z(buffer, i):
        for t in range(1, ring):
            remote(buffer.at[me_z], buffer.at[me_z], stage_s.at[i], stage_r.at[i], at(group, z_of(t), me_q)).start()

    def across(src, dst, i):
        remote(src, dst, stage_s.at[i], stage_r.at[i], pair).start()

    def arrived(dst, i):
        with jax.named_scope(f"W_stage{i}"):
            pltpu.make_async_copy(dst, dst, stage_r.at[i]).wait()

    def all_of(buffer, sem, count):
        part = buffer.at[pl.ds(0, count)]
        pltpu.make_async_copy(part, part, sem).wait()

    def collect(i, buffer, count):
        with jax.named_scope(f"W_stage{i}"):
            all_of(buffer, stage_r.at[i], count - 1)
        rows13 = []
        for r in range(13):
            row = buffer[0, r]
            for t in range(1, count):
                row = row + buffer[t, r]
            rows13.append(row)
        return rows13

    in_quad(qb0, 0)
    more()

    for copy in small_loads:
        copy.wait()
    mine, far = slice(0, cells), slice(cells, both)
    slot_id = lax.broadcasted_iota(jnp.int32, (cells, cells), 0)
    eye = (slot_id == lax.broadcasted_iota(jnp.int32, (cells, cells), 1)).astype(jnp.float32)
    vx_col = x_column(0, VXY, cells)

    def listed(send_row, adjacency):
        hit = jnp.where(slot_id == adjacency - cells, 1.0, 0.0).astype(jnp.bfloat16)
        values = jnp.broadcast_to(send_row, (8, cells)).astype(jnp.float32).astype(jnp.bfloat16)
        got = jnp.dot(values, hit, preferred_element_type=jnp.float32)
        return jnp.where(adjacency < cells, -1, got[0:1].astype(jnp.int32))

    def choose(k, source, target, index):
        hit = jnp.where(slot_id == index, 1.0, 0.0)
        oh[k, source, target] = (hit - eye if source == target else hit).astype(jnp.bfloat16)

    def lay_normals(ref, target):
        for d in range(3):
            lines = [ref[d, k : k + 1, :] for k in range(faces)]
            lines.append(sum(lines[1:], lines[0]))
            for k, line in enumerate(lines):
                if d == 0:
                    xn[k, :, target] = vx_col * line
                else:
                    ncat[d, k : k + 1, target] = line

    lay_normals(n_ref, mine)
    for k in range(faces):
        choose(k, mine, mine, adj_ref[k : k + 1, :])

    lay_rows(zb0.at[me_z], collect(0, qb0, QUAD))
    along_z(zb0, 1)
    more()

    with jax.named_scope("W_meta"):
        for copy in metas:
            copy.wait_recv()
    to_me = sendx[0, pl.ds(group, 1), :]
    to_other = send_ref[0, pl.ds(other, 1), :]
    lay_normals(nx, far)
    for k in range(faces):
        choose(k, mine, far, listed(to_other, adjx[k : k + 1, :]))

    centre = (VXY - 1) / 2.0
    shift = VXY.bit_length() - 1

    def line_velocity(first):
        line = (vel * nodes + first) // VXY
        vy = ((line & (VXY - 1)).astype(jnp.float32) - centre) * spacing
        vz = ((line >> shift).astype(jnp.float32) - (z_count - 1) / 2.0) * spacing
        return vy, vz

    def halves(state):
        high = state.astype(jnp.bfloat16)
        low = (state - high.astype(jnp.float32)).astype(jnp.bfloat16)
        return jnp.concatenate([high, low], axis=0)

    def transport(lhs, source, target, leaving, first, count):
        speeds = [line_velocity(first + sub * VXY) for sub in range(count // VXY)]

        def speed(k, sub):
            vy, vz = speeds[sub]
            return xn[k, :, target] + (vy * ncat[1, k : k + 1, target] + vz * ncat[2, k : k + 1, target])

        def lines(sub, offset=0):
            return slice(offset + sub * VXY, offset + (sub + 1) * VXY)

        result = [
            None if leaving is None else leaving[lines(sub)] * speed(faces, sub) for sub in range(count // VXY)
        ]
        for k in range(faces):
            got = jnp.dot(lhs, oh[k, source, target], preferred_element_type=jnp.float32)
            for sub in range(count // VXY):
                value = got[lines(sub)]
                if lhs.shape[0] > count:
                    value = value + got[lines(sub, count)]
                term = jnp.minimum(speed(k, sub), 0.0) * value
                result[sub] = term if result[sub] is None else result[sub] + term
        return jnp.concatenate(result, axis=0)

    def equilibrium(quad, first, count):
        square = quad[0] * vx_col
        parts = []
        for sub in range(count // VXY):
            vy, vz = line_velocity(first + sub * VXY)
            slope = quad[3] * vy + quad[4] * vz + quad[6]
            level = vy * (quad[1] * vy + quad[5] * vz + quad[7]) + (vz * (quad[2] * vz + quad[8]) + quad[9])
            parts.append(jnp.exp2(vx_col * (square + slope) + level))
        return jnp.concatenate(parts, axis=0)

    blocks = [(c * (nodes // SLABS), nodes // SLABS) for c in range(SLABS)]
    sent = jnp.zeros((16, cells), jnp.float32)
    with jax.named_scope("T0p_far"):
        for first, count in blocks:
            part = slice(first, first + count)
            lhs = halves(f_ref[part, :])
            split[2 * first : 2 * (first + count), :] = lhs
            moved = transport(lhs[:count], mine, far, None, first, count)
            tr0[part, far] = moved
            sent = sent + two_dot(part, moved)
            more()
    lay_rows(lent0, sent * (-time_step * inv_total))
    across(lent0, got0, 7)
    more()
    with jax.named_scope("T0p_mine"):
        for first, count in blocks:
            part = slice(first, first + count)
            lhs = split[2 * first : 2 * (first + count), :]
            tr0[part, mine] = transport(lhs, mine, mine, f_ref[part, :], first, count)
            more()

    with jax.named_scope("oh2"):
        for k in range(faces):
            choose(k, far, mine, listed(to_me, adj_ref[k : k + 1, :]))
            theirs = adjx[k : k + 1, :]
            choose(k, far, far, theirs)

    more()
    fields0, own_quad, freq0 = coefficient_rows(collect(1, zb0, ring))
    more()
    with jax.named_scope("G_tot0"):
        norm0 = gauss_total(own_quad, cells, z_count) * inv_total
    own_gain = time_step * freq0 * fields0[0] / norm0
    own_keep = 1.0 - time_step * freq0
    for r, row in enumerate(own_quad + [own_gain, own_keep]):
        total_mine[r] = row
    across(total_mine, total_theirs, 2)
    more()

    with jax.named_scope("f1p"):
        for first, count in blocks:
            part = slice(first, first + count)
            state = (
                own_keep * f_ref[part, :] - time_step * tr0[part, mine] + own_gain * equilibrium(own_quad, first, count)
            )
            fnew[part, :] = state
            wide[part, mine] = state.astype(jnp.bfloat16)
            away = -time_step * tr0[part, far]
            tr0[part, far] = away
            wide[part, far] = away.astype(jnp.bfloat16)
        kept = two_dot(slice(0, nodes), fnew[...]) * inv_total
    arrived(got0, 7)
    lay_rows(qb1.at[me_q], kept, got0)
    in_quad(qb1, 3)

    def second_moments(target, leaving):
        part = slice(0, nodes)
        moved = transport(wide[part, :], slice(0, both), target, leaving(part), 0, nodes)
        return two_dot(part, moved) * inv_total

    with jax.named_scope("T1p_far"):
        lay_rows(lent1, second_moments(far, lambda part: tr0[part, far]))
    across(lent1, got1, 8)
    more()
    with jax.named_scope("T1p_mine"):
        stay = second_moments(mine, lambda part: fnew[part, :])

    def received(i):
        first, last = TAKEN[i] * piece, TAKEN[i + 1] * piece
        count, part = last - first, slice(first, last)
        with jax.named_scope("W_bulk"):
            ref = fx.at[pl.ds(first, count)]
            pltpu.make_async_copy(ref, ref, bulk_r.at[i]).wait()
        their_quad = [total_theirs[r] for r in range(10)]
        their_gain, their_keep = total_theirs[10], total_theirs[11]
        state = fx[part, :]
        lhs = halves(state)
        here = fnew[part, :] - time_step * transport(lhs, far, mine, None, first, count)
        there = (
            their_keep * state
            + (tr0[part, far] - time_step * transport(lhs[:count], far, far, state, first, count))
            + their_gain * equilibrium(their_quad, first, count)
        )
        fnew[part, :] = here
        lhs = halves(jnp.concatenate([here, there], axis=1))
        tr1[part, :] = transport(lhs, slice(0, both), mine, here, first, count)

    lay_rows(zb1.at[me_z], collect(3, qb1, QUAD))
    along_z(zb1, 4)
    arrived(got1, 8)
    lay_rows(qb2.at[me_q], stay, got1)
    in_quad(qb2, 5)
    arrived(total_theirs, 2)
    for i in range(PLACES[0]):
        received(i)
    lay_rows(zb2.at[me_z], collect(5, qb2, QUAD))
    along_z(zb2, 6)
    for i in range(PLACES[0], PLACES[1]):
        received(i)
    mom1 = collect(4, zb1, ring)
    fields1, quad1, freq1 = coefficient_rows(mom1)
    with jax.named_scope("G_mom1"):
        sums = gauss_moments(quad1, cells, z_count)
    inv_sum = 1.0 / sums[0]
    lift = time_step * freq1 * fields1[0]
    gain1 = lift * inv_sum * float(total_vel)
    keep1 = 1.0 - time_step * freq1

    for i in range(PLACES[1], len(TAKEN) - 1):
        received(i)

    def finish(c, carry):
        part = chunk(c)
        out_ref[part, :] = (
            keep1 * fnew[part, :] - time_step * tr1[part, :] + gain1 * equilibrium(quad1, c * rows, rows)
        )
        return carry

    with jax.named_scope("fin"):
        lax.fori_loop(0, CHUNKS, finish, 0)
    mom_t = collect(6, zb2, ring)
    slope = lift * inv_sum
    last = [
        keep1 * mom1[r] - time_step * mom_t[r] + slope * sums[r] for r in range(13)
    ]
    final = macroscopic_rows(last)
    for r in range(13):
        fields_ref[r : r + 1, :] = final[r]
    with jax.named_scope("W_send"):
        pltpu.make_async_copy(fx, fx, bulk_s).wait()
        for copy in metas:
            copy.wait_send()
        for i, buffer in ((2, total_mine), (7, lent0), (8, lent1)):
            pltpu.make_async_copy(buffer, buffer, stage_s.at[i]).wait()
        for i, buffer, count in (
            (0, qb0, QUAD), (1, zb0, ring), (3, qb1, QUAD), (4, zb1, ring), (5, qb2, QUAD), (6, zb2, ring),
        ):
            all_of(buffer, stage_s.at[i], count - 1)


def store_kernel(state_ref, fields_ref, state_out, fields_out, sems):
    copies = [
        pltpu.make_async_copy(fields_ref, fields_out, sems.at[0]),
        pltpu.make_async_copy(state_ref, state_out, sems.at[1]),
    ]
    for copy in copies:
        copy.start()
    for copy in copies:
        copy.wait()


def per_device_pair(distribution, normals, adjacency, send_list, block_counts):
    nodes, cells = distribution.shape
    normals = normals.transpose(1, 0, 2)
    size = lax.axis_size("vel")
    ring = size // QUAD
    faces = normals.shape[1]
    f32 = jnp.float32
    dma = pltpu.SemaphoreType.DMA
    vmem = pl.BlockSpec(memory_space=pltpu.VMEM)
    hbm = pl.BlockSpec(memory_space=pltpu.HBM)
    shapes = (
        jax.ShapeDtypeStruct((nodes, cells), f32),
        jax.ShapeDtypeStruct((13, cells), f32),
    )
    state, fields = pl.pallas_call(
        functools.partial(step_kernel, nodes * size),
        out_shape=shapes,
        in_specs=[hbm] * 4,
        out_specs=(vmem, vmem),
        scratch_shapes=[
            pltpu.VMEM((nodes, cells), f32),
            pltpu.VMEM(normals.shape, f32),
            pltpu.VMEM(adjacency.shape, jnp.int32),
            pltpu.VMEM(send_list.shape, jnp.int32),
            dma((CHUNKS + 3,)),
            pltpu.VMEM((nodes, cells), f32),
            pltpu.VMEM(normals.shape, f32),
            pltpu.VMEM(adjacency.shape, jnp.int32),
            pltpu.VMEM(send_list.shape, jnp.int32),
            pltpu.VMEM((3, 8, 2 * cells), f32),
            pltpu.VMEM((faces + 1, VXY, 2 * cells), f32),
            pltpu.VMEM((faces, 2 * cells, 2 * cells), jnp.bfloat16),
            pltpu.VMEM((nodes, 2 * cells), f32),
            pltpu.VMEM((2 * nodes, cells), jnp.bfloat16),
            pltpu.VMEM((nodes, 2 * cells), jnp.bfloat16),
            pltpu.VMEM((nodes, cells), f32),
            pltpu.VMEM((nodes, cells), f32),
            pltpu.VMEM((16, nodes), f32),
            pltpu.VMEM((48, nodes), jnp.bfloat16),
            pltpu.VMEM((QUAD, 13, 1, cells), f32),
            pltpu.VMEM((ring, 13, 1, cells), f32),
            pltpu.VMEM((12, 1, cells), f32),
            pltpu.VMEM((12, 1, cells), f32),
            pltpu.VMEM((QUAD, 13, 1, cells), f32),
            pltpu.VMEM((ring, 13, 1, cells), f32),
            pltpu.VMEM((QUAD, 13, 1, cells), f32),
            pltpu.VMEM((ring, 13, 1, cells), f32),
            pltpu.VMEM((13, 1, cells), f32),
            pltpu.VMEM((13, 1, cells), f32),
            pltpu.VMEM((13, 1, cells), f32),
            pltpu.VMEM((13, 1, cells), f32),
            dma, dma((len(TAKEN) - 1,)), dma((3,)), dma((3,)), dma((9,)), dma((9,)),
        ],
        compiler_params=pltpu.CompilerParams(
            collective_id=0, has_side_effects=True, vmem_limit_bytes=16 * 1024 * 1024
        ),
        name="steps",
    )(*[pltpu.with_memory_space_constraint(x, pltpu.HBM) for x in (distribution, normals, adjacency, send_list)])
    anywhere = pl.BlockSpec(memory_space=pl.ANY)
    return pl.pallas_call(
        store_kernel,
        out_shape=shapes,
        in_specs=[anywhere, anywhere],
        out_specs=(hbm, hbm),
        scratch_shapes=[dma((2,))],
        compiler_params=pltpu.CompilerParams(vmem_limit_bytes=16 * 1024 * 1024),
        name="store",
    )(state, fields)


def solution(mesh):
    placed = (
        P("vel", "space"),
        P(None, None, "space"),
        P(None, "space"),
        P("space", None, None),
        P(None, "space"),
    )
    pair = mesh.shape["space"] == 2 and mesh.shape["vel"] % QUAD == 0 and ITERS == 2
    return jax.shard_map(
        per_device_pair if pair else per_device,
        mesh=mesh,
        in_specs=placed,
        out_specs=(P("vel", "space"), P(None, "space")),
        check_vma=False,
    )
```

```python
import functools

import jax
import jax.numpy as jnp
from jax import lax
from jax.experimental import pallas as pl
from jax.experimental.pallas import tpu as pltpu
from jax.sharding import PartitionSpec as P

VXY = 32
TILE = 128
ITERS = 2


spacing = 0.3
ellipsoid_mix = -0.25
prandtl = 0.8
visc_power = 0.26
time_step = 0.025


def velocity_nodes(vel_index, z_count):
    comp_x = (vel_index % VXY).astype(jnp.float32)
    comp_y = (vel_index // VXY % VXY).astype(jnp.float32)
    comp_z = (vel_index // (VXY * VXY)).astype(jnp.float32)
    centre = (VXY - 1) / 2.0
    return jnp.stack(
        [
            (comp_x - centre) * spacing,
            (comp_y - centre) * spacing,
            (comp_z - (z_count - 1) / 2.0) * spacing,
        ]
    )


def moment_rows(velocity):
    comp_x, comp_y, comp_z = (velocity[0], velocity[1], velocity[2])
    squared = comp_x * comp_x + comp_y * comp_y + comp_z * comp_z
    return jnp.stack(
        [
            jnp.ones_like(comp_x),
            comp_x,
            comp_y,
            comp_z,
            comp_x * comp_x,
            comp_y * comp_y,
            comp_z * comp_z,
            comp_x * comp_y,
            comp_x * comp_z,
            comp_y * comp_z,
            comp_x * squared,
            comp_y * squared,
            comp_z * squared,
        ]
    )


def quad_rows(velocity):
    comp_x, comp_y, comp_z = (velocity[0], velocity[1], velocity[2])
    return jnp.stack(
        [
            comp_x * comp_x,
            comp_y * comp_y,
            comp_z * comp_z,
            comp_x * comp_y,
            comp_x * comp_z,
            comp_y * comp_z,
            comp_x,
            comp_y,
            comp_z,
            jnp.ones_like(comp_x),
        ]
    )


def macroscopic(moments):
    density = moments[0]
    mean_x = moments[1] / density
    mean_y = moments[2] / density
    mean_z = moments[3] / density
    second = moments[4:10] / density[None, :]
    third = moments[10:13] / density[None, :]
    theta_xx = second[0] - mean_x * mean_x
    theta_yy = second[1] - mean_y * mean_y
    theta_zz = second[2] - mean_z * mean_z
    theta_xy = second[3] - mean_x * mean_y
    theta_xz = second[4] - mean_x * mean_z
    theta_yz = second[5] - mean_y * mean_z
    temper = (theta_xx + theta_yy + theta_zz) / 3.0
    trace_b = second[0] + second[1] + second[2]
    bu_x = second[0] * mean_x + second[3] * mean_y + second[4] * mean_z
    bu_y = second[3] * mean_x + second[1] * mean_y + second[5] * mean_z
    bu_z = second[4] * mean_x + second[5] * mean_y + second[2] * mean_z
    mean_sq = mean_x * mean_x + mean_y * mean_y + mean_z * mean_z
    flux_x = 0.5 * (third[0] - 2.0 * bu_x - mean_x * trace_b + 2.0 * mean_x * mean_sq)
    flux_y = 0.5 * (third[1] - 2.0 * bu_y - mean_y * trace_b + 2.0 * mean_y * mean_sq)
    flux_z = 0.5 * (third[2] - 2.0 * bu_z - mean_z * trace_b + 2.0 * mean_z * mean_sq)
    iso_part = (1.0 - ellipsoid_mix) * temper
    lam_xx = iso_part + ellipsoid_mix * theta_xx
    lam_yy = iso_part + ellipsoid_mix * theta_yy
    lam_zz = iso_part + ellipsoid_mix * theta_zz
    lam_xy = ellipsoid_mix * theta_xy
    lam_xz = ellipsoid_mix * theta_xz
    lam_yz = ellipsoid_mix * theta_yz
    cof_xx = lam_yy * lam_zz - lam_yz * lam_yz
    cof_xy = lam_yz * lam_xz - lam_xy * lam_zz
    cof_xz = lam_xy * lam_yz - lam_yy * lam_xz
    cof_yy = lam_xx * lam_zz - lam_xz * lam_xz
    cof_yz = lam_xy * lam_xz - lam_xx * lam_yz
    cof_zz = lam_xx * lam_yy - lam_xy * lam_xy
    determinant = lam_xx * cof_xx + lam_xy * cof_xy + lam_xz * cof_xz
    inv_xx = cof_xx / determinant
    inv_yy = cof_yy / determinant
    inv_zz = cof_zz / determinant
    inv_xy = cof_xy / determinant
    inv_xz = cof_xz / determinant
    inv_yz = cof_yz / determinant
    lin_x = inv_xx * mean_x + inv_xy * mean_y + inv_xz * mean_z
    lin_y = inv_xy * mean_x + inv_yy * mean_y + inv_yz * mean_z
    lin_z = inv_xz * mean_x + inv_yz * mean_y + inv_zz * mean_z
    offset = mean_x * lin_x + mean_y * lin_y + mean_z * lin_z
    collide = prandtl * density * jnp.exp(visc_power * jnp.log(temper))
    return jnp.stack(
        [
            density,
            mean_x,
            mean_y,
            mean_z,
            theta_xx,
            theta_yy,
            theta_zz,
            theta_xy,
            theta_xz,
            theta_yz,
            flux_x,
            flux_y,
            flux_z,
            inv_xx,
            inv_yy,
            inv_zz,
            2.0 * inv_xy,
            2.0 * inv_xz,
            2.0 * inv_yz,
            -2.0 * lin_x,
            -2.0 * lin_y,
            -2.0 * lin_z,
            offset,
            collide,
        ]
    )


def ghost_slots(adjacency, counts, cells, groups, slot_count):
    ends = jnp.cumsum(counts) * TILE
    starts = ends - counts * TILE
    is_local = adjacency < cells
    position = jnp.maximum(adjacency - cells, 0)
    source = jnp.sum((ends[:, None, None] <= position[None]).astype(jnp.int32), axis=0)
    source = jnp.minimum(source, groups - 1)
    group_ids = jnp.arange(groups, dtype=jnp.int32)[:, None, None]
    chosen = jnp.sum(jnp.where(group_ids == source[None], starts[:, None, None], 0), axis=0)
    slot_pos = jnp.clip(position - chosen, 0, slot_count - 1)
    return (is_local, source, slot_pos)


def relax(current, neighbours, velocity, normals, params, norm_z, equilibrium):
    gauss = params[0][None, :] * equilibrium / norm_z[None, :]
    outflow = jnp.zeros(current.shape, jnp.float32)
    inflow = jnp.zeros(current.shape, jnp.float32)
    for side in range(normals.shape[0]):
        normal_speed = (
            velocity[0][:, None] * normals[side, 0][None, :]
            + velocity[1][:, None] * normals[side, 1][None, :]
            + velocity[2][:, None] * normals[side, 2][None, :]
        )
        outflow = outflow + jnp.maximum(normal_speed, 0.0)
        inflow = inflow + jnp.minimum(normal_speed, 0.0) * neighbours[side]
    return current + time_step * (
        params[23][None, :] * (gauss - current) - outflow * current - inflow
    )


def per_device(distribution, normals, adjacency, send_list, block_counts):
    vel_local = distribution.shape[0]
    cells = distribution.shape[1]
    total_vel = vel_local * lax.axis_size("vel")
    z_count = total_vel // (VXY * VXY)
    groups = send_list.shape[1]
    slot_count = send_list.shape[2]
    vel_index = lax.axis_index("vel") * vel_local + jnp.arange(vel_local, dtype=jnp.int32)
    velocity = velocity_nodes(vel_index, z_count)
    moment_table = moment_rows(velocity)
    quad_table = quad_rows(velocity).T
    is_local, source, slot_pos = ghost_slots(
        adjacency, block_counts[:, 0], cells, groups, slot_count
    )
    ghost_index = source * slot_count + slot_pos
    local_index = jnp.where(is_local, adjacency, 0)
    send_rows = send_list[0].reshape(-1)

    def reduce_moments(current):
        partial_value = (
            jnp.dot(
                moment_table,
                current,
                precision=lax.Precision.HIGHEST,
                preferred_element_type=jnp.float32,
            )
            / total_vel
        )
        return macroscopic(lax.psum(partial_value, "vel"))

    current = distribution
    for iteration in range(ITERS):
        params = reduce_moments(current)
        ghosts = lax.all_to_all(
            jnp.take(current, send_rows, axis=1), "space", split_axis=1, concat_axis=1, tiled=True
        )
        exponent = jnp.dot(
            quad_table,
            params[13:23],
            precision=lax.Precision.HIGHEST,
            preferred_element_type=jnp.float32,
        )
        equilibrium = jnp.exp(-0.5 * exponent)
        norm_z = lax.psum(jnp.sum(equilibrium, axis=0) / total_vel, "vel")
        neighbours = [
            jnp.where(
                is_local[side][None, :],
                jnp.take(current, local_index[side], axis=1),
                jnp.take(ghosts, ghost_index[side], axis=1),
            )
            for side in range(normals.shape[0])
        ]
        current = relax(current, neighbours, velocity, normals, params, norm_z, equilibrium)
    final = reduce_moments(current)
    return (current, final[:13])


MESH = pl.DeviceIdType.MESH
LOG2E = 1.4426950408889634
QUAD = 4
CHUNKS = 4
PIECES = 16
ISSUE = (1, 4, 1, 0, 0, 1, 1, 1, 1, 1, 1, 16)
TAKEN = (0, 8, 12, 16)
PLACES = (2, 2)
SLABS = 2
HI = lax.Precision.HIGHEST


def coefficient_rows(m):
    full = macroscopic_rows(m)
    scale = -0.5 * LOG2E
    return full[:13], [row * scale for row in full[13:23]], full[23]


def macroscopic_rows(m):
    density = m[0]
    inv_d = 1.0 / density
    ux, uy, uz = (m[1] * inv_d, m[2] * inv_d, m[3] * inv_d)
    b = [m[r] * inv_d for r in range(4, 10)]
    third = [m[r] * inv_d for r in range(10, 13)]
    txx, tyy, tzz = (b[0] - ux * ux, b[1] - uy * uy, b[2] - uz * uz)
    txy, txz, tyz = (b[3] - ux * uy, b[4] - ux * uz, b[5] - uy * uz)
    temper = (txx + tyy + tzz) * (1.0 / 3.0)
    trace_b = b[0] + b[1] + b[2]
    bux = b[0] * ux + b[3] * uy + b[4] * uz
    buy = b[3] * ux + b[1] * uy + b[5] * uz
    buz = b[4] * ux + b[5] * uy + b[2] * uz
    usq = ux * ux + uy * uy + uz * uz
    qx = 0.5 * (third[0] - 2.0 * bux - ux * trace_b + 2.0 * ux * usq)
    qy = 0.5 * (third[1] - 2.0 * buy - uy * trace_b + 2.0 * uy * usq)
    qz = 0.5 * (third[2] - 2.0 * buz - uz * trace_b + 2.0 * uz * usq)
    iso = (1.0 - ellipsoid_mix) * temper
    lxx, lyy, lzz = (iso + ellipsoid_mix * txx, iso + ellipsoid_mix * tyy, iso + ellipsoid_mix * tzz)
    lxy, lxz, lyz = (ellipsoid_mix * txy, ellipsoid_mix * txz, ellipsoid_mix * tyz)
    cxx = lyy * lzz - lyz * lyz
    cxy = lyz * lxz - lxy * lzz
    cxz = lxy * lyz - lyy * lxz
    cyy = lxx * lzz - lxz * lxz
    cyz = lxy * lxz - lxx * lyz
    czz = lxx * lyy - lxy * lxy
    inv_det = 1.0 / (lxx * cxx + lxy * cxy + lxz * cxz)
    ixx, iyy, izz = (cxx * inv_det, cyy * inv_det, czz * inv_det)
    ixy, ixz, iyz = (cxy * inv_det, cxz * inv_det, cyz * inv_det)
    wx = ixx * ux + ixy * uy + ixz * uz
    wy = ixy * ux + iyy * uy + iyz * uz
    wz = ixz * ux + iyz * uy + izz * uz
    offset = ux * wx + uy * wy + uz * wz
    collide = prandtl * density * jnp.exp(visc_power * jnp.log(temper))
    return [
        density, ux, uy, uz, txx, tyy, tzz, txy, txz, tyz, qx, qy, qz,
        ixx, iyy, izz, 2.0 * ixy, 2.0 * ixz, 2.0 * iyz,
        -2.0 * wx, -2.0 * wy, -2.0 * wz, offset, collide,
    ]


def node_velocity(index, z_count):
    shift = VXY.bit_length() - 1
    centre = (VXY - 1) / 2.0
    vx = ((index & (VXY - 1)).astype(jnp.float32) - centre) * spacing
    vy = (((index >> shift) & (VXY - 1)).astype(jnp.float32) - centre) * spacing
    vz = ((index >> (2 * shift)).astype(jnp.float32) - (z_count - 1) / 2.0) * spacing
    return vx, vy, vz


def x_column(first, rows, width):
    index = lax.broadcasted_iota(jnp.int32, (rows, width), 0) + first
    return (index.astype(jnp.float32) - (VXY - 1) / 2.0) * spacing


def pair_polynomials(half):
    def grow(before, now):
        rows = [now]
        for _ in range(half - 1):
            shifted = [0.0] + rows[-1]
            twice = [2.0 * v for v in rows[-1]] + [0.0]
            older = before + [0.0] * (len(shifted) - len(before))
            before = rows[-1]
            rows.append([x + y - z for x, y, z in zip(shifted, twice, older)])
        return rows

    return grow([1.0], [1.0]), grow([-1.0], [1.0])


def level_coefficients(q, z_count, powers):
    half = z_count // 2
    even, odd = pair_polynomials(half)
    weights = [jnp.exp2(q[2] * ((k + 0.5) * spacing) ** 2) for k in range(half)]
    result = []
    for c in range(powers):
        table = odd if c % 2 else even
        row = []
        for j in range(half):
            total = None
            for k in range(j, half):
                term = weights[k] * (table[k][j] * ((k + 0.5) * spacing) ** c)
                total = term if total is None else total + term
            row.append(total)
        result.append(row)
    return result


def horner(row, x):
    value = row[-1]
    for c in row[-2::-1]:
        value = value * x + c
    return value


def gauss_columns(q, width, block):
    step = 0.5 * spacing
    vx = x_column(block * 8, 8, width)
    base = (q[0] * vx + q[6]) * vx + q[9]
    lean = q[3] * vx + q[7]
    rise = (q[4] * vx + q[8]) * step
    for j in range(VXY // 2):
        vy = (j + 0.5) * spacing
        mid = base + q[1] * (vy * vy)
        tilt = lean * vy
        side = q[5] * (vy * step)
        columns = []
        for sign in (1.0, -1.0):
            flat = jnp.exp2(mid + tilt if sign > 0 else mid - tilt)
            slope = rise + side if sign > 0 else rise - side
            up, down = jnp.exp2(slope), jnp.exp2(-slope)
            diff = up - down
            columns.append((flat * (up + down), flat * diff, diff * diff))
        yield vx, vy, columns


def gauss_total(q, width, z_count):
    (even,) = level_coefficients(q, z_count, 1)

    def block(b, acc):
        for _, _, columns in gauss_columns(q, width, b):
            for plus, _, delta in columns:
                acc = acc + plus * horner(even, delta)
        return acc

    acc = jnp.zeros((8, width), jnp.float32)
    for b in range(VXY // 8):
        acc = block(b, acc)
    return jnp.sum(acc, axis=0, keepdims=True)


def column_weights(block):
    k = lax.broadcasted_iota(jnp.int32, (1, 8 * VXY), 1)
    x = ((k & 7) + block * 8).astype(jnp.float32) - (VXY - 1) / 2.0
    y = (k >> 4).astype(jnp.float32) + 0.5
    y = jnp.where((k & 8) == 0, y, -y)
    square = x * x + y * y
    rows = [jnp.ones_like(x), x, y, x * x, y * y, x * y, x * square, y * square]
    row_id = lax.broadcasted_iota(jnp.int32, (8, 8 * VXY), 0)
    table = jnp.zeros((8, 8 * VXY), jnp.float32)
    for r, row in enumerate(rows):
        table = jnp.where(row_id == r, row, table)
    high = table.astype(jnp.bfloat16).astype(jnp.float32)
    return jnp.concatenate([high, table - high], axis=0).astype(jnp.bfloat16)


def gauss_moments(q, width, z_count, weights_ref):
    levels = level_coefficients(q, z_count, 4)
    half = z_count // 2
    zero = jnp.zeros((16, width), jnp.float32)

    def block(b, carry):
        tiles = [[] for _ in range(2 * half + 1)]
        for _, _, ((p_up, d_up, x_up), (p_down, d_down, x_down)) in gauss_columns(q, width, b):
            plus = jnp.concatenate([p_up, p_down], axis=0)
            diff = jnp.concatenate([d_up, d_down], axis=0)
            delta = jnp.concatenate([x_up, x_down], axis=0)
            for j in range(half):
                lead = plus.astype(jnp.bfloat16)
                tiles[j].append(lead)
                tiles[half + j].append(diff.astype(jnp.bfloat16))
                if j == 0:
                    tiles[2 * half].append((plus - lead.astype(jnp.float32)).astype(jnp.bfloat16))
                if j < half - 1:
                    plus, diff = plus * delta, diff * delta
        weights = weights_ref[b]
        sums = [
            jnp.dot(weights, jnp.concatenate(t, axis=0), preferred_element_type=jnp.float32) for t in tiles
        ]
        sums[0] = sums[0] + sums.pop()
        return tuple(x + y for x, y in zip(carry, sums))

    sums = (zero,) * (2 * half)
    for b in range(VXY // 8):
        sums = block(b, sums)
    sums = [t[:8] + t[8:] for t in sums]
    m0, m1, m2, m3 = [
        sum(levels[c][j] * sums[(c % 2) * half + j] for j in range(half)) for c in range(4)
    ]
    h = spacing
    row = lambda m, r: m[r : r + 1]
    return [
        row(m0, 0), h * row(m0, 1), h * row(m0, 2), row(m1, 0),
        h * h * row(m0, 3), h * h * row(m0, 4), row(m2, 0),
        h * h * row(m0, 5), h * row(m1, 1), h * row(m1, 2),
        h * (h * h * row(m0, 6) + row(m2, 1)), h * (h * h * row(m0, 7) + row(m2, 2)),
        h * h * (row(m1, 3) + row(m1, 4)) + row(m3, 0),
    ]


def step_kernel(
    total_vel,
    f_hbm, n_hbm, adj_hbm, send_hbm,
    out_ref, fields_ref,
    f_ref, n_ref, adj_ref, send_ref, load_s,
    fx, nx, adjx, sendx, ncat, xn, oh, tr0, split, wide, fnew, tr1, phi_parts, weights,
    qb0, zb0, total_mine, total_theirs, qb1, zb1, qb2, zb2, lent0, got0, lent1, got1,
    bulk_s, bulk_r, meta_s, meta_r, stage_s, stage_r,
):
    nodes, cells = f_hbm.shape
    both = 2 * cells
    faces = n_hbm.shape[1]
    z_count = total_vel // (VXY * VXY)
    rows = nodes // CHUNKS
    group = lax.axis_index("space")
    other = 1 - group
    vel = lax.axis_index("vel")
    ring = total_vel // nodes // QUAD
    me_q = lax.rem(vel, QUAD)
    me_z = vel // QUAD

    def at(space, z, q):
        return (space, z * QUAD + q)

    def q_of(step):
        return lax.rem(me_q + step, QUAD)

    def z_of(step):
        return lax.rem(me_z + step, ring)

    def lay_rows(ref, moments, extra=None):
        for r in range(13):
            row = moments[r] if isinstance(moments, list) else moments[r : r + 1]
            ref[r] = row if extra is None else row + extra[r]

    barrier = pltpu.get_barrier_semaphore()
    for step in range(1, ring):
        pl.semaphore_signal(barrier, inc=1, device_id=at(group, z_of(step), me_q), device_id_type=MESH)
    for step in range(1, QUAD):
        pl.semaphore_signal(barrier, inc=1, device_id=at(group, me_z, q_of(step)), device_id_type=MESH)
    for step in range(QUAD):
        pl.semaphore_signal(barrier, inc=1, device_id=at(other, me_z, q_of(step)), device_id_type=MESH)

    def chunk(c):
        return pl.ds(pl.multiple_of(c * rows, rows), rows)

    loads = [
        pltpu.make_async_copy(f_hbm.at[pl.ds(c * rows, rows)], f_ref.at[pl.ds(c * rows, rows)], load_s.at[c])
        for c in range(CHUNKS)
    ]
    small_loads = [
        pltpu.make_async_copy(src, dst, load_s.at[CHUNKS + i])
        for i, (src, dst) in enumerate([(send_hbm, send_ref), (adj_hbm, adj_ref), (n_hbm, n_ref)])
    ]
    for copy in loads + small_loads:
        copy.start()

    lane_v = node_velocity(lax.broadcasted_iota(jnp.int32, (1, nodes), 1) + vel * nodes, z_count)
    lx, ly, lz = lane_v
    sq = lx * lx + ly * ly + lz * lz
    table = [
        jnp.ones_like(lx), lx, ly, lz, lx * lx, ly * ly, lz * lz,
        lx * ly, lx * lz, ly * lz, lx * sq, ly * sq, lz * sq,
    ]
    row_id = lax.broadcasted_iota(jnp.int32, (16, nodes), 0)
    phi = jnp.zeros((16, nodes), jnp.float32)
    for r, row in enumerate(table):
        phi = jnp.where(row_id == r, row, phi)
    rest = phi
    for i in range(3):
        leading = rest.astype(jnp.bfloat16)
        phi_parts[i * 16 : (i + 1) * 16, :] = leading
        rest = rest - leading.astype(jnp.float32)
    with jax.named_scope("W_bar"):
        pl.semaphore_wait(barrier, 2 * QUAD + ring - 2)

    def remote(src, dst, s, r, dev):
        return pltpu.make_async_remote_copy(
            src_ref=src, dst_ref=dst, send_sem=s, recv_sem=r, device_id=dev, device_id_type=MESH
        )

    pair = at(other, me_z, me_q)

    piece = nodes // PIECES

    plan, started = iter(ISSUE), []

    def more():
        first = len(started)
        last = min(PIECES, first + next(plan))
        for c in range(first, last):
            started.append(c)
            part = pl.ds(c * piece, piece)
            remote(f_hbm.at[part], fx.at[part], bulk_s, bulk_r.at[sum(c >= t for t in TAKEN) - 1], pair).start()

    metas = [
        remote(send_hbm, sendx, meta_s.at[0], meta_r.at[0], pair),
        remote(adj_hbm, adjx, meta_s.at[1], meta_r.at[1], pair),
        remote(n_hbm, nx, meta_s.at[2], meta_r.at[2], pair),
    ]
    for copy in metas:
        copy.start()
    more()

    def two_dot(part, state):
        high = state.astype(jnp.bfloat16)
        low = (state - high.astype(jnp.float32)).astype(jnp.bfloat16)
        lead = jnp.dot(phi_parts[:, part], high, preferred_element_type=jnp.float32)
        tail = jnp.dot(phi_parts[0:32, part], low, preferred_element_type=jnp.float32)
        return lead[0:16] + (lead[16:32] + tail[0:16]) + (lead[32:48] + tail[16:32])

    inv_total = 1.0 / total_vel
    partial = jnp.zeros((16, cells), jnp.float32)
    for c in range(CHUNKS):
        loads[c].wait()
        part = slice(c * rows, (c + 1) * rows)
        partial = partial + two_dot(part, f_ref[part, :])
    lay_rows(qb0.at[me_q], partial * inv_total)

    def in_quad(buffer, i):
        for t in range(1, QUAD):
            remote(buffer.at[me_q], buffer.at[me_q], stage_s.at[i], stage_r.at[i], at(group, me_z, q_of(t))).start()

    def along_z(buffer, i):
        for t in range(1, ring):
            remote(buffer.at[me_z], buffer.at[me_z], stage_s.at[i], stage_r.at[i], at(group, z_of(t), me_q)).start()

    def across(src, dst, i):
        remote(src, dst, stage_s.at[i], stage_r.at[i], pair).start()

    def arrived(dst, i):
        with jax.named_scope(f"W_stage{i}"):
            pltpu.make_async_copy(dst, dst, stage_r.at[i]).wait()

    def all_of(buffer, sem, count):
        part = buffer.at[pl.ds(0, count)]
        pltpu.make_async_copy(part, part, sem).wait()

    def collect(i, buffer, count):
        with jax.named_scope(f"W_stage{i}"):
            all_of(buffer, stage_r.at[i], count - 1)
        rows13 = []
        for r in range(13):
            row = buffer[0, r]
            for t in range(1, count):
                row = row + buffer[t, r]
            rows13.append(row)
        return rows13

    in_quad(qb0, 0)
    more()

    for copy in small_loads:
        copy.wait()
    mine, far = slice(0, cells), slice(cells, both)
    slot_id = lax.broadcasted_iota(jnp.int32, (cells, cells), 0)
    eye = (slot_id == lax.broadcasted_iota(jnp.int32, (cells, cells), 1)).astype(jnp.float32)
    vx_col = x_column(0, VXY, cells)

    def listed(send_row, adjacency):
        hit = jnp.where(slot_id == adjacency - cells, 1.0, 0.0).astype(jnp.bfloat16)
        values = jnp.broadcast_to(send_row, (8, cells)).astype(jnp.float32).astype(jnp.bfloat16)
        got = jnp.dot(values, hit, preferred_element_type=jnp.float32)
        return jnp.where(adjacency < cells, -1, got[0:1].astype(jnp.int32))

    def choose(k, source, target, index):
        hit = jnp.where(slot_id == index, 1.0, 0.0)
        oh[k, source, target] = (hit - eye if source == target else hit).astype(jnp.bfloat16)

    def lay_normals(ref, target):
        for d in range(3):
            lines = [ref[d, k : k + 1, :] for k in range(faces)]
            lines.append(sum(lines[1:], lines[0]))
            for k, line in enumerate(lines):
                if d == 0:
                    xn[k, :, target] = vx_col * line
                else:
                    ncat[d, k : k + 1, target] = line

    lay_normals(n_ref, mine)
    for k in range(faces):
        choose(k, mine, mine, adj_ref[k : k + 1, :])

    for b in range(VXY // 8):
        weights[b] = column_weights(b)
    lay_rows(zb0.at[me_z], collect(0, qb0, QUAD))
    along_z(zb0, 1)
    more()

    with jax.named_scope("W_meta"):
        for copy in metas:
            copy.wait_recv()
    to_me = sendx[0, pl.ds(group, 1), :]
    to_other = send_ref[0, pl.ds(other, 1), :]
    lay_normals(nx, far)
    for k in range(faces):
        choose(k, mine, far, listed(to_other, adjx[k : k + 1, :]))

    centre = (VXY - 1) / 2.0
    shift = VXY.bit_length() - 1

    def line_velocity(first):
        line = (vel * nodes + first) // VXY
        vy = ((line & (VXY - 1)).astype(jnp.float32) - centre) * spacing
        vz = ((line >> shift).astype(jnp.float32) - (z_count - 1) / 2.0) * spacing
        return vy, vz

    def halves(state):
        high = state.astype(jnp.bfloat16)
        low = (state - high.astype(jnp.float32)).astype(jnp.bfloat16)
        return jnp.concatenate([high, low], axis=0)

    def transport(lhs, source, target, leaving, first, count):
        speeds = [line_velocity(first + sub * VXY) for sub in range(count // VXY)]

        def speed(k, sub):
            vy, vz = speeds[sub]
            return xn[k, :, target] + (vy * ncat[1, k : k + 1, target] + vz * ncat[2, k : k + 1, target])

        def lines(sub, offset=0):
            return slice(offset + sub * VXY, offset + (sub + 1) * VXY)

        result = [
            None if leaving is None else leaving[lines(sub)] * speed(faces, sub) for sub in range(count // VXY)
        ]
        for k in range(faces):
            got = jnp.dot(lhs, oh[k, source, target], preferred_element_type=jnp.float32)
            for sub in range(count // VXY):
                value = got[lines(sub)]
                if lhs.shape[0] > count:
                    value = value + got[lines(sub, count)]
                term = jnp.minimum(speed(k, sub), 0.0) * value
                result[sub] = term if result[sub] is None else result[sub] + term
        return jnp.concatenate(result, axis=0)

    def equilibrium(quad, first, count):
        square = quad[0] * vx_col
        parts = []
        for sub in range(count // VXY):
            vy, vz = line_velocity(first + sub * VXY)
            slope = quad[3] * vy + quad[4] * vz + quad[6]
            level = vy * (quad[1] * vy + quad[5] * vz + quad[7]) + (vz * (quad[2] * vz + quad[8]) + quad[9])
            parts.append(jnp.exp2(vx_col * (square + slope) + level))
        return jnp.concatenate(parts, axis=0)

    blocks = [(c * (nodes // SLABS), nodes // SLABS) for c in range(SLABS)]
    sent = jnp.zeros((16, cells), jnp.float32)
    with jax.named_scope("T0p_far"):
        for first, count in blocks:
            part = slice(first, first + count)
            lhs = halves(f_ref[part, :])
            split[2 * first : 2 * (first + count), :] = lhs
            moved = transport(lhs[:count], mine, far, None, first, count)
            tr0[part, far] = moved
            sent = sent + two_dot(part, moved)
            more()
    lay_rows(lent0, sent * (-time_step * inv_total))
    across(lent0, got0, 7)
    more()
    with jax.named_scope("T0p_mine"):
        for first, count in blocks:
            part = slice(first, first + count)
            lhs = split[2 * first : 2 * (first + count), :]
            tr0[part, mine] = transport(lhs, mine, mine, f_ref[part, :], first, count)
            more()

    with jax.named_scope("oh2"):
        for k in range(faces):
            choose(k, far, mine, listed(to_me, adj_ref[k : k + 1, :]))
            theirs = adjx[k : k + 1, :]
            choose(k, far, far, theirs)

    more()
    fields0, own_quad, freq0 = coefficient_rows(collect(1, zb0, ring))
    more()
    with jax.named_scope("G_tot0"):
        norm0 = gauss_total(own_quad, cells, z_count) * inv_total
    own_gain = time_step * freq0 * fields0[0] / norm0
    own_keep = 1.0 - time_step * freq0
    for r, row in enumerate(own_quad + [own_gain, own_keep]):
        total_mine[r] = row
    across(total_mine, total_theirs, 2)
    more()

    with jax.named_scope("f1p"):
        for first, count in blocks:
            part = slice(first, first + count)
            state = (
                own_keep * f_ref[part, :] - time_step * tr0[part, mine] + own_gain * equilibrium(own_quad, first, count)
            )
            fnew[part, :] = state
            wide[part, mine] = state.astype(jnp.bfloat16)
            away = -time_step * tr0[part, far]
            tr0[part, far] = away
            wide[part, far] = away.astype(jnp.bfloat16)
        kept = two_dot(slice(0, nodes), fnew[...]) * inv_total
    arrived(got0, 7)
    lay_rows(qb1.at[me_q], kept, got0)
    in_quad(qb1, 3)

    def second_moments(target, leaving):
        part = slice(0, nodes)
        moved = transport(wide[part, :], slice(0, both), target, leaving(part), 0, nodes)
        return two_dot(part, moved) * inv_total

    with jax.named_scope("T1p_far"):
        lay_rows(lent1, second_moments(far, lambda part: tr0[part, far]))
    for t in range(QUAD):
        remote(lent1, got1.at[me_q], stage_s.at[8], stage_r.at[8], at(other, me_z, q_of(t))).start()
    more()
    with jax.named_scope("T1p_mine"):
        stay = second_moments(mine, lambda part: fnew[part, :])

    def received(i):
        first, last = TAKEN[i] * piece, TAKEN[i + 1] * piece
        count, part = last - first, slice(first, last)
        with jax.named_scope("W_bulk"):
            ref = fx.at[pl.ds(first, count)]
            pltpu.make_async_copy(ref, ref, bulk_r.at[i]).wait()
        their_quad = [total_theirs[r] for r in range(10)]
        their_gain, their_keep = total_theirs[10], total_theirs[11]
        state = fx[part, :]
        lhs = halves(state)
        here = fnew[part, :] - time_step * transport(lhs, far, mine, None, first, count)
        there = (
            their_keep * state
            + (tr0[part, far] - time_step * transport(lhs[:count], far, far, state, first, count))
            + their_gain * equilibrium(their_quad, first, count)
        )
        fnew[part, :] = here
        lhs = halves(jnp.concatenate([here, there], axis=1))
        tr1[part, :] = transport(lhs, slice(0, both), mine, here, first, count)

    lay_rows(qb2.at[me_q], stay)
    in_quad(qb2, 5)
    lay_rows(zb1.at[me_z], collect(3, qb1, QUAD))
    along_z(zb1, 4)
    arrived(total_theirs, 2)
    for i in range(PLACES[0]):
        received(i)
    arrived(got1, 8)
    from_far = [got1[0, r] + got1[1, r] + (got1[2, r] + got1[3, r]) for r in range(13)]
    lay_rows(zb2.at[me_z], collect(5, qb2, QUAD), from_far)
    along_z(zb2, 6)
    for i in range(PLACES[0], PLACES[1]):
        received(i)
    mom1 = collect(4, zb1, ring)
    fields1, quad1, freq1 = coefficient_rows(mom1)
    with jax.named_scope("G_mom1"):
        sums = gauss_moments(quad1, cells, z_count, weights)
    inv_sum = 1.0 / sums[0]
    lift = time_step * freq1 * fields1[0]
    gain1 = lift * inv_sum * float(total_vel)
    keep1 = 1.0 - time_step * freq1

    for i in range(PLACES[1], len(TAKEN) - 1):
        received(i)

    def finish(c, carry):
        part = chunk(c)
        out_ref[part, :] = (
            keep1 * fnew[part, :] - time_step * tr1[part, :] + gain1 * equilibrium(quad1, c * rows, rows)
        )
        return carry

    with jax.named_scope("fin"):
        lax.fori_loop(0, CHUNKS, finish, 0)
    mom_t = collect(6, zb2, ring)
    slope = lift * inv_sum
    last = [
        keep1 * mom1[r] - time_step * mom_t[r] + slope * sums[r] for r in range(13)
    ]
    final = macroscopic_rows(last)
    for r in range(13):
        fields_ref[r : r + 1, :] = final[r]
    with jax.named_scope("W_send"):
        pltpu.make_async_copy(fx, fx, bulk_s).wait()
        for copy in metas:
            copy.wait_send()
        for i, buffer in ((2, total_mine), (7, lent0), (8, got1)):
            pltpu.make_async_copy(buffer, buffer, stage_s.at[i]).wait()
        for i, buffer, count in (
            (0, qb0, QUAD), (1, zb0, ring), (3, qb1, QUAD), (4, zb1, ring), (5, qb2, QUAD), (6, zb2, ring),
        ):
            all_of(buffer, stage_s.at[i], count - 1)


def store_kernel(state_ref, fields_ref, state_out, fields_out, sems):
    copies = [
        pltpu.make_async_copy(fields_ref, fields_out, sems.at[0]),
        pltpu.make_async_copy(state_ref, state_out, sems.at[1]),
    ]
    for copy in copies:
        copy.start()
    for copy in copies:
        copy.wait()


def per_device_pair(distribution, normals, adjacency, send_list, block_counts):
    nodes, cells = distribution.shape
    normals = normals.transpose(1, 0, 2)
    size = lax.axis_size("vel")
    ring = size // QUAD
    faces = normals.shape[1]
    f32 = jnp.float32
    dma = pltpu.SemaphoreType.DMA
    vmem = pl.BlockSpec(memory_space=pltpu.VMEM)
    hbm = pl.BlockSpec(memory_space=pltpu.HBM)
    shapes = (
        jax.ShapeDtypeStruct((nodes, cells), f32),
        jax.ShapeDtypeStruct((13, cells), f32),
    )
    state, fields = pl.pallas_call(
        functools.partial(step_kernel, nodes * size),
        out_shape=shapes,
        in_specs=[hbm] * 4,
        out_specs=(vmem, vmem),
        scratch_shapes=[
            pltpu.VMEM((nodes, cells), f32),
            pltpu.VMEM(normals.shape, f32),
            pltpu.VMEM(adjacency.shape, jnp.int32),
            pltpu.VMEM(send_list.shape, jnp.int32),
            dma((CHUNKS + 3,)),
            pltpu.VMEM((nodes, cells), f32),
            pltpu.VMEM(normals.shape, f32),
            pltpu.VMEM(adjacency.shape, jnp.int32),
            pltpu.VMEM(send_list.shape, jnp.int32),
            pltpu.VMEM((3, 8, 2 * cells), f32),
            pltpu.VMEM((faces + 1, VXY, 2 * cells), f32),
            pltpu.VMEM((faces, 2 * cells, 2 * cells), jnp.bfloat16),
            pltpu.VMEM((nodes, 2 * cells), f32),
            pltpu.VMEM((2 * nodes, cells), jnp.bfloat16),
            pltpu.VMEM((nodes, 2 * cells), jnp.bfloat16),
            pltpu.VMEM((nodes, cells), f32),
            pltpu.VMEM((nodes, cells), f32),
            pltpu.VMEM((48, nodes), jnp.bfloat16),
            pltpu.VMEM((VXY // 8, 16, 8 * VXY), jnp.bfloat16),
            pltpu.VMEM((QUAD, 13, 1, cells), f32),
            pltpu.VMEM((ring, 13, 1, cells), f32),
            pltpu.VMEM((12, 1, cells), f32),
            pltpu.VMEM((12, 1, cells), f32),
            pltpu.VMEM((QUAD, 13, 1, cells), f32),
            pltpu.VMEM((ring, 13, 1, cells), f32),
            pltpu.VMEM((QUAD, 13, 1, cells), f32),
            pltpu.VMEM((ring, 13, 1, cells), f32),
            pltpu.VMEM((13, 1, cells), f32),
            pltpu.VMEM((13, 1, cells), f32),
            pltpu.VMEM((13, 1, cells), f32),
            pltpu.VMEM((QUAD, 13, 1, cells), f32),
            dma, dma((len(TAKEN) - 1,)), dma((3,)), dma((3,)), dma((9,)), dma((9,)),
        ],
        compiler_params=pltpu.CompilerParams(
            collective_id=0, has_side_effects=True, vmem_limit_bytes=16 * 1024 * 1024
        ),
        name="steps",
    )(*[pltpu.with_memory_space_constraint(x, pltpu.HBM) for x in (distribution, normals, adjacency, send_list)])
    anywhere = pl.BlockSpec(memory_space=pl.ANY)
    return pl.pallas_call(
        store_kernel,
        out_shape=shapes,
        in_specs=[anywhere, anywhere],
        out_specs=(hbm, hbm),
        scratch_shapes=[dma((2,))],
        compiler_params=pltpu.CompilerParams(vmem_limit_bytes=16 * 1024 * 1024),
        name="store",
    )(state, fields)


def solution(mesh):
    placed = (
        P("vel", "space"),
        P(None, None, "space"),
        P(None, "space"),
        P("space", None, None),
        P(None, "space"),
    )
    pair = mesh.shape["space"] == 2 and mesh.shape["vel"] % QUAD == 0 and ITERS == 2
    return jax.shard_map(
        per_device_pair if pair else per_device,
        mesh=mesh,
        in_specs=placed,
        out_specs=(P("vel", "space"), P(None, "space")),
        check_vma=False,
    )
```

```python
import functools

import jax
import jax.numpy as jnp
from jax import lax
from jax.experimental import pallas as pl
from jax.experimental.pallas import tpu as pltpu
from jax.sharding import PartitionSpec as P

VXY = 32
TILE = 128
ITERS = 2


spacing = 0.3
ellipsoid_mix = -0.25
prandtl = 0.8
visc_power = 0.26
time_step = 0.025


def velocity_nodes(vel_index, z_count):
    comp_x = (vel_index % VXY).astype(jnp.float32)
    comp_y = (vel_index // VXY % VXY).astype(jnp.float32)
    comp_z = (vel_index // (VXY * VXY)).astype(jnp.float32)
    centre = (VXY - 1) / 2.0
    return jnp.stack(
        [
            (comp_x - centre) * spacing,
            (comp_y - centre) * spacing,
            (comp_z - (z_count - 1) / 2.0) * spacing,
        ]
    )


def moment_rows(velocity):
    comp_x, comp_y, comp_z = (velocity[0], velocity[1], velocity[2])
    squared = comp_x * comp_x + comp_y * comp_y + comp_z * comp_z
    return jnp.stack(
        [
            jnp.ones_like(comp_x),
            comp_x,
            comp_y,
            comp_z,
            comp_x * comp_x,
            comp_y * comp_y,
            comp_z * comp_z,
            comp_x * comp_y,
            comp_x * comp_z,
            comp_y * comp_z,
            comp_x * squared,
            comp_y * squared,
            comp_z * squared,
        ]
    )


def quad_rows(velocity):
    comp_x, comp_y, comp_z = (velocity[0], velocity[1], velocity[2])
    return jnp.stack(
        [
            comp_x * comp_x,
            comp_y * comp_y,
            comp_z * comp_z,
            comp_x * comp_y,
            comp_x * comp_z,
            comp_y * comp_z,
            comp_x,
            comp_y,
            comp_z,
            jnp.ones_like(comp_x),
        ]
    )


def macroscopic(moments):
    density = moments[0]
    mean_x = moments[1] / density
    mean_y = moments[2] / density
    mean_z = moments[3] / density
    second = moments[4:10] / density[None, :]
    third = moments[10:13] / density[None, :]
    theta_xx = second[0] - mean_x * mean_x
    theta_yy = second[1] - mean_y * mean_y
    theta_zz = second[2] - mean_z * mean_z
    theta_xy = second[3] - mean_x * mean_y
    theta_xz = second[4] - mean_x * mean_z
    theta_yz = second[5] - mean_y * mean_z
    temper = (theta_xx + theta_yy + theta_zz) / 3.0
    trace_b = second[0] + second[1] + second[2]
    bu_x = second[0] * mean_x + second[3] * mean_y + second[4] * mean_z
    bu_y = second[3] * mean_x + second[1] * mean_y + second[5] * mean_z
    bu_z = second[4] * mean_x + second[5] * mean_y + second[2] * mean_z
    mean_sq = mean_x * mean_x + mean_y * mean_y + mean_z * mean_z
    flux_x = 0.5 * (third[0] - 2.0 * bu_x - mean_x * trace_b + 2.0 * mean_x * mean_sq)
    flux_y = 0.5 * (third[1] - 2.0 * bu_y - mean_y * trace_b + 2.0 * mean_y * mean_sq)
    flux_z = 0.5 * (third[2] - 2.0 * bu_z - mean_z * trace_b + 2.0 * mean_z * mean_sq)
    iso_part = (1.0 - ellipsoid_mix) * temper
    lam_xx = iso_part + ellipsoid_mix * theta_xx
    lam_yy = iso_part + ellipsoid_mix * theta_yy
    lam_zz = iso_part + ellipsoid_mix * theta_zz
    lam_xy = ellipsoid_mix * theta_xy
    lam_xz = ellipsoid_mix * theta_xz
    lam_yz = ellipsoid_mix * theta_yz
    cof_xx = lam_yy * lam_zz - lam_yz * lam_yz
    cof_xy = lam_yz * lam_xz - lam_xy * lam_zz
    cof_xz = lam_xy * lam_yz - lam_yy * lam_xz
    cof_yy = lam_xx * lam_zz - lam_xz * lam_xz
    cof_yz = lam_xy * lam_xz - lam_xx * lam_yz
    cof_zz = lam_xx * lam_yy - lam_xy * lam_xy
    determinant = lam_xx * cof_xx + lam_xy * cof_xy + lam_xz * cof_xz
    inv_xx = cof_xx / determinant
    inv_yy = cof_yy / determinant
    inv_zz = cof_zz / determinant
    inv_xy = cof_xy / determinant
    inv_xz = cof_xz / determinant
    inv_yz = cof_yz / determinant
    lin_x = inv_xx * mean_x + inv_xy * mean_y + inv_xz * mean_z
    lin_y = inv_xy * mean_x + inv_yy * mean_y + inv_yz * mean_z
    lin_z = inv_xz * mean_x + inv_yz * mean_y + inv_zz * mean_z
    offset = mean_x * lin_x + mean_y * lin_y + mean_z * lin_z
    collide = prandtl * density * jnp.exp(visc_power * jnp.log(temper))
    return jnp.stack(
        [
            density,
            mean_x,
            mean_y,
            mean_z,
            theta_xx,
            theta_yy,
            theta_zz,
            theta_xy,
            theta_xz,
            theta_yz,
            flux_x,
            flux_y,
            flux_z,
            inv_xx,
            inv_yy,
            inv_zz,
            2.0 * inv_xy,
            2.0 * inv_xz,
            2.0 * inv_yz,
            -2.0 * lin_x,
            -2.0 * lin_y,
            -2.0 * lin_z,
            offset,
            collide,
        ]
    )


def ghost_slots(adjacency, counts, cells, groups, slot_count):
    ends = jnp.cumsum(counts) * TILE
    starts = ends - counts * TILE
    is_local = adjacency < cells
    position = jnp.maximum(adjacency - cells, 0)
    source = jnp.sum((ends[:, None, None] <= position[None]).astype(jnp.int32), axis=0)
    source = jnp.minimum(source, groups - 1)
    group_ids = jnp.arange(groups, dtype=jnp.int32)[:, None, None]
    chosen = jnp.sum(jnp.where(group_ids == source[None], starts[:, None, None], 0), axis=0)
    slot_pos = jnp.clip(position - chosen, 0, slot_count - 1)
    return (is_local, source, slot_pos)


def relax(current, neighbours, velocity, normals, params, norm_z, equilibrium):
    gauss = params[0][None, :] * equilibrium / norm_z[None, :]
    outflow = jnp.zeros(current.shape, jnp.float32)
    inflow = jnp.zeros(current.shape, jnp.float32)
    for side in range(normals.shape[0]):
        normal_speed = (
            velocity[0][:, None] * normals[side, 0][None, :]
            + velocity[1][:, None] * normals[side, 1][None, :]
            + velocity[2][:, None] * normals[side, 2][None, :]
        )
        outflow = outflow + jnp.maximum(normal_speed, 0.0)
        inflow = inflow + jnp.minimum(normal_speed, 0.0) * neighbours[side]
    return current + time_step * (
        params[23][None, :] * (gauss - current) - outflow * current - inflow
    )


def per_device(distribution, normals, adjacency, send_list, block_counts):
    vel_local = distribution.shape[0]
    cells = distribution.shape[1]
    total_vel = vel_local * lax.axis_size("vel")
    z_count = total_vel // (VXY * VXY)
    groups = send_list.shape[1]
    slot_count = send_list.shape[2]
    vel_index = lax.axis_index("vel") * vel_local + jnp.arange(vel_local, dtype=jnp.int32)
    velocity = velocity_nodes(vel_index, z_count)
    moment_table = moment_rows(velocity)
    quad_table = quad_rows(velocity).T
    is_local, source, slot_pos = ghost_slots(
        adjacency, block_counts[:, 0], cells, groups, slot_count
    )
    ghost_index = source * slot_count + slot_pos
    local_index = jnp.where(is_local, adjacency, 0)
    send_rows = send_list[0].reshape(-1)

    def reduce_moments(current):
        partial_value = (
            jnp.dot(
                moment_table,
                current,
                precision=lax.Precision.HIGHEST,
                preferred_element_type=jnp.float32,
            )
            / total_vel
        )
        return macroscopic(lax.psum(partial_value, "vel"))

    current = distribution
    for iteration in range(ITERS):
        params = reduce_moments(current)
        ghosts = lax.all_to_all(
            jnp.take(current, send_rows, axis=1), "space", split_axis=1, concat_axis=1, tiled=True
        )
        exponent = jnp.dot(
            quad_table,
            params[13:23],
            precision=lax.Precision.HIGHEST,
            preferred_element_type=jnp.float32,
        )
        equilibrium = jnp.exp(-0.5 * exponent)
        norm_z = lax.psum(jnp.sum(equilibrium, axis=0) / total_vel, "vel")
        neighbours = [
            jnp.where(
                is_local[side][None, :],
                jnp.take(current, local_index[side], axis=1),
                jnp.take(ghosts, ghost_index[side], axis=1),
            )
            for side in range(normals.shape[0])
        ]
        current = relax(current, neighbours, velocity, normals, params, norm_z, equilibrium)
    final = reduce_moments(current)
    return (current, final[:13])


MESH = pl.DeviceIdType.MESH
LOG2E = 1.4426950408889634
QUAD = 4
CHUNKS = 4
PIECES = 16
ISSUE = (1, 4, 1, 0, 0, 1, 1, 1, 1, 1, 1, 16)
TAKEN = (0, 8, 12, 16)
PLACES = (2, 2)
SLABS = 2
HI = lax.Precision.HIGHEST


def coefficient_rows(m):
    full = macroscopic_rows(m)
    scale = -0.5 * LOG2E
    return full[:13], [row * scale for row in full[13:23]], full[23]


def macroscopic_rows(m):
    density = m[0]
    inv_d = 1.0 / density
    ux, uy, uz = (m[1] * inv_d, m[2] * inv_d, m[3] * inv_d)
    b = [m[r] * inv_d for r in range(4, 10)]
    third = [m[r] * inv_d for r in range(10, 13)]
    txx, tyy, tzz = (b[0] - ux * ux, b[1] - uy * uy, b[2] - uz * uz)
    txy, txz, tyz = (b[3] - ux * uy, b[4] - ux * uz, b[5] - uy * uz)
    temper = (txx + tyy + tzz) * (1.0 / 3.0)
    trace_b = b[0] + b[1] + b[2]
    bux = b[0] * ux + b[3] * uy + b[4] * uz
    buy = b[3] * ux + b[1] * uy + b[5] * uz
    buz = b[4] * ux + b[5] * uy + b[2] * uz
    usq = ux * ux + uy * uy + uz * uz
    qx = 0.5 * (third[0] - 2.0 * bux - ux * trace_b + 2.0 * ux * usq)
    qy = 0.5 * (third[1] - 2.0 * buy - uy * trace_b + 2.0 * uy * usq)
    qz = 0.5 * (third[2] - 2.0 * buz - uz * trace_b + 2.0 * uz * usq)
    iso = (1.0 - ellipsoid_mix) * temper
    lxx, lyy, lzz = (iso + ellipsoid_mix * txx, iso + ellipsoid_mix * tyy, iso + ellipsoid_mix * tzz)
    lxy, lxz, lyz = (ellipsoid_mix * txy, ellipsoid_mix * txz, ellipsoid_mix * tyz)
    cxx = lyy * lzz - lyz * lyz
    cxy = lyz * lxz - lxy * lzz
    cxz = lxy * lyz - lyy * lxz
    cyy = lxx * lzz - lxz * lxz
    cyz = lxy * lxz - lxx * lyz
    czz = lxx * lyy - lxy * lxy
    inv_det = 1.0 / (lxx * cxx + lxy * cxy + lxz * cxz)
    ixx, iyy, izz = (cxx * inv_det, cyy * inv_det, czz * inv_det)
    ixy, ixz, iyz = (cxy * inv_det, cxz * inv_det, cyz * inv_det)
    wx = ixx * ux + ixy * uy + ixz * uz
    wy = ixy * ux + iyy * uy + iyz * uz
    wz = ixz * ux + iyz * uy + izz * uz
    offset = ux * wx + uy * wy + uz * wz
    collide = prandtl * density * jnp.exp(visc_power * jnp.log(temper))
    return [
        density, ux, uy, uz, txx, tyy, tzz, txy, txz, tyz, qx, qy, qz,
        ixx, iyy, izz, 2.0 * ixy, 2.0 * ixz, 2.0 * iyz,
        -2.0 * wx, -2.0 * wy, -2.0 * wz, offset, collide,
    ]


def node_velocity(index, z_count):
    shift = VXY.bit_length() - 1
    centre = (VXY - 1) / 2.0
    vx = ((index & (VXY - 1)).astype(jnp.float32) - centre) * spacing
    vy = (((index >> shift) & (VXY - 1)).astype(jnp.float32) - centre) * spacing
    vz = ((index >> (2 * shift)).astype(jnp.float32) - (z_count - 1) / 2.0) * spacing
    return vx, vy, vz


def x_column(first, rows, width):
    index = lax.broadcasted_iota(jnp.int32, (rows, width), 0) + first
    return (index.astype(jnp.float32) - (VXY - 1) / 2.0) * spacing


def pair_polynomials(half):
    def grow(before, now):
        rows = [now]
        for _ in range(half - 1):
            shifted = [0.0] + rows[-1]
            twice = [2.0 * v for v in rows[-1]] + [0.0]
            older = before + [0.0] * (len(shifted) - len(before))
            before = rows[-1]
            rows.append([x + y - z for x, y, z in zip(shifted, twice, older)])
        return rows

    return grow([1.0], [1.0]), grow([-1.0], [1.0])


def level_coefficients(q, z_count, powers):
    half = z_count // 2
    even, odd = pair_polynomials(half)
    weights = [jnp.exp2(q[2] * ((k + 0.5) * spacing) ** 2) for k in range(half)]
    result = []
    for c in range(powers):
        table = odd if c % 2 else even
        row = []
        for j in range(half):
            total = None
            for k in range(j, half):
                term = weights[k] * (table[k][j] * ((k + 0.5) * spacing) ** c)
                total = term if total is None else total + term
            row.append(total)
        result.append(row)
    return result


def horner(row, x):
    value = row[-1]
    for c in row[-2::-1]:
        value = value * x + c
    return value


def gauss_columns(q, width, block):
    step = 0.5 * spacing
    vx = x_column(block * 8, 8, width)
    base = (q[0] * vx + q[6]) * vx + q[9]
    lean = q[3] * vx + q[7]
    rise = (q[4] * vx + q[8]) * step
    for j in range(VXY // 2):
        vy = (j + 0.5) * spacing
        mid = base + q[1] * (vy * vy)
        tilt = lean * vy
        side = q[5] * (vy * step)
        columns = []
        for sign in (1.0, -1.0):
            flat = jnp.exp2(mid + tilt if sign > 0 else mid - tilt)
            slope = rise + side if sign > 0 else rise - side
            up, down = jnp.exp2(slope), jnp.exp2(-slope)
            diff = up - down
            columns.append((flat * (up + down), flat * diff, diff * diff))
        yield vx, vy, columns


def gauss_total(q, width, z_count):
    (even,) = level_coefficients(q, z_count, 1)

    def block(b, acc):
        for _, _, columns in gauss_columns(q, width, b):
            for plus, _, delta in columns:
                acc = acc + plus * horner(even, delta)
        return acc

    acc = jnp.zeros((8, width), jnp.float32)
    for b in range(VXY // 8):
        acc = block(b, acc)
    return jnp.sum(acc, axis=0, keepdims=True)


def column_weights(block):
    k = lax.broadcasted_iota(jnp.int32, (1, 8 * VXY), 1)
    x = ((k & 7) + block * 8).astype(jnp.float32) - (VXY - 1) / 2.0
    y = (k >> 4).astype(jnp.float32) + 0.5
    y = jnp.where((k & 8) == 0, y, -y)
    square = x * x + y * y
    rows = [jnp.ones_like(x), x, y, x * x, y * y, x * y, x * square, y * square]
    row_id = lax.broadcasted_iota(jnp.int32, (8, 8 * VXY), 0)
    table = jnp.zeros((8, 8 * VXY), jnp.float32)
    for r, row in enumerate(rows):
        table = jnp.where(row_id == r, row, table)
    high = table.astype(jnp.bfloat16).astype(jnp.float32)
    return jnp.concatenate([high, table - high], axis=0).astype(jnp.bfloat16)


def gauss_moments(q, width, z_count, weights_ref):
    levels = level_coefficients(q, z_count, 4)
    half = z_count // 2
    zero = jnp.zeros((16, width), jnp.float32)

    def block(b, carry):
        tiles = [[] for _ in range(2 * half + 1)]
        for _, _, ((p_up, d_up, x_up), (p_down, d_down, x_down)) in gauss_columns(q, width, b):
            plus = jnp.concatenate([p_up, p_down], axis=0)
            diff = jnp.concatenate([d_up, d_down], axis=0)
            delta = jnp.concatenate([x_up, x_down], axis=0)
            for j in range(half):
                lead = plus.astype(jnp.bfloat16)
                tiles[j].append(lead)
                tiles[half + j].append(diff.astype(jnp.bfloat16))
                if j == 0:
                    tiles[2 * half].append((plus - lead.astype(jnp.float32)).astype(jnp.bfloat16))
                if j < half - 1:
                    plus, diff = plus * delta, diff * delta
        weights = weights_ref[b]
        sums = [
            jnp.dot(weights, jnp.concatenate(t, axis=0), preferred_element_type=jnp.float32) for t in tiles
        ]
        sums[0] = sums[0] + sums.pop()
        return tuple(x + y for x, y in zip(carry, sums))

    sums = (zero,) * (2 * half)
    for b in range(VXY // 8):
        sums = block(b, sums)
    sums = [t[:8] + t[8:] for t in sums]
    m0, m1, m2, m3 = [
        sum(levels[c][j] * sums[(c % 2) * half + j] for j in range(half)) for c in range(4)
    ]
    h = spacing
    row = lambda m, r: m[r : r + 1]
    return [
        row(m0, 0), h * row(m0, 1), h * row(m0, 2), row(m1, 0),
        h * h * row(m0, 3), h * h * row(m0, 4), row(m2, 0),
        h * h * row(m0, 5), h * row(m1, 1), h * row(m1, 2),
        h * (h * h * row(m0, 6) + row(m2, 1)), h * (h * h * row(m0, 7) + row(m2, 2)),
        h * h * (row(m1, 3) + row(m1, 4)) + row(m3, 0),
    ]


def step_kernel(
    total_vel,
    f_hbm, n_hbm, adj_hbm, send_hbm,
    out_ref, fields_ref,
    f_ref, n_ref, adj_ref, send_ref, load_s,
    fx, nx, adjx, sendx, ncat, xn, oh, tr0, split, wide, fnew, tr1, phi_parts, weights,
    qb0, zb0, total_mine, total_theirs, qb1, zb1, qb2, zb2, lent0, got0, lent1, got1,
    bulk_s, bulk_r, meta_s, meta_r, stage_s, stage_r,
):
    nodes, cells = f_hbm.shape
    both = 2 * cells
    faces = n_hbm.shape[1]
    z_count = total_vel // (VXY * VXY)
    rows = nodes // CHUNKS
    group = lax.axis_index("space")
    other = 1 - group
    vel = lax.axis_index("vel")
    ring = total_vel // nodes // QUAD
    me_q = lax.rem(vel, QUAD)
    me_z = vel // QUAD

    def at(space, z, q):
        return (space, z * QUAD + q)

    def q_of(step):
        return lax.rem(me_q + step, QUAD)

    def z_of(step):
        return lax.rem(me_z + step, ring)

    def lay_rows(ref, moments, extra=None):
        for r in range(13):
            row = moments[r] if isinstance(moments, list) else moments[r : r + 1]
            ref[r] = row if extra is None else row + extra[r]

    barrier = pltpu.get_barrier_semaphore()
    for step in range(1, ring):
        pl.semaphore_signal(barrier, inc=1, device_id=at(group, z_of(step), me_q), device_id_type=MESH)
    for step in range(1, QUAD):
        pl.semaphore_signal(barrier, inc=1, device_id=at(group, me_z, q_of(step)), device_id_type=MESH)
    for step in range(QUAD):
        pl.semaphore_signal(barrier, inc=1, device_id=at(other, me_z, q_of(step)), device_id_type=MESH)

    def chunk(c):
        return pl.ds(pl.multiple_of(c * rows, rows), rows)

    loads = [
        pltpu.make_async_copy(f_hbm.at[pl.ds(c * rows, rows)], f_ref.at[pl.ds(c * rows, rows)], load_s.at[c])
        for c in range(CHUNKS)
    ]
    small_loads = [
        pltpu.make_async_copy(src, dst, load_s.at[CHUNKS + i])
        for i, (src, dst) in enumerate([(send_hbm, send_ref), (adj_hbm, adj_ref), (n_hbm, n_ref)])
    ]
    for copy in loads + small_loads:
        copy.start()

    lane_v = node_velocity(lax.broadcasted_iota(jnp.int32, (1, nodes), 1) + vel * nodes, z_count)
    lx, ly, lz = lane_v
    sq = lx * lx + ly * ly + lz * lz
    table = [
        jnp.ones_like(lx), lx, ly, lz, lx * lx, ly * ly, lz * lz,
        lx * ly, lx * lz, ly * lz, lx * sq, ly * sq, lz * sq,
    ]
    row_id = lax.broadcasted_iota(jnp.int32, (16, nodes), 0)
    phi = jnp.zeros((16, nodes), jnp.float32)
    for r, row in enumerate(table):
        phi = jnp.where(row_id == r, row, phi)
    rest = phi
    for i in range(3):
        leading = rest.astype(jnp.bfloat16)
        phi_parts[i * 16 : (i + 1) * 16, :] = leading
        rest = rest - leading.astype(jnp.float32)
    with jax.named_scope("W_bar"):
        pl.semaphore_wait(barrier, 2 * QUAD + ring - 2)

    def remote(src, dst, s, r, dev):
        return pltpu.make_async_remote_copy(
            src_ref=src, dst_ref=dst, send_sem=s, recv_sem=r, device_id=dev, device_id_type=MESH
        )

    pair = at(other, me_z, me_q)

    piece = nodes // PIECES

    plan, started = iter(ISSUE), []

    def more():
        first = len(started)
        last = min(PIECES, first + next(plan))
        for c in range(first, last):
            started.append(c)
            part = pl.ds(c * piece, piece)
            remote(f_hbm.at[part], fx.at[part], bulk_s, bulk_r.at[sum(c >= t for t in TAKEN) - 1], pair).start()

    metas = [
        remote(send_hbm, sendx, meta_s.at[0], meta_r.at[0], pair),
        remote(adj_hbm, adjx, meta_s.at[1], meta_r.at[1], pair),
        remote(n_hbm, nx, meta_s.at[2], meta_r.at[2], pair),
    ]
    for copy in metas:
        copy.start()
    more()

    def two_dot(part, state):
        high = state.astype(jnp.bfloat16)
        low = (state - high.astype(jnp.float32)).astype(jnp.bfloat16)
        lead = jnp.dot(phi_parts[:, part], high, preferred_element_type=jnp.float32)
        tail = jnp.dot(phi_parts[0:32, part], low, preferred_element_type=jnp.float32)
        return lead[0:16] + (lead[16:32] + tail[0:16]) + (lead[32:48] + tail[16:32])

    inv_total = 1.0 / total_vel
    partial = jnp.zeros((16, cells), jnp.float32)
    for c in range(CHUNKS):
        loads[c].wait()
        part = slice(c * rows, (c + 1) * rows)
        partial = partial + two_dot(part, f_ref[part, :])
    lay_rows(qb0.at[me_q], partial * inv_total)

    def in_quad(buffer, i):
        for t in range(1, QUAD):
            remote(buffer.at[me_q], buffer.at[me_q], stage_s.at[i], stage_r.at[i], at(group, me_z, q_of(t))).start()

    def along_z(buffer, i):
        for t in range(1, ring):
            remote(buffer.at[me_z], buffer.at[me_z], stage_s.at[i], stage_r.at[i], at(group, z_of(t), me_q)).start()

    def across(src, dst, i):
        remote(src, dst, stage_s.at[i], stage_r.at[i], pair).start()

    def arrived(dst, i):
        with jax.named_scope(f"W_stage{i}"):
            pltpu.make_async_copy(dst, dst, stage_r.at[i]).wait()

    def all_of(buffer, sem, count):
        part = buffer.at[pl.ds(0, count)]
        pltpu.make_async_copy(part, part, sem).wait()

    def collect(i, buffer, count):
        with jax.named_scope(f"W_stage{i}"):
            all_of(buffer, stage_r.at[i], count - 1)
        rows13 = []
        for r in range(13):
            row = buffer[0, r]
            for t in range(1, count):
                row = row + buffer[t, r]
            rows13.append(row)
        return rows13

    in_quad(qb0, 0)
    more()

    for copy in small_loads:
        copy.wait()
    mine, far = slice(0, cells), slice(cells, both)
    slot_id = lax.broadcasted_iota(jnp.int32, (cells, cells), 0)
    eye = (slot_id == lax.broadcasted_iota(jnp.int32, (cells, cells), 1)).astype(jnp.float32)
    vx_col = x_column(0, VXY, cells)

    def listed(send_row, adjacency):
        hit = jnp.where(slot_id == adjacency - cells, 1.0, 0.0).astype(jnp.bfloat16)
        values = jnp.broadcast_to(send_row, (8, cells)).astype(jnp.float32).astype(jnp.bfloat16)
        got = jnp.dot(values, hit, preferred_element_type=jnp.float32)
        return jnp.where(adjacency < cells, -1, got[0:1].astype(jnp.int32))

    def choose(k, source, target, index):
        hit = jnp.where(slot_id == index, 1.0, 0.0)
        oh[k, source, target] = (hit - eye if source == target else hit).astype(jnp.bfloat16)

    def lay_normals(ref, target):
        for d in range(3):
            lines = [ref[d, k : k + 1, :] for k in range(faces)]
            lines.append(sum(lines[1:], lines[0]))
            for k, line in enumerate(lines):
                if d == 0:
                    xn[k, :, target] = vx_col * line
                else:
                    ncat[d, k : k + 1, target] = line

    lay_normals(n_ref, mine)
    for k in range(faces):
        choose(k, mine, mine, adj_ref[k : k + 1, :])

    for b in range(VXY // 8):
        weights[b] = column_weights(b)
    lay_rows(zb0.at[me_z], collect(0, qb0, QUAD))
    along_z(zb0, 1)
    more()

    with jax.named_scope("W_meta"):
        for copy in metas:
            copy.wait_recv()
    to_me = sendx[0, pl.ds(group, 1), :]
    to_other = send_ref[0, pl.ds(other, 1), :]
    lay_normals(nx, far)
    for k in range(faces):
        choose(k, mine, far, listed(to_other, adjx[k : k + 1, :]))

    centre = (VXY - 1) / 2.0
    shift = VXY.bit_length() - 1

    def line_velocity(first):
        line = (vel * nodes + first) // VXY
        vy = ((line & (VXY - 1)).astype(jnp.float32) - centre) * spacing
        vz = ((line >> shift).astype(jnp.float32) - (z_count - 1) / 2.0) * spacing
        return vy, vz

    def halves(state):
        high = state.astype(jnp.bfloat16)
        low = (state - high.astype(jnp.float32)).astype(jnp.bfloat16)
        return jnp.concatenate([high, low], axis=0)

    def transport(lhs, source, target, leaving, first, count):
        speeds = [line_velocity(first + sub * VXY) for sub in range(count // VXY)]

        def speed(k, sub):
            vy, vz = speeds[sub]
            return xn[k, :, target] + (vy * ncat[1, k : k + 1, target] + vz * ncat[2, k : k + 1, target])

        def lines(sub, offset=0):
            return slice(offset + sub * VXY, offset + (sub + 1) * VXY)

        result = [
            None if leaving is None else leaving[lines(sub)] * speed(faces, sub) for sub in range(count // VXY)
        ]
        for k in range(faces):
            got = jnp.dot(lhs, oh[k, source, target], preferred_element_type=jnp.float32)
            for sub in range(count // VXY):
                value = got[lines(sub)]
                if lhs.shape[0] > count:
                    value = value + got[lines(sub, count)]
                term = jnp.minimum(speed(k, sub), 0.0) * value
                result[sub] = term if result[sub] is None else result[sub] + term
        return jnp.concatenate(result, axis=0)

    def equilibrium(quad, first, count):
        square = quad[0] * vx_col
        parts = []
        for sub in range(count // VXY):
            vy, vz = line_velocity(first + sub * VXY)
            slope = quad[3] * vy + quad[4] * vz + quad[6]
            level = vy * (quad[1] * vy + quad[5] * vz + quad[7]) + (vz * (quad[2] * vz + quad[8]) + quad[9])
            parts.append(jnp.exp2(vx_col * (square + slope) + level))
        return jnp.concatenate(parts, axis=0)

    blocks = [(c * (nodes // SLABS), nodes // SLABS) for c in range(SLABS)]
    sent = jnp.zeros((16, cells), jnp.float32)
    with jax.named_scope("T0p_far"):
        for first, count in blocks:
            part = slice(first, first + count)
            lhs = halves(f_ref[part, :])
            split[2 * first : 2 * (first + count), :] = lhs
            moved = transport(lhs[:count], mine, far, None, first, count)
            tr0[part, far] = moved
            sent = sent + two_dot(part, moved)
            more()
    lay_rows(lent0, sent * (-time_step * inv_total))
    across(lent0, got0, 7)
    more()
    with jax.named_scope("T0p_mine"):
        for first, count in blocks:
            part = slice(first, first + count)
            lhs = split[2 * first : 2 * (first + count), :]
            tr0[part, mine] = transport(lhs, mine, mine, f_ref[part, :], first, count)
            more()

    with jax.named_scope("oh2"):
        for k in range(faces):
            choose(k, far, mine, listed(to_me, adj_ref[k : k + 1, :]))
            theirs = adjx[k : k + 1, :]
            choose(k, far, far, theirs)

    more()
    fields0, own_quad, freq0 = coefficient_rows(collect(1, zb0, ring))
    more()
    with jax.named_scope("G_tot0"):
        norm0 = gauss_total(own_quad, cells, z_count) * inv_total
    own_gain = time_step * freq0 * fields0[0] / norm0
    own_keep = 1.0 - time_step * freq0
    for r, row in enumerate(own_quad + [own_gain, own_keep]):
        total_mine[r] = row
    across(total_mine, total_theirs, 2)
    more()

    with jax.named_scope("f1p"):
        for first, count in blocks:
            part = slice(first, first + count)
            state = (
                own_keep * f_ref[part, :] - time_step * tr0[part, mine] + own_gain * equilibrium(own_quad, first, count)
            )
            fnew[part, :] = state
            wide[part, mine] = state.astype(jnp.bfloat16)
            away = -time_step * tr0[part, far]
            tr0[part, far] = away
            wide[part, far] = away.astype(jnp.bfloat16)
        kept = two_dot(slice(0, nodes), fnew[...]) * inv_total
    arrived(got0, 7)
    lay_rows(qb1.at[me_q], kept, got0)
    in_quad(qb1, 3)

    def second_moments(target, leaving):
        part = slice(0, nodes)
        moved = transport(wide[part, :], slice(0, both), target, leaving(part), 0, nodes)
        return two_dot(part, moved) * inv_total

    with jax.named_scope("T1p_far"):
        lay_rows(lent1, second_moments(far, lambda part: tr0[part, far]))
    for t in range(QUAD):
        remote(lent1, got1.at[me_q], stage_s.at[8], stage_r.at[8], at(other, me_z, q_of(t))).start()
    more()
    with jax.named_scope("T1p_mine"):
        stay = second_moments(mine, lambda part: fnew[part, :])

    def received(i):
        first, last = TAKEN[i] * piece, TAKEN[i + 1] * piece
        count, part = last - first, slice(first, last)
        with jax.named_scope("W_bulk"):
            ref = fx.at[pl.ds(first, count)]
            pltpu.make_async_copy(ref, ref, bulk_r.at[i]).wait()
        their_quad = [total_theirs[r] for r in range(10)]
        their_gain, their_keep = total_theirs[10], total_theirs[11]
        state = fx[part, :]
        lhs = halves(state)
        here = fnew[part, :] - time_step * transport(lhs, far, mine, None, first, count)
        there = (
            their_keep * state
            + (tr0[part, far] - time_step * transport(lhs[:count], far, far, state, first, count))
            + their_gain * equilibrium(their_quad, first, count)
        )
        fnew[part, :] = here
        lhs = halves(jnp.concatenate([here, there], axis=1))
        tr1[part, :] = transport(lhs, slice(0, both), mine, here, first, count)

    lay_rows(qb2.at[me_q], stay)
    in_quad(qb2, 5)
    lay_rows(zb1.at[me_z], collect(3, qb1, QUAD))
    along_z(zb1, 4)
    arrived(total_theirs, 2)
    for i in range(PLACES[0]):
        received(i)
    arrived(got1, 8)
    from_far = [got1[0, r] + got1[1, r] + (got1[2, r] + got1[3, r]) for r in range(13)]
    lay_rows(zb2.at[me_z], collect(5, qb2, QUAD), from_far)
    along_z(zb2, 6)
    for i in range(PLACES[0], PLACES[1]):
        received(i)
    mom1 = collect(4, zb1, ring)
    fields1, quad1, freq1 = coefficient_rows(mom1)
    with jax.named_scope("G_mom1"):
        sums = gauss_moments(quad1, cells, z_count, weights)
    inv_sum = 1.0 / sums[0]
    lift = time_step * freq1 * fields1[0]
    gain1 = lift * inv_sum * float(total_vel)
    keep1 = 1.0 - time_step * freq1


    def finish(i):
        first, last = TAKEN[i] * piece, TAKEN[i + 1] * piece
        part = slice(first, last)
        out_ref[part, :] = (
            keep1 * fnew[part, :] - time_step * tr1[part, :] + gain1 * equilibrium(quad1, first, last - first)
        )

    with jax.named_scope("fin"):
        for i in range(PLACES[1]):
            finish(i)
    for i in range(PLACES[1], len(TAKEN) - 1):
        received(i)
        finish(i)
    mom_t = collect(6, zb2, ring)
    slope = lift * inv_sum
    last = [
        keep1 * mom1[r] - time_step * mom_t[r] + slope * sums[r] for r in range(13)
    ]
    final = macroscopic_rows(last)
    for r in range(13):
        fields_ref[r : r + 1, :] = final[r]
    with jax.named_scope("W_send"):
        pltpu.make_async_copy(fx, fx, bulk_s).wait()
        for copy in metas:
            copy.wait_send()
        for i, buffer in ((2, total_mine), (7, lent0), (8, got1)):
            pltpu.make_async_copy(buffer, buffer, stage_s.at[i]).wait()
        for i, buffer, count in (
            (0, qb0, QUAD), (1, zb0, ring), (3, qb1, QUAD), (4, zb1, ring), (5, qb2, QUAD), (6, zb2, ring),
        ):
            all_of(buffer, stage_s.at[i], count - 1)


def store_kernel(state_ref, fields_ref, state_out, fields_out, sems):
    copies = [
        pltpu.make_async_copy(fields_ref, fields_out, sems.at[0]),
        pltpu.make_async_copy(state_ref, state_out, sems.at[1]),
    ]
    for copy in copies:
        copy.start()
    for copy in copies:
        copy.wait()


def per_device_pair(distribution, normals, adjacency, send_list, block_counts):
    nodes, cells = distribution.shape
    normals = normals.transpose(1, 0, 2)
    size = lax.axis_size("vel")
    ring = size // QUAD
    faces = normals.shape[1]
    f32 = jnp.float32
    dma = pltpu.SemaphoreType.DMA
    vmem = pl.BlockSpec(memory_space=pltpu.VMEM)
    hbm = pl.BlockSpec(memory_space=pltpu.HBM)
    shapes = (
        jax.ShapeDtypeStruct((nodes, cells), f32),
        jax.ShapeDtypeStruct((13, cells), f32),
    )
    state, fields = pl.pallas_call(
        functools.partial(step_kernel, nodes * size),
        out_shape=shapes,
        in_specs=[hbm] * 4,
        out_specs=(vmem, vmem),
        scratch_shapes=[
            pltpu.VMEM((nodes, cells), f32),
            pltpu.VMEM(normals.shape, f32),
            pltpu.VMEM(adjacency.shape, jnp.int32),
            pltpu.VMEM(send_list.shape, jnp.int32),
            dma((CHUNKS + 3,)),
            pltpu.VMEM((nodes, cells), f32),
            pltpu.VMEM(normals.shape, f32),
            pltpu.VMEM(adjacency.shape, jnp.int32),
            pltpu.VMEM(send_list.shape, jnp.int32),
            pltpu.VMEM((3, 8, 2 * cells), f32),
            pltpu.VMEM((faces + 1, VXY, 2 * cells), f32),
            pltpu.VMEM((faces, 2 * cells, 2 * cells), jnp.bfloat16),
            pltpu.VMEM((nodes, 2 * cells), f32),
            pltpu.VMEM((2 * nodes, cells), jnp.bfloat16),
            pltpu.VMEM((nodes, 2 * cells), jnp.bfloat16),
            pltpu.VMEM((nodes, cells), f32),
            pltpu.VMEM((nodes, cells), f32),
            pltpu.VMEM((48, nodes), jnp.bfloat16),
            pltpu.VMEM((VXY // 8, 16, 8 * VXY), jnp.bfloat16),
            pltpu.VMEM((QUAD, 13, 1, cells), f32),
            pltpu.VMEM((ring, 13, 1, cells), f32),
            pltpu.VMEM((12, 1, cells), f32),
            pltpu.VMEM((12, 1, cells), f32),
            pltpu.VMEM((QUAD, 13, 1, cells), f32),
            pltpu.VMEM((ring, 13, 1, cells), f32),
            pltpu.VMEM((QUAD, 13, 1, cells), f32),
            pltpu.VMEM((ring, 13, 1, cells), f32),
            pltpu.VMEM((13, 1, cells), f32),
            pltpu.VMEM((13, 1, cells), f32),
            pltpu.VMEM((13, 1, cells), f32),
            pltpu.VMEM((QUAD, 13, 1, cells), f32),
            dma, dma((len(TAKEN) - 1,)), dma((3,)), dma((3,)), dma((9,)), dma((9,)),
        ],
        compiler_params=pltpu.CompilerParams(
            collective_id=0, has_side_effects=True, vmem_limit_bytes=16 * 1024 * 1024
        ),
        name="steps",
    )(*[pltpu.with_memory_space_constraint(x, pltpu.HBM) for x in (distribution, normals, adjacency, send_list)])
    anywhere = pl.BlockSpec(memory_space=pl.ANY)
    return pl.pallas_call(
        store_kernel,
        out_shape=shapes,
        in_specs=[anywhere, anywhere],
        out_specs=(hbm, hbm),
        scratch_shapes=[dma((2,))],
        compiler_params=pltpu.CompilerParams(vmem_limit_bytes=16 * 1024 * 1024),
        name="store",
    )(state, fields)


def solution(mesh):
    placed = (
        P("vel", "space"),
        P(None, None, "space"),
        P(None, "space"),
        P("space", None, None),
        P(None, "space"),
    )
    pair = mesh.shape["space"] == 2 and mesh.shape["vel"] % QUAD == 0 and ITERS == 2
    return jax.shard_map(
        per_device_pair if pair else per_device,
        mesh=mesh,
        in_specs=placed,
        out_specs=(P("vel", "space"), P(None, "space")),
        check_vma=False,
    )
```

```python
import functools

import jax
import jax.numpy as jnp
from jax import lax
from jax.experimental import pallas as pl
from jax.experimental.pallas import tpu as pltpu
from jax.sharding import PartitionSpec as P

VXY = 32
TILE = 128
ITERS = 2


spacing = 0.3
ellipsoid_mix = -0.25
prandtl = 0.8
visc_power = 0.26
time_step = 0.025


def velocity_nodes(vel_index, z_count):
    comp_x = (vel_index % VXY).astype(jnp.float32)
    comp_y = (vel_index // VXY % VXY).astype(jnp.float32)
    comp_z = (vel_index // (VXY * VXY)).astype(jnp.float32)
    centre = (VXY - 1) / 2.0
    return jnp.stack(
        [
            (comp_x - centre) * spacing,
            (comp_y - centre) * spacing,
            (comp_z - (z_count - 1) / 2.0) * spacing,
        ]
    )


def moment_rows(velocity):
    comp_x, comp_y, comp_z = (velocity[0], velocity[1], velocity[2])
    squared = comp_x * comp_x + comp_y * comp_y + comp_z * comp_z
    return jnp.stack(
        [
            jnp.ones_like(comp_x),
            comp_x,
            comp_y,
            comp_z,
            comp_x * comp_x,
            comp_y * comp_y,
            comp_z * comp_z,
            comp_x * comp_y,
            comp_x * comp_z,
            comp_y * comp_z,
            comp_x * squared,
            comp_y * squared,
            comp_z * squared,
        ]
    )


def quad_rows(velocity):
    comp_x, comp_y, comp_z = (velocity[0], velocity[1], velocity[2])
    return jnp.stack(
        [
            comp_x * comp_x,
            comp_y * comp_y,
            comp_z * comp_z,
            comp_x * comp_y,
            comp_x * comp_z,
            comp_y * comp_z,
            comp_x,
            comp_y,
            comp_z,
            jnp.ones_like(comp_x),
        ]
    )


def macroscopic(moments):
    density = moments[0]
    mean_x = moments[1] / density
    mean_y = moments[2] / density
    mean_z = moments[3] / density
    second = moments[4:10] / density[None, :]
    third = moments[10:13] / density[None, :]
    theta_xx = second[0] - mean_x * mean_x
    theta_yy = second[1] - mean_y * mean_y
    theta_zz = second[2] - mean_z * mean_z
    theta_xy = second[3] - mean_x * mean_y
    theta_xz = second[4] - mean_x * mean_z
    theta_yz = second[5] - mean_y * mean_z
    temper = (theta_xx + theta_yy + theta_zz) / 3.0
    trace_b = second[0] + second[1] + second[2]
    bu_x = second[0] * mean_x + second[3] * mean_y + second[4] * mean_z
    bu_y = second[3] * mean_x + second[1] * mean_y + second[5] * mean_z
    bu_z = second[4] * mean_x + second[5] * mean_y + second[2] * mean_z
    mean_sq = mean_x * mean_x + mean_y * mean_y + mean_z * mean_z
    flux_x = 0.5 * (third[0] - 2.0 * bu_x - mean_x * trace_b + 2.0 * mean_x * mean_sq)
    flux_y = 0.5 * (third[1] - 2.0 * bu_y - mean_y * trace_b + 2.0 * mean_y * mean_sq)
    flux_z = 0.5 * (third[2] - 2.0 * bu_z - mean_z * trace_b + 2.0 * mean_z * mean_sq)
    iso_part = (1.0 - ellipsoid_mix) * temper
    lam_xx = iso_part + ellipsoid_mix * theta_xx
    lam_yy = iso_part + ellipsoid_mix * theta_yy
    lam_zz = iso_part + ellipsoid_mix * theta_zz
    lam_xy = ellipsoid_mix * theta_xy
    lam_xz = ellipsoid_mix * theta_xz
    lam_yz = ellipsoid_mix * theta_yz
    cof_xx = lam_yy * lam_zz - lam_yz * lam_yz
    cof_xy = lam_yz * lam_xz - lam_xy * lam_zz
    cof_xz = lam_xy * lam_yz - lam_yy * lam_xz
    cof_yy = lam_xx * lam_zz - lam_xz * lam_xz
    cof_yz = lam_xy * lam_xz - lam_xx * lam_yz
    cof_zz = lam_xx * lam_yy - lam_xy * lam_xy
    determinant = lam_xx * cof_xx + lam_xy * cof_xy + lam_xz * cof_xz
    inv_xx = cof_xx / determinant
    inv_yy = cof_yy / determinant
    inv_zz = cof_zz / determinant
    inv_xy = cof_xy / determinant
    inv_xz = cof_xz / determinant
    inv_yz = cof_yz / determinant
    lin_x = inv_xx * mean_x + inv_xy * mean_y + inv_xz * mean_z
    lin_y = inv_xy * mean_x + inv_yy * mean_y + inv_yz * mean_z
    lin_z = inv_xz * mean_x + inv_yz * mean_y + inv_zz * mean_z
    offset = mean_x * lin_x + mean_y * lin_y + mean_z * lin_z
    collide = prandtl * density * jnp.exp(visc_power * jnp.log(temper))
    return jnp.stack(
        [
            density,
            mean_x,
            mean_y,
            mean_z,
            theta_xx,
            theta_yy,
            theta_zz,
            theta_xy,
            theta_xz,
            theta_yz,
            flux_x,
            flux_y,
            flux_z,
            inv_xx,
            inv_yy,
            inv_zz,
            2.0 * inv_xy,
            2.0 * inv_xz,
            2.0 * inv_yz,
            -2.0 * lin_x,
            -2.0 * lin_y,
            -2.0 * lin_z,
            offset,
            collide,
        ]
    )


def ghost_slots(adjacency, counts, cells, groups, slot_count):
    ends = jnp.cumsum(counts) * TILE
    starts = ends - counts * TILE
    is_local = adjacency < cells
    position = jnp.maximum(adjacency - cells, 0)
    source = jnp.sum((ends[:, None, None] <= position[None]).astype(jnp.int32), axis=0)
    source = jnp.minimum(source, groups - 1)
    group_ids = jnp.arange(groups, dtype=jnp.int32)[:, None, None]
    chosen = jnp.sum(jnp.where(group_ids == source[None], starts[:, None, None], 0), axis=0)
    slot_pos = jnp.clip(position - chosen, 0, slot_count - 1)
    return (is_local, source, slot_pos)


def relax(current, neighbours, velocity, normals, params, norm_z, equilibrium):
    gauss = params[0][None, :] * equilibrium / norm_z[None, :]
    outflow = jnp.zeros(current.shape, jnp.float32)
    inflow = jnp.zeros(current.shape, jnp.float32)
    for side in range(normals.shape[0]):
        normal_speed = (
            velocity[0][:, None] * normals[side, 0][None, :]
            + velocity[1][:, None] * normals[side, 1][None, :]
            + velocity[2][:, None] * normals[side, 2][None, :]
        )
        outflow = outflow + jnp.maximum(normal_speed, 0.0)
        inflow = inflow + jnp.minimum(normal_speed, 0.0) * neighbours[side]
    return current + time_step * (
        params[23][None, :] * (gauss - current) - outflow * current - inflow
    )


def per_device(distribution, normals, adjacency, send_list, block_counts):
    vel_local = distribution.shape[0]
    cells = distribution.shape[1]
    total_vel = vel_local * lax.axis_size("vel")
    z_count = total_vel // (VXY * VXY)
    groups = send_list.shape[1]
    slot_count = send_list.shape[2]
    vel_index = lax.axis_index("vel") * vel_local + jnp.arange(vel_local, dtype=jnp.int32)
    velocity = velocity_nodes(vel_index, z_count)
    moment_table = moment_rows(velocity)
    quad_table = quad_rows(velocity).T
    is_local, source, slot_pos = ghost_slots(
        adjacency, block_counts[:, 0], cells, groups, slot_count
    )
    ghost_index = source * slot_count + slot_pos
    local_index = jnp.where(is_local, adjacency, 0)
    send_rows = send_list[0].reshape(-1)

    def reduce_moments(current):
        partial_value = (
            jnp.dot(
                moment_table,
                current,
                precision=lax.Precision.HIGHEST,
                preferred_element_type=jnp.float32,
            )
            / total_vel
        )
        return macroscopic(lax.psum(partial_value, "vel"))

    current = distribution
    for iteration in range(ITERS):
        params = reduce_moments(current)
        ghosts = lax.all_to_all(
            jnp.take(current, send_rows, axis=1), "space", split_axis=1, concat_axis=1, tiled=True
        )
        exponent = jnp.dot(
            quad_table,
            params[13:23],
            precision=lax.Precision.HIGHEST,
            preferred_element_type=jnp.float32,
        )
        equilibrium = jnp.exp(-0.5 * exponent)
        norm_z = lax.psum(jnp.sum(equilibrium, axis=0) / total_vel, "vel")
        neighbours = [
            jnp.where(
                is_local[side][None, :],
                jnp.take(current, local_index[side], axis=1),
                jnp.take(ghosts, ghost_index[side], axis=1),
            )
            for side in range(normals.shape[0])
        ]
        current = relax(current, neighbours, velocity, normals, params, norm_z, equilibrium)
    final = reduce_moments(current)
    return (current, final[:13])


MESH = pl.DeviceIdType.MESH
LOG2E = 1.4426950408889634
QUAD = 4
CHUNKS = 4
PIECES = 16
ISSUE = (1, 4, 1, 0, 0, 1, 1, 1, 1, 1, 1, 16)
TAKEN = (0, 8, 12, 16)
PLACES = (2, 2)
SLABS = 2
HI = lax.Precision.HIGHEST


def coefficient_rows(m):
    full = macroscopic_rows(m)
    scale = -0.5 * LOG2E
    return full[:13], [row * scale for row in full[13:23]], full[23]


def macroscopic_rows(m):
    density = m[0]
    inv_d = 1.0 / density
    ux, uy, uz = (m[1] * inv_d, m[2] * inv_d, m[3] * inv_d)
    b = [m[r] * inv_d for r in range(4, 10)]
    third = [m[r] * inv_d for r in range(10, 13)]
    txx, tyy, tzz = (b[0] - ux * ux, b[1] - uy * uy, b[2] - uz * uz)
    txy, txz, tyz = (b[3] - ux * uy, b[4] - ux * uz, b[5] - uy * uz)
    temper = (txx + tyy + tzz) * (1.0 / 3.0)
    trace_b = b[0] + b[1] + b[2]
    bux = b[0] * ux + b[3] * uy + b[4] * uz
    buy = b[3] * ux + b[1] * uy + b[5] * uz
    buz = b[4] * ux + b[5] * uy + b[2] * uz
    usq = ux * ux + uy * uy + uz * uz
    qx = 0.5 * (third[0] - 2.0 * bux - ux * trace_b + 2.0 * ux * usq)
    qy = 0.5 * (third[1] - 2.0 * buy - uy * trace_b + 2.0 * uy * usq)
    qz = 0.5 * (third[2] - 2.0 * buz - uz * trace_b + 2.0 * uz * usq)
    iso = (1.0 - ellipsoid_mix) * temper
    lxx, lyy, lzz = (iso + ellipsoid_mix * txx, iso + ellipsoid_mix * tyy, iso + ellipsoid_mix * tzz)
    lxy, lxz, lyz = (ellipsoid_mix * txy, ellipsoid_mix * txz, ellipsoid_mix * tyz)
    cxx = lyy * lzz - lyz * lyz
    cxy = lyz * lxz - lxy * lzz
    cxz = lxy * lyz - lyy * lxz
    cyy = lxx * lzz - lxz * lxz
    cyz = lxy * lxz - lxx * lyz
    czz = lxx * lyy - lxy * lxy
    inv_det = 1.0 / (lxx * cxx + lxy * cxy + lxz * cxz)
    ixx, iyy, izz = (cxx * inv_det, cyy * inv_det, czz * inv_det)
    ixy, ixz, iyz = (cxy * inv_det, cxz * inv_det, cyz * inv_det)
    wx = ixx * ux + ixy * uy + ixz * uz
    wy = ixy * ux + iyy * uy + iyz * uz
    wz = ixz * ux + iyz * uy + izz * uz
    offset = ux * wx + uy * wy + uz * wz
    collide = prandtl * density * jnp.exp(visc_power * jnp.log(temper))
    return [
        density, ux, uy, uz, txx, tyy, tzz, txy, txz, tyz, qx, qy, qz,
        ixx, iyy, izz, 2.0 * ixy, 2.0 * ixz, 2.0 * iyz,
        -2.0 * wx, -2.0 * wy, -2.0 * wz, offset, collide,
    ]


def node_velocity(index, z_count):
    shift = VXY.bit_length() - 1
    centre = (VXY - 1) / 2.0
    vx = ((index & (VXY - 1)).astype(jnp.float32) - centre) * spacing
    vy = (((index >> shift) & (VXY - 1)).astype(jnp.float32) - centre) * spacing
    vz = ((index >> (2 * shift)).astype(jnp.float32) - (z_count - 1) / 2.0) * spacing
    return vx, vy, vz


def x_column(first, rows, width):
    index = lax.broadcasted_iota(jnp.int32, (rows, width), 0) + first
    return (index.astype(jnp.float32) - (VXY - 1) / 2.0) * spacing


def pair_polynomials(half):
    def grow(before, now):
        rows = [now]
        for _ in range(half - 1):
            shifted = [0.0] + rows[-1]
            twice = [2.0 * v for v in rows[-1]] + [0.0]
            older = before + [0.0] * (len(shifted) - len(before))
            before = rows[-1]
            rows.append([x + y - z for x, y, z in zip(shifted, twice, older)])
        return rows

    return grow([1.0], [1.0]), grow([-1.0], [1.0])


def level_coefficients(q, z_count, powers):
    half = z_count // 2
    even, odd = pair_polynomials(half)
    weights = [jnp.exp2(q[2] * ((k + 0.5) * spacing) ** 2) for k in range(half)]
    result = []
    for c in range(powers):
        table = odd if c % 2 else even
        row = []
        for j in range(half):
            total = None
            for k in range(j, half):
                term = weights[k] * (table[k][j] * ((k + 0.5) * spacing) ** c)
                total = term if total is None else total + term
            row.append(total)
        result.append(row)
    return result


def horner(row, x):
    value = row[-1]
    for c in row[-2::-1]:
        value = value * x + c
    return value


def gauss_columns(q, width, block):
    step = 0.5 * spacing
    vx = x_column(block * 8, 8, width)
    base = (q[0] * vx + q[6]) * vx + q[9]
    lean = q[3] * vx + q[7]
    rise = (q[4] * vx + q[8]) * step
    for j in range(VXY // 2):
        vy = (j + 0.5) * spacing
        mid = base + q[1] * (vy * vy)
        tilt = lean * vy
        side = q[5] * (vy * step)
        columns = []
        for sign in (1.0, -1.0):
            flat = jnp.exp2(mid + tilt if sign > 0 else mid - tilt)
            slope = rise + side if sign > 0 else rise - side
            up, down = jnp.exp2(slope), jnp.exp2(-slope)
            diff = up - down
            columns.append((flat * (up + down), flat * diff, diff * diff))
        yield vx, vy, columns


def gauss_total(q, width, z_count):
    (even,) = level_coefficients(q, z_count, 1)

    def block(b, acc):
        for _, _, columns in gauss_columns(q, width, b):
            for plus, _, delta in columns:
                acc = acc + plus * horner(even, delta)
        return acc

    acc = jnp.zeros((8, width), jnp.float32)
    for b in range(VXY // 8):
        acc = block(b, acc)
    return jnp.sum(acc, axis=0, keepdims=True)


def column_weights(block):
    k = lax.broadcasted_iota(jnp.int32, (1, 8 * VXY), 1)
    x = ((k & 7) + block * 8).astype(jnp.float32) - (VXY - 1) / 2.0
    y = (k >> 4).astype(jnp.float32) + 0.5
    y = jnp.where((k & 8) == 0, y, -y)
    square = x * x + y * y
    rows = [jnp.ones_like(x), x, y, x * x, y * y, x * y, x * square, y * square]
    row_id = lax.broadcasted_iota(jnp.int32, (8, 8 * VXY), 0)
    table = jnp.zeros((8, 8 * VXY), jnp.float32)
    for r, row in enumerate(rows):
        table = jnp.where(row_id == r, row, table)
    high = table.astype(jnp.bfloat16).astype(jnp.float32)
    return jnp.concatenate([high, table - high], axis=0).astype(jnp.bfloat16)


def gauss_moments(q, width, z_count, weights_ref):
    levels = level_coefficients(q, z_count, 4)
    half = z_count // 2
    zero = jnp.zeros((16, width), jnp.float32)

    def block(b, carry):
        tiles = [[] for _ in range(2 * half + 1)]
        for _, _, ((p_up, d_up, x_up), (p_down, d_down, x_down)) in gauss_columns(q, width, b):
            plus = jnp.concatenate([p_up, p_down], axis=0)
            diff = jnp.concatenate([d_up, d_down], axis=0)
            delta = jnp.concatenate([x_up, x_down], axis=0)
            for j in range(half):
                lead = plus.astype(jnp.bfloat16)
                tiles[j].append(lead)
                tiles[half + j].append(diff.astype(jnp.bfloat16))
                if j == 0:
                    tiles[2 * half].append((plus - lead.astype(jnp.float32)).astype(jnp.bfloat16))
                if j < half - 1:
                    plus, diff = plus * delta, diff * delta
        weights = weights_ref[b]
        sums = [
            jnp.dot(weights, jnp.concatenate(t, axis=0), preferred_element_type=jnp.float32) for t in tiles
        ]
        sums[0] = sums[0] + sums.pop()
        return tuple(x + y for x, y in zip(carry, sums))

    sums = (zero,) * (2 * half)
    for b in range(VXY // 8):
        sums = block(b, sums)
    sums = [t[:8] + t[8:] for t in sums]
    m0, m1, m2, m3 = [
        sum(levels[c][j] * sums[(c % 2) * half + j] for j in range(half)) for c in range(4)
    ]
    h = spacing
    row = lambda m, r: m[r : r + 1]
    return [
        row(m0, 0), h * row(m0, 1), h * row(m0, 2), row(m1, 0),
        h * h * row(m0, 3), h * h * row(m0, 4), row(m2, 0),
        h * h * row(m0, 5), h * row(m1, 1), h * row(m1, 2),
        h * (h * h * row(m0, 6) + row(m2, 1)), h * (h * h * row(m0, 7) + row(m2, 2)),
        h * h * (row(m1, 3) + row(m1, 4)) + row(m3, 0),
    ]


def step_kernel(
    total_vel,
    f_hbm, n_hbm, adj_hbm, send_hbm,
    out_ref, fields_ref,
    f_ref, n_ref, adj_ref, send_ref, load_s,
    fx, nx, adjx, sendx, ncat, xn, oh, tr0, split, wide, fnew, tr1, phi_parts, weights,
    qb0, zb0, total_mine, total_theirs, qb1, zb1, qb2, zb2, lent0, got0, lent1, got1,
    bulk_s, bulk_r, meta_s, meta_r, stage_s, stage_r,
):
    nodes, cells = f_hbm.shape
    both = 2 * cells
    faces = n_hbm.shape[1]
    z_count = total_vel // (VXY * VXY)
    rows = nodes // CHUNKS
    group = lax.axis_index("space")
    other = 1 - group
    vel = lax.axis_index("vel")
    ring = total_vel // nodes // QUAD
    me_q = lax.rem(vel, QUAD)
    me_z = vel // QUAD

    def at(space, z, q):
        return (space, z * QUAD + q)

    def q_of(step):
        return lax.rem(me_q + step, QUAD)

    def z_of(step):
        return lax.rem(me_z + step, ring)

    def lay_rows(ref, moments, extra=None):
        for r in range(13):
            row = moments[r] if isinstance(moments, list) else moments[r : r + 1]
            ref[r] = row if extra is None else row + extra[r]

    barrier = pltpu.get_barrier_semaphore()
    for step in range(1, ring):
        pl.semaphore_signal(barrier, inc=1, device_id=at(group, z_of(step), me_q), device_id_type=MESH)
    for step in range(1, QUAD):
        pl.semaphore_signal(barrier, inc=1, device_id=at(group, me_z, q_of(step)), device_id_type=MESH)
    for step in range(QUAD):
        pl.semaphore_signal(barrier, inc=1, device_id=at(other, me_z, q_of(step)), device_id_type=MESH)

    def chunk(c):
        return pl.ds(pl.multiple_of(c * rows, rows), rows)

    loads = [
        pltpu.make_async_copy(f_hbm.at[pl.ds(c * rows, rows)], f_ref.at[pl.ds(c * rows, rows)], load_s.at[c])
        for c in range(CHUNKS)
    ]
    small_loads = [
        pltpu.make_async_copy(src, dst, load_s.at[CHUNKS + i])
        for i, (src, dst) in enumerate([(send_hbm, send_ref), (adj_hbm, adj_ref), (n_hbm, n_ref)])
    ]
    for copy in loads + small_loads:
        copy.start()

    lane_v = node_velocity(lax.broadcasted_iota(jnp.int32, (1, nodes), 1) + vel * nodes, z_count)
    lx, ly, lz = lane_v
    sq = lx * lx + ly * ly + lz * lz
    table = [
        jnp.ones_like(lx), lx, ly, lz, lx * lx, ly * ly, lz * lz,
        lx * ly, lx * lz, ly * lz, lx * sq, ly * sq, lz * sq,
    ]
    row_id = lax.broadcasted_iota(jnp.int32, (16, nodes), 0)
    phi = jnp.zeros((16, nodes), jnp.float32)
    for r, row in enumerate(table):
        phi = jnp.where(row_id == r, row, phi)
    rest = phi
    for i in range(3):
        leading = rest.astype(jnp.bfloat16)
        phi_parts[i * 16 : (i + 1) * 16, :] = leading
        rest = rest - leading.astype(jnp.float32)
    with jax.named_scope("W_bar"):
        pl.semaphore_wait(barrier, 2 * QUAD + ring - 2)

    def remote(src, dst, s, r, dev):
        return pltpu.make_async_remote_copy(
            src_ref=src, dst_ref=dst, send_sem=s, recv_sem=r, device_id=dev, device_id_type=MESH
        )

    pair = at(other, me_z, me_q)

    piece = nodes // PIECES

    plan, started = iter(ISSUE), []

    def more():
        first = len(started)
        last = min(PIECES, first + next(plan))
        for c in range(first, last):
            started.append(c)
            part = pl.ds(c * piece, piece)
            remote(f_hbm.at[part], fx.at[part], bulk_s, bulk_r.at[sum(c >= t for t in TAKEN) - 1], pair).start()

    metas = [
        remote(send_hbm, sendx, meta_s.at[0], meta_r.at[0], pair),
        remote(adj_hbm, adjx, meta_s.at[1], meta_r.at[1], pair),
        remote(n_hbm, nx, meta_s.at[2], meta_r.at[2], pair),
    ]
    for copy in metas:
        copy.start()
    more()

    def two_dot(part, state):
        high = state.astype(jnp.bfloat16)
        low = (state - high.astype(jnp.float32)).astype(jnp.bfloat16)
        lead = jnp.dot(phi_parts[:, part], high, preferred_element_type=jnp.float32)
        tail = jnp.dot(phi_parts[0:32, part], low, preferred_element_type=jnp.float32)
        return lead[0:16] + (lead[16:32] + tail[0:16]) + (lead[32:48] + tail[16:32])

    inv_total = 1.0 / total_vel
    partial = jnp.zeros((16, cells), jnp.float32)
    for c in range(CHUNKS):
        loads[c].wait()
        part = slice(c * rows, (c + 1) * rows)
        partial = partial + two_dot(part, f_ref[part, :])
    lay_rows(qb0.at[me_q], partial * inv_total)

    def in_quad(buffer, i):
        for t in range(1, QUAD):
            remote(buffer.at[me_q], buffer.at[me_q], stage_s.at[i], stage_r.at[i], at(group, me_z, q_of(t))).start()

    def along_z(buffer, i):
        for t in range(1, ring):
            remote(buffer.at[me_z], buffer.at[me_z], stage_s.at[i], stage_r.at[i], at(group, z_of(t), me_q)).start()

    def across(src, dst, i):
        remote(src, dst, stage_s.at[i], stage_r.at[i], pair).start()

    def arrived(dst, i):
        with jax.named_scope(f"W_stage{i}"):
            pltpu.make_async_copy(dst, dst, stage_r.at[i]).wait()

    def all_of(buffer, sem, count):
        part = buffer.at[pl.ds(0, count)]
        pltpu.make_async_copy(part, part, sem).wait()

    def collect(i, buffer, count):
        with jax.named_scope(f"W_stage{i}"):
            all_of(buffer, stage_r.at[i], count - 1)
        rows13 = []
        for r in range(13):
            row = buffer[0, r]
            for t in range(1, count):
                row = row + buffer[t, r]
            rows13.append(row)
        return rows13

    in_quad(qb0, 0)
    more()

    for copy in small_loads:
        copy.wait()
    mine, far = slice(0, cells), slice(cells, both)
    slot_id = lax.broadcasted_iota(jnp.int32, (cells, cells), 0)
    eye = (slot_id == lax.broadcasted_iota(jnp.int32, (cells, cells), 1)).astype(jnp.float32)
    vx_col = x_column(0, VXY, cells)

    def listed(send_row, adjacency):
        hit = jnp.where(slot_id == adjacency - cells, 1.0, 0.0).astype(jnp.bfloat16)
        values = jnp.broadcast_to(send_row, (8, cells)).astype(jnp.float32).astype(jnp.bfloat16)
        got = jnp.dot(values, hit, preferred_element_type=jnp.float32)
        return jnp.where(adjacency < cells, -1, got[0:1].astype(jnp.int32))

    def choose(k, source, target, index):
        hit = jnp.where(slot_id == index, 1.0, 0.0)
        oh[k, source, target] = (hit - eye if source == target else hit).astype(jnp.bfloat16)

    def lay_normals(ref, target):
        for d in range(3):
            lines = [ref[d, k : k + 1, :] for k in range(faces)]
            lines.append(sum(lines[1:], lines[0]))
            for k, line in enumerate(lines):
                if d == 0:
                    xn[k, :, target] = vx_col * line
                else:
                    ncat[d, k : k + 1, target] = line

    lay_normals(n_ref, mine)
    for k in range(faces):
        choose(k, mine, mine, adj_ref[k : k + 1, :])

    for b in range(VXY // 8):
        weights[b] = column_weights(b)
    lay_rows(zb0.at[me_z], collect(0, qb0, QUAD))
    along_z(zb0, 1)
    more()

    with jax.named_scope("W_meta"):
        for copy in metas:
            copy.wait_recv()
    to_me = sendx[0, pl.ds(group, 1), :]
    to_other = send_ref[0, pl.ds(other, 1), :]
    lay_normals(nx, far)
    for k in range(faces):
        choose(k, mine, far, listed(to_other, adjx[k : k + 1, :]))

    centre = (VXY - 1) / 2.0
    shift = VXY.bit_length() - 1

    def line_velocity(first):
        line = (vel * nodes + first) // VXY
        vy = ((line & (VXY - 1)).astype(jnp.float32) - centre) * spacing
        vz = ((line >> shift).astype(jnp.float32) - (z_count - 1) / 2.0) * spacing
        return vy, vz

    def halves(state):
        high = state.astype(jnp.bfloat16)
        low = (state - high.astype(jnp.float32)).astype(jnp.bfloat16)
        return jnp.concatenate([high, low], axis=0)

    def transport(lhs, source, target, leaving, first, count):
        speeds = [line_velocity(first + sub * VXY) for sub in range(count // VXY)]

        def speed(k, sub):
            vy, vz = speeds[sub]
            return xn[k, :, target] + (vy * ncat[1, k : k + 1, target] + vz * ncat[2, k : k + 1, target])

        def lines(sub, offset=0):
            return slice(offset + sub * VXY, offset + (sub + 1) * VXY)

        result = [
            None if leaving is None else leaving[lines(sub)] * speed(faces, sub) for sub in range(count // VXY)
        ]
        for k in range(faces):
            got = jnp.dot(lhs, oh[k, source, target], preferred_element_type=jnp.float32)
            for sub in range(count // VXY):
                value = got[lines(sub)]
                if lhs.shape[0] > count:
                    value = value + got[lines(sub, count)]
                term = jnp.minimum(speed(k, sub), 0.0) * value
                result[sub] = term if result[sub] is None else result[sub] + term
        return jnp.concatenate(result, axis=0)

    def equilibrium(quad, first, count):
        square = quad[0] * vx_col
        parts = []
        for sub in range(count // VXY):
            vy, vz = line_velocity(first + sub * VXY)
            slope = quad[3] * vy + quad[4] * vz + quad[6]
            level = vy * (quad[1] * vy + quad[5] * vz + quad[7]) + (vz * (quad[2] * vz + quad[8]) + quad[9])
            parts.append(jnp.exp2(vx_col * (square + slope) + level))
        return jnp.concatenate(parts, axis=0)

    blocks = [(c * (nodes // SLABS), nodes // SLABS) for c in range(SLABS)]
    sent = jnp.zeros((16, cells), jnp.float32)
    with jax.named_scope("T0p_far"):
        for first, count in blocks:
            part = slice(first, first + count)
            lhs = halves(f_ref[part, :])
            split[2 * first : 2 * (first + count), :] = lhs
            moved = transport(lhs[:count], mine, far, None, first, count)
            tr0[part, far] = moved
            sent = sent + two_dot(part, moved)
            more()
    lay_rows(lent0, sent * (-time_step * inv_total))
    across(lent0, got0, 7)
    more()
    with jax.named_scope("T0p_mine"):
        for first, count in blocks:
            part = slice(first, first + count)
            lhs = split[2 * first : 2 * (first + count), :]
            tr0[part, mine] = transport(lhs, mine, mine, f_ref[part, :], first, count)
            more()

    with jax.named_scope("oh2"):
        for k in range(faces):
            choose(k, far, mine, listed(to_me, adj_ref[k : k + 1, :]))
            theirs = adjx[k : k + 1, :]
            choose(k, far, far, theirs)

    more()
    fields0, own_quad, freq0 = coefficient_rows(collect(1, zb0, ring))
    more()
    with jax.named_scope("G_tot0"):
        norm0 = gauss_total(own_quad, cells, z_count) * inv_total
    own_gain = time_step * freq0 * fields0[0] / norm0
    own_keep = 1.0 - time_step * freq0
    for r, row in enumerate(own_quad + [own_gain, own_keep]):
        total_mine[r] = row
    across(total_mine, total_theirs, 2)
    more()

    with jax.named_scope("f1p"):
        for first, count in blocks:
            part = slice(first, first + count)
            state = (
                own_keep * f_ref[part, :] - time_step * tr0[part, mine] + own_gain * equilibrium(own_quad, first, count)
            )
            fnew[part, :] = state
            wide[part, mine] = state.astype(jnp.bfloat16)
            away = -time_step * tr0[part, far]
            tr0[part, far] = away
            wide[part, far] = away.astype(jnp.bfloat16)
        kept = two_dot(slice(0, nodes), fnew[...]) * inv_total
    arrived(got0, 7)
    lay_rows(qb1.at[me_q], kept, got0)
    in_quad(qb1, 3)

    def second_moments(target, leaving):
        part = slice(0, nodes)
        moved = transport(wide[part, :], slice(0, both), target, leaving(part), 0, nodes)
        return two_dot(part, moved) * inv_total

    with jax.named_scope("T1p_far"):
        lay_rows(lent1, second_moments(far, lambda part: tr0[part, far]))
    for t in range(QUAD):
        remote(lent1, got1.at[me_q], stage_s.at[8], stage_r.at[8], at(other, me_z, q_of(t))).start()
    more()
    with jax.named_scope("T1p_mine"):
        stay = second_moments(mine, lambda part: fnew[part, :])

    def received(i):
        first, last = TAKEN[i] * piece, TAKEN[i + 1] * piece
        count, part = last - first, slice(first, last)
        with jax.named_scope("W_bulk"):
            ref = fx.at[pl.ds(first, count)]
            pltpu.make_async_copy(ref, ref, bulk_r.at[i]).wait()
        their_quad = [total_theirs[r] for r in range(10)]
        their_gain, their_keep = total_theirs[10], total_theirs[11]
        state = fx[part, :]
        lhs = halves(state)
        there = (
            their_keep * state
            + (tr0[part, far] - time_step * transport(lhs[:count], far, far, state, first, count))
            + their_gain * equilibrium(their_quad, first, count)
        )
        stacked = jnp.concatenate([lhs, halves(there)], axis=0)
        subs = range(count // VXY)
        speeds = [line_velocity(first + sub * VXY) for sub in subs]
        once, twice = [None] * len(subs), [None] * len(subs)
        for k in range(faces):
            got = jnp.dot(stacked, oh[k, far, mine], preferred_element_type=jnp.float32)
            for sub in subs:
                vy, vz = speeds[sub]
                speed = xn[k, :, mine] + (vy * ncat[1, k : k + 1, mine] + vz * ncat[2, k : k + 1, mine])
                inward = jnp.minimum(speed, 0.0)
                low, high = sub * VXY, (sub + 1) * VXY
                before = inward * (got[low:high] + got[count + low : count + high])
                after = inward * (got[2 * count + low : 2 * count + high] + got[3 * count + low : 3 * count + high])
                once[sub] = before if once[sub] is None else once[sub] + before
                twice[sub] = after if twice[sub] is None else twice[sub] + after
        here = fnew[part, :] - time_step * jnp.concatenate(once, axis=0)
        fnew[part, :] = here
        tr1[part, :] = jnp.concatenate(twice, axis=0) + transport(halves(here), mine, mine, here, first, count)

    lay_rows(qb2.at[me_q], stay)
    in_quad(qb2, 5)
    lay_rows(zb1.at[me_z], collect(3, qb1, QUAD))
    along_z(zb1, 4)
    arrived(total_theirs, 2)
    for i in range(PLACES[0]):
        received(i)
    arrived(got1, 8)
    from_far = [got1[0, r] + got1[1, r] + (got1[2, r] + got1[3, r]) for r in range(13)]
    lay_rows(zb2.at[me_z], collect(5, qb2, QUAD), from_far)
    along_z(zb2, 6)
    for i in range(PLACES[0], PLACES[1]):
        received(i)
    mom1 = collect(4, zb1, ring)
    fields1, quad1, freq1 = coefficient_rows(mom1)
    with jax.named_scope("G_mom1"):
        sums = gauss_moments(quad1, cells, z_count, weights)
    inv_sum = 1.0 / sums[0]
    lift = time_step * freq1 * fields1[0]
    gain1 = lift * inv_sum * float(total_vel)
    keep1 = 1.0 - time_step * freq1


    def finish(i):
        first, last = TAKEN[i] * piece, TAKEN[i + 1] * piece
        part = slice(first, last)
        out_ref[part, :] = (
            keep1 * fnew[part, :] - time_step * tr1[part, :] + gain1 * equilibrium(quad1, first, last - first)
        )

    with jax.named_scope("fin"):
        for i in range(PLACES[1]):
            finish(i)
    for i in range(PLACES[1], len(TAKEN) - 1):
        received(i)
        finish(i)
    mom_t = collect(6, zb2, ring)
    slope = lift * inv_sum
    last = [
        keep1 * mom1[r] - time_step * mom_t[r] + slope * sums[r] for r in range(13)
    ]
    final = macroscopic_rows(last)
    for r in range(13):
        fields_ref[r : r + 1, :] = final[r]
    with jax.named_scope("W_send"):
        pltpu.make_async_copy(fx, fx, bulk_s).wait()
        for copy in metas:
            copy.wait_send()
        for i, buffer in ((2, total_mine), (7, lent0), (8, got1)):
            pltpu.make_async_copy(buffer, buffer, stage_s.at[i]).wait()
        for i, buffer, count in (
            (0, qb0, QUAD), (1, zb0, ring), (3, qb1, QUAD), (4, zb1, ring), (5, qb2, QUAD), (6, zb2, ring),
        ):
            all_of(buffer, stage_s.at[i], count - 1)


def store_kernel(state_ref, fields_ref, state_out, fields_out, sems):
    copies = [
        pltpu.make_async_copy(fields_ref, fields_out, sems.at[0]),
        pltpu.make_async_copy(state_ref, state_out, sems.at[1]),
    ]
    for copy in copies:
        copy.start()
    for copy in copies:
        copy.wait()


def per_device_pair(distribution, normals, adjacency, send_list, block_counts):
    nodes, cells = distribution.shape
    normals = normals.transpose(1, 0, 2)
    size = lax.axis_size("vel")
    ring = size // QUAD
    faces = normals.shape[1]
    f32 = jnp.float32
    dma = pltpu.SemaphoreType.DMA
    vmem = pl.BlockSpec(memory_space=pltpu.VMEM)
    hbm = pl.BlockSpec(memory_space=pltpu.HBM)
    shapes = (
        jax.ShapeDtypeStruct((nodes, cells), f32),
        jax.ShapeDtypeStruct((13, cells), f32),
    )
    state, fields = pl.pallas_call(
        functools.partial(step_kernel, nodes * size),
        out_shape=shapes,
        in_specs=[hbm] * 4,
        out_specs=(vmem, vmem),
        scratch_shapes=[
            pltpu.VMEM((nodes, cells), f32),
            pltpu.VMEM(normals.shape, f32),
            pltpu.VMEM(adjacency.shape, jnp.int32),
            pltpu.VMEM(send_list.shape, jnp.int32),
            dma((CHUNKS + 3,)),
            pltpu.VMEM((nodes, cells), f32),
            pltpu.VMEM(normals.shape, f32),
            pltpu.VMEM(adjacency.shape, jnp.int32),
            pltpu.VMEM(send_list.shape, jnp.int32),
            pltpu.VMEM((3, 8, 2 * cells), f32),
            pltpu.VMEM((faces + 1, VXY, 2 * cells), f32),
            pltpu.VMEM((faces, 2 * cells, 2 * cells), jnp.bfloat16),
            pltpu.VMEM((nodes, 2 * cells), f32),
            pltpu.VMEM((2 * nodes, cells), jnp.bfloat16),
            pltpu.VMEM((nodes, 2 * cells), jnp.bfloat16),
            pltpu.VMEM((nodes, cells), f32),
            pltpu.VMEM((nodes, cells), f32),
            pltpu.VMEM((48, nodes), jnp.bfloat16),
            pltpu.VMEM((VXY // 8, 16, 8 * VXY), jnp.bfloat16),
            pltpu.VMEM((QUAD, 13, 1, cells), f32),
            pltpu.VMEM((ring, 13, 1, cells), f32),
            pltpu.VMEM((12, 1, cells), f32),
            pltpu.VMEM((12, 1, cells), f32),
            pltpu.VMEM((QUAD, 13, 1, cells), f32),
            pltpu.VMEM((ring, 13, 1, cells), f32),
            pltpu.VMEM((QUAD, 13, 1, cells), f32),
            pltpu.VMEM((ring, 13, 1, cells), f32),
            pltpu.VMEM((13, 1, cells), f32),
            pltpu.VMEM((13, 1, cells), f32),
            pltpu.VMEM((13, 1, cells), f32),
            pltpu.VMEM((QUAD, 13, 1, cells), f32),
            dma, dma((len(TAKEN) - 1,)), dma((3,)), dma((3,)), dma((9,)), dma((9,)),
        ],
        compiler_params=pltpu.CompilerParams(
            collective_id=0, has_side_effects=True, vmem_limit_bytes=16 * 1024 * 1024
        ),
        name="steps",
    )(*[pltpu.with_memory_space_constraint(x, pltpu.HBM) for x in (distribution, normals, adjacency, send_list)])
    anywhere = pl.BlockSpec(memory_space=pl.ANY)
    return pl.pallas_call(
        store_kernel,
        out_shape=shapes,
        in_specs=[anywhere, anywhere],
        out_specs=(hbm, hbm),
        scratch_shapes=[dma((2,))],
        compiler_params=pltpu.CompilerParams(vmem_limit_bytes=16 * 1024 * 1024),
        name="store",
    )(state, fields)


def solution(mesh):
    placed = (
        P("vel", "space"),
        P(None, None, "space"),
        P(None, "space"),
        P("space", None, None),
        P(None, "space"),
    )
    pair = mesh.shape["space"] == 2 and mesh.shape["vel"] % QUAD == 0 and ITERS == 2
    return jax.shard_map(
        per_device_pair if pair else per_device,
        mesh=mesh,
        in_specs=placed,
        out_specs=(P("vel", "space"), P(None, "space")),
        check_vma=False,
    )
```
